32 devices in a mesh: fsdp: 32 (over z, y, x, core).
Axes of the slice: x: 2, y: 2, z: 4, core: 2. Of those that a mesh axis runs over, the one named last changes fastest.
Arguments:
- inputs: bfloat16 [6144, 1280], P('fsdp'), may hold values from -6 to 6
- ln1_gain: float32 [1280], P('fsdp'), may hold values from 0.5 to 1.5
- ln1_bias: float32 [1280], P('fsdp'), may hold values from -1 to 1
- w_query: float32 [1280, 1280], P('fsdp'), may hold values from -0.3125 to 0.3125
- b_query: float32 [1280], P('fsdp'), may hold values from -2.5 to 2.5
- w_key: float32 [1280, 1280], P('fsdp'), may hold values from -0.15625 to 0.15625
- w_value: float32 [1280, 1280], P('fsdp'), may hold values from -0.15625 to 0.15625
- b_value: float32 [1280], P('fsdp'), may hold values from -2.5 to 2.5
- w_out: float32 [1280, 1280], P('fsdp'), may hold values from -0.625 to 0.625
- b_out: float32 [1280], P('fsdp'), may hold values from -2.5 to 2.5
- ln2_gain: float32 [1280], P('fsdp'), may hold values from 0.5 to 1.5
- ln2_bias: float32 [1280], P('fsdp'), may hold values from -1 to 1
- w_up: float32 [1280, 5120], P('fsdp'), may hold values from -0.15625 to 0.15625
- b_up: float32 [5120], P('fsdp'), may hold values from -2.5 to 2.5
- w_down: float32 [5120, 1280], P('fsdp'), may hold values from -0.078125 to 0.078125
- b_down: float32 [1280], P('fsdp'), may hold values from -2.5 to 2.5
- lengths: int32 [4], replicated, may hold values from 1153 to 1536, as said below
- cotangent: bfloat16 [6144, 1280], P('fsdp'), may hold values from -6 to 6
Outputs:
- output: float32 [6144, 1280], P('fsdp')
- grad_inputs: float32 [6144, 1280], P('fsdp')
- grad_ln1_gain: float32 [1280], P('fsdp')
- grad_ln1_bias: float32 [1280], P('fsdp')
- grad_w_query: float32 [1280, 1280], P('fsdp')
- grad_b_query: float32 [1280], P('fsdp')
- grad_w_key: float32 [1280, 1280], P('fsdp')
- grad_w_value: float32 [1280, 1280], P('fsdp')
- grad_b_value: float32 [1280], P('fsdp')
- grad_w_out: float32 [1280, 1280], P('fsdp')
- grad_b_out: float32 [1280], P('fsdp')
- grad_ln2_gain: float32 [1280], P('fsdp')
- grad_ln2_bias: float32 [1280], P('fsdp')
- grad_w_up: float32 [1280, 5120], P('fsdp')
- grad_b_up: float32 [5120], P('fsdp')
- grad_w_down: float32 [5120, 1280], P('fsdp')
- grad_b_down: float32 [1280], P('fsdp')
The draws below stay inside these ranges and needn't reach their ends.
Inputs may be any that keep to these rules, and one draw needn't show every extreme that they name: Frames of clip c at positions lengths[c] and beyond are padding; some clip has exactly 1536 real frames and some exactly 1153.
All inputs are finite; a program needn't handle non-finite values.
Results may differ from the reference program's by a relative error of at most 0.014.
The reference program's roundings to bfloat16 on the way count: a program that leaves them out, or rounds other values in their place, can miss the bound.
Values may be sent and summed in bfloat16 or wider, within the bound.
A program may use at most 320 MiB of HBM per device.

```python
import math
import jax
import jax.numpy as jnp
from jax import lax

D = 1280
H = 16
HD = 80
FF = 5120
CLIP_LEN = 1536
CLIPS = 4
TOKENS = 6144


def draw_lengths(key, part):
    key_values, key_ordering = jax.random.split(jax.random.fold_in(key, 7))
    counts = jax.random.randint(key_values, (CLIPS,), CLIP_LEN * 3 // 4 + 1, CLIP_LEN + 1, dtype=jnp.int32)
    ordering = jax.random.permutation(key_ordering, CLIPS)
    counts = counts.at[ordering[0]].set(CLIP_LEN)
    counts = counts.at[ordering[1]].set(CLIP_LEN * 3 // 4 + 1)
    return counts


def raised(array, stream_key, source, target, parts, factor):
    def block_of(position):
        return (jnp.arange(array.shape[position]) // (array.shape[position] // parts)).reshape((-1,) + (1,) * (array.ndim - 1 - position))

    first = jax.random.permutation(stream_key, parts)[block_of(target)]
    second = (block_of(target) + parts // 2) % parts
    return jnp.where((block_of(source) == first) | (block_of(source) == second), factor * array, array)


def block_scale(own_key, shape, pieces, least, high):
    loudness = 1.0
    for dim, blocks in pieces:
        steps = jax.random.uniform(jax.random.fold_in(jax.random.fold_in(own_key, 6), dim), (blocks,), jnp.float32, least / len(pieces), high / len(pieces))
        loudness = loudness * jnp.repeat(jnp.exp(steps), shape[dim] // blocks).reshape((-1,) + (1,) * (len(shape) - 1 - dim))
    return loudness


def bell_draw(own_key, extent, width, bound, cuts=(), kind=jnp.bfloat16):
    factor_of = block_scale(own_key, extent, cuts, -0.22, 0.18) if cuts else 1.0
    values = jax.random.normal(own_key, extent, jnp.float32) * width * factor_of
    return jnp.minimum(jnp.maximum(values, -bound), bound).astype(kind)


def noise_with(own_key, extent, scale, bound, shards, heavy, kind=jnp.bfloat16):
    values = scale * jax.random.normal(own_key, extent, jnp.float32)
    if shards:
        values = values * block_scale(own_key, extent, shards, -0.22, 0.18)
    return jnp.clip(raised(values, jax.random.fold_in(own_key, 3), *heavy), -bound, bound).astype(kind)


def setup_inputs(seed: int = 0) -> dict:
    key_of = jax.random.split(jax.random.key(seed), 19)
    return {
        "inputs": noise_with(key_of[0], (TOKENS, D), 1.0, 6.0, ((0, 32),), (0, 1, 32, 2.75)),
        "ln1_gain": jnp.clip(1.0 + 0.1 * jax.random.normal(key_of[1], (D,), jnp.float32), 0.5, 1.5),
        "ln1_bias": bell_draw(key_of[2], (D,), 0.2, 1.0, ((0, 32),), jnp.float32),
        "w_query": bell_draw(key_of[3], (D, D), (D // 4) ** -0.5, 0.3125, ((0, 32),), jnp.float32),
        "b_query": bell_draw(key_of[4], (D,), 0.5, 2.5, ((0, 32),), jnp.float32),
        "w_key": bell_draw(key_of[5], (D, D), D ** -0.5, 0.15625, ((0, 32),), jnp.float32),
        "w_value": bell_draw(key_of[6], (D, D), D ** -0.5, 0.15625, ((0, 32),), jnp.float32),
        "b_value": bell_draw(key_of[7], (D,), 0.5, 2.5, ((0, 32),), jnp.float32),
        "w_out": bell_draw(key_of[8], (D, D), (D // 16) ** -0.5, 0.625, ((0, 32),), jnp.float32),
        "b_out": bell_draw(key_of[9], (D,), 0.5, 2.5, ((0, 32),), jnp.float32),
        "ln2_gain": jnp.clip(1.0 + 0.1 * jax.random.normal(key_of[10], (D,), jnp.float32), 0.5, 1.5),
        "ln2_bias": bell_draw(key_of[11], (D,), 0.2, 1.0, ((0, 32),), jnp.float32),
        "w_up": bell_draw(key_of[12], (D, FF), D ** -0.5, 0.15625, ((0, 32),), jnp.float32),
        "b_up": bell_draw(key_of[13], (FF,), 0.5, 2.5, ((0, 32),), jnp.float32),
        "w_down": bell_draw(key_of[14], (FF, D), FF ** -0.5, 0.078125, ((0, 32),), jnp.float32),
        "b_down": bell_draw(key_of[15], (D,), 0.5, 2.5, ((0, 32),), jnp.float32),
        "lengths": draw_lengths(jax.random.fold_in(key_of[18], 71), 0),
        "cotangent": bell_draw(key_of[17], (TOKENS, D), 1.0, 6.0, ((0, 32),)),
    }


@jax.custom_vjp
def low(v):
    return lax.optimization_barrier(v.astype(jnp.bfloat16)).astype(jnp.float32)

@jax.custom_vjp
def low_back(v):
    return v

def low_keep(v):
    return (low(v), None)

def low_pass(kept, grad):
    return (grad,)

def back_keep(v):
    return (v, None)

def back_low(kept, grad):
    return (low(grad),)
low.defvjp(low_keep, low_pass)
low_back.defvjp(back_keep, back_low)
epsilon = 1e-05
masked_value = -1e+30
highest = lax.Precision.HIGHEST

def layer_norm(values, gain, offset):
    average = lax.optimization_barrier(jnp.mean(values, axis=-1, keepdims=True))
    centred = values - average
    variance = lax.optimization_barrier(jnp.mean(centred * centred, axis=-1, keepdims=True))
    return centred * lax.rsqrt(variance + epsilon) * gain + offset

def attend_clip(operands):
    query_clip, key_clip, value_clip, length = operands
    score_scale = 1.0 / math.sqrt(HD)
    scores = low_back(jnp.einsum('qhd,khd->hqk', query_clip, key_clip, precision=highest) * score_scale)
    key_valid = jnp.arange(CLIP_LEN, dtype=jnp.int32)[None, None, :] < length
    masked = jnp.where(key_valid, scores, masked_value)
    largest = lax.optimization_barrier(jnp.max(masked, axis=-1, keepdims=True))
    exponent = jnp.exp(masked - largest)
    attn_weights = exponent / lax.optimization_barrier(jnp.sum(exponent, axis=-1, keepdims=True))
    return jnp.einsum('hqk,khd->qhd', low(attn_weights), value_clip, precision=highest)

def forward(inputs, masters, lengths):
    ln1_gain, ln1_bias, w_query, b_query, w_key, w_value, b_value, w_out, b_out, ln2_gain, ln2_bias, w_up, b_up, w_down, b_down = tuple((low(master) for master in masters))
    normed = low(layer_norm(inputs, ln1_gain, ln1_bias))
    query_rows = low_back(low(jnp.dot(normed, w_query, precision=highest) + b_query))
    key_rows = low_back(low(jnp.dot(normed, w_key, precision=highest)))
    value_rows = low_back(low(jnp.dot(normed, w_value, precision=highest) + b_value))
    clip_shape = (CLIPS, CLIP_LEN, H, HD)
    attended = lax.map(jax.checkpoint(attend_clip), (query_rows.reshape(clip_shape), key_rows.reshape(clip_shape), value_rows.reshape(clip_shape), lengths))
    attended = low_back(low(attended.reshape(TOKENS, D)))
    branch = low_back(jnp.dot(attended, w_out, precision=highest) + b_out)
    residual = inputs + branch
    normed_two = low(layer_norm(residual, ln2_gain, ln2_bias))
    hidden = low_back(jnp.dot(normed_two, w_up, precision=highest) + b_up)
    activated = low(jax.nn.gelu(hidden, approximate=False))
    return residual + low_back(jnp.dot(activated, w_down, precision=highest) + b_down)

def reference(inputs, ln1_gain, ln1_bias, w_query, b_query, w_key, w_value, b_value, w_out, b_out, ln2_gain, ln2_bias, w_up, b_up, w_down, b_down, lengths, cotangent):
    masters = (ln1_gain, ln1_bias, w_query, b_query, w_key, w_value, b_value, w_out, b_out, ln2_gain, ln2_bias, w_up, b_up, w_down, b_down)

    def layer_forward(source, weights):
        return forward(source, weights, lengths)
    output, pullback = jax.vjp(layer_forward, inputs.astype(jnp.float32), masters)
    grad_inputs, grad_params = pullback(cotangent.astype(jnp.float32))
    grad_ln1_gain, grad_ln1_bias, grad_w_query, grad_b_query, grad_w_key, grad_w_value, grad_b_value, grad_w_out, grad_b_out, grad_ln2_gain, grad_ln2_bias, grad_w_up, grad_b_up, grad_w_down, grad_b_down = grad_params
    return (output, grad_inputs, grad_ln1_gain, grad_ln1_bias, grad_w_query, grad_b_query, grad_w_key, grad_w_value, grad_b_value, grad_w_out, grad_b_out, grad_ln2_gain, grad_ln2_bias, grad_w_up, grad_b_up, grad_w_down, grad_b_down)
```

```python
import functools
import math

import jax
import jax.numpy as jnp
from jax import lax
from jax.experimental import pallas as pl
from jax.experimental.pallas import tpu as pltpu
from jax.sharding import PartitionSpec as P

D = 1280
H = 16
HD = 80
CLIP_LEN = 1536
GROUP = 8
LANES = 128
HEADS_HERE = H // GROUP
HEAD_COLS = HEADS_HERE * HD
SURE = CLIP_LEN * 3 // 4

epsilon = 1e-05
masked_value = -1e30
MESH = pl.DeviceIdType.MESH
VMEM = pltpu.VMEM
DMA = pltpu.SemaphoreType.DMA
bf16 = jnp.bfloat16
f32 = jnp.float32


def matmul(left, right):
    return jnp.dot(left, right, preferred_element_type=f32)


def outer_sum(left, right):
    return lax.dot_general(left, right, (((0,), (0,)), ((), ())), preferred_element_type=f32)


def times_transposed(left, right):
    return lax.dot_general(left, right, (((1,), (1,)), ((), ())), preferred_element_type=f32)


def flip(place, mask):
    for bit in (1, 2, 4):
        if mask & bit:
            place = place + bit - 2 * bit * (place // bit % 2)
    return place


def remote(src, dst, send_sem, recv_sem, target):
    return pltpu.make_async_remote_copy(
        src_ref=src,
        dst_ref=dst,
        send_sem=send_sem,
        recv_sem=recv_sem,
        device_id=(target,),
        device_id_type=MESH,
    )


def greet(targets):
    barrier = pltpu.get_barrier_semaphore()
    for target in targets:
        pl.semaphore_signal(barrier, inc=1, device_id=(target,), device_id_type=MESH)
    pl.semaphore_wait(barrier, len(targets))


def greet_all(me, count):
    barrier = pltpu.get_barrier_semaphore()

    def signal(step, unused):
        pl.semaphore_signal(
            barrier, inc=1, device_id=((me + step) % count,), device_id_type=MESH
        )
        return unused

    lax.fori_loop(1, count, signal, 0)
    pl.semaphore_wait(barrier, count - 1)


def params(collective_id):
    return pltpu.CompilerParams(collective_id=collective_id, has_side_effects=True)


ANYSPEC = pl.BlockSpec(memory_space=pl.ANY)
VSPEC = pl.BlockSpec(memory_space=pltpu.VMEM)


FAR = (2, 4, 6)


def gather_start(place, base, block, out, sems):
    local, send, recv = sems[:3]
    pltpu.make_async_copy(block, out.at[place], local).start()
    for slot, mask in enumerate(FAR + (1,)):
        remote(
            block, out.at[place], send.at[slot], recv.at[slot], base + flip(place, mask)
        ).start()


def gather_finish(place, base, block, out, sems):
    local, send, recv, pass_send, pass_recv = sems
    for slot, mask in enumerate(FAR):
        came = out.at[flip(place, mask)]
        remote(block, came, send.at[slot], recv.at[slot], base + place).wait_recv()
        remote(
            came, came, pass_send.at[slot], pass_recv.at[slot], base + flip(place, 1)
        ).start()
    pltpu.make_async_copy(block, out.at[place], local).wait()
    for slot, mask in enumerate(FAR + (1,)):
        remote(block, out.at[place], send.at[slot], recv.at[slot], base + place).wait_send()
    remote(block, out.at[place], send.at[3], recv.at[3], base + place).wait_recv()
    for slot, mask in enumerate(FAR):
        came = out.at[flip(place, mask)]
        remote(came, came, pass_send.at[slot], pass_recv.at[slot], base + place).wait()


def gather_sems():
    return [DMA, DMA((4,)), DMA((4,)), DMA((3,)), DMA((3,))]


def gather_kernel(x_ref, out_ref, *sems):
    me = lax.axis_index("fsdp")
    place = me % GROUP
    base = me - place
    greet([base + flip(place, mask) for mask in FAR + (1,)])
    gather_start(place, base, x_ref, out_ref, sems)
    gather_finish(place, base, x_ref, out_ref, sems)


def plane_gather(block, collective_id):
    return pl.pallas_call(
        gather_kernel,
        out_shape=jax.ShapeDtypeStruct((GROUP,) + block.shape, block.dtype),
        in_specs=[VSPEC],
        out_specs=ANYSPEC,
        scratch_shapes=gather_sems(),
        compiler_params=params(collective_id),
        name=f"plane_gather_{collective_id}",
    )(block)


def scatter_kernel(count, *refs):
    parts = refs[:count]
    outs = refs[count : 2 * count]
    rest = refs[2 * count :]
    me = lax.axis_index("fsdp")
    place = me % GROUP
    base = me - place
    greet([base + flip(place, mask) for mask in FAR + (1,)])
    held = []
    for which in range(count):
        sib, stage, got, sib_send, sib_recv, send, recv = rest[7 * which : 7 * which + 7]
        part = parts[which]
        for slot, mask in enumerate(FAR + (0,)):
            remote(
                part.at[flip(place, mask ^ 1)],
                sib.at[slot],
                sib_send.at[slot],
                sib_recv.at[slot],
                base + flip(place, 1),
            ).start()
        held.append((part, outs[which], sib, stage, got, sib_send, sib_recv, send, recv))
    rows = parts[0].shape[1]
    step = 32
    for part, out, sib, stage, got, sib_send, sib_recv, send, recv in held:
        for slot, mask in enumerate(FAR):
            remote(
                part.at[0], sib.at[slot], sib_send.at[slot], sib_recv.at[slot], me
            ).wait_recv()
            target = flip(place, mask)

            def add(index, unused, part=part, sib=sib, stage=stage, slot=slot, target=target):
                span = pl.ds(pl.multiple_of(index * step, step), step)
                stage[slot, span, :] = (
                    part[target, span, :].astype(f32) + sib[slot, span, :].astype(f32)
                ).astype(bf16)
                return unused

            lax.fori_loop(0, rows // step, add, 0)
            remote(
                stage.at[slot], got.at[slot], send.at[slot], recv.at[slot], base + target
            ).start()
    for part, out, sib, stage, got, sib_send, sib_recv, send, recv in held:
        remote(part.at[0], sib.at[3], sib_send.at[3], sib_recv.at[3], me).wait_recv()
        for slot in range(3):
            remote(stage.at[slot], got.at[slot], send.at[slot], recv.at[slot], me).wait_recv()

        def total(index, unused, part=part, sib=sib, got=got, out=out):
            span = pl.ds(pl.multiple_of(index * step, step), step)
            value = part[place, span, :].astype(f32) + sib[3, span, :].astype(f32)
            for slot in range(3):
                value = value + got[slot, span, :].astype(f32)
            out[span, :] = value
            return unused

        lax.fori_loop(0, rows // step, total, 0)
    for part, out, sib, stage, got, sib_send, sib_recv, send, recv in held:
        for slot in range(4):
            remote(part.at[0], sib.at[slot], sib_send.at[slot], sib_recv.at[slot], me).wait_send()
        for slot in range(3):
            remote(stage.at[slot], got.at[slot], send.at[slot], recv.at[slot], me).wait_send()


def plane_scatter(parts, collective_id):
    rows, width = parts[0].shape[1:]
    scratch = []
    for part in parts:
        scratch += [
            VMEM((4, rows, width), bf16),
            VMEM((3, rows, width), bf16),
            VMEM((3, rows, width), bf16),
            DMA((4,)),
            DMA((4,)),
            DMA((3,)),
            DMA((3,)),
        ]
    return pl.pallas_call(
        functools.partial(scatter_kernel, len(parts)),
        out_shape=[jax.ShapeDtypeStruct((rows, width), f32) for part in parts],
        in_specs=[VSPEC] * len(parts),
        out_specs=[VSPEC] * len(parts),
        scratch_shapes=scratch,
        compiler_params=params(collective_id),
        name=f"plane_scatter_{collective_id}",
    )(*parts)


def line_gather(me, groups, outs, sems):
    mine = me // GROUP
    for step in range(groups - 1):
        for which, out in enumerate(outs):
            up_send, up_recv, down_send, down_recv = sems[4 * which : 4 * which + 4]

            @pl.when((mine - step >= 0) & (mine + 1 < groups))
            def _(out=out, up_send=up_send, up_recv=up_recv):
                slab = out.at[mine - step]
                remote(slab, slab, up_send.at[step], up_recv.at[step], me + GROUP).start()

            @pl.when((mine + step < groups) & (mine >= 1))
            def _(out=out, down_send=down_send, down_recv=down_recv):
                slab = out.at[mine + step]
                remote(slab, slab, down_send.at[step], down_recv.at[step], me - GROUP).start()

        for which, out in enumerate(outs):
            up_send, up_recv, down_send, down_recv = sems[4 * which : 4 * which + 4]

            @pl.when(mine - 1 - step >= 0)
            def _(out=out, up_send=up_send, up_recv=up_recv):
                slab = out.at[mine - 1 - step]
                remote(slab, slab, up_send.at[step], up_recv.at[step], me).wait_recv()

            @pl.when(mine + 1 + step < groups)
            def _(out=out, down_send=down_send, down_recv=down_recv):
                slab = out.at[mine + 1 + step]
                remote(slab, slab, down_send.at[step], down_recv.at[step], me).wait_recv()


def line_gather_drain(me, groups, outs, sems):
    mine = me // GROUP
    for step in range(groups - 1):
        for which, out in enumerate(outs):
            up_send, up_recv, down_send, down_recv = sems[4 * which : 4 * which + 4]

            @pl.when((mine - step >= 0) & (mine + 1 < groups))
            def _(out=out, up_send=up_send, up_recv=up_recv):
                slab = out.at[0]
                remote(slab, slab, up_send.at[step], up_recv.at[step], me).wait_send()

            @pl.when((mine + step < groups) & (mine >= 1))
            def _(out=out, down_send=down_send, down_recv=down_recv):
                slab = out.at[0]
                remote(slab, slab, down_send.at[step], down_recv.at[step], me).wait_send()


def line_sems(groups, arrays):
    return [DMA((groups,))] * (4 * arrays)


def spread_start(me, place, base, pack, out, local, send, recv):
    slot_of = me // GROUP
    pltpu.make_async_copy(pack.at[place], out.at[slot_of, place], local).start()
    for mask in range(1, GROUP):
        target = flip(place, mask)
        remote(
            pack.at[target],
            out.at[slot_of, place],
            send.at[mask],
            recv.at[mask],
            base + target,
        ).start()


def spread_wait(me, place, base, pack, out, local, send, recv):
    slot_of = me // GROUP
    pltpu.make_async_copy(pack.at[place], out.at[slot_of, place], local).wait()
    for mask in range(1, GROUP):
        source = flip(place, mask)
        remote(
            pack.at[source], out.at[slot_of, source], send.at[mask], recv.at[mask], base + place
        ).wait()


def fetch_kernel(
    count,
    x_ref,
    ct_ref,
    qkv_ref,
    up_ref,
    down_ref,
    out_ref,
    x_all,
    ct_all,
    qkv_all,
    up_all,
    down_all,
    out_all,
    *sems,
):
    groups = count // GROUP
    me = lax.axis_index("fsdp")
    place = me % GROUP
    base = me - place
    mine = me // GROUP
    x_sems, sems = sems[:5], sems[5:]
    ct_sems, sems = sems[:5], sems[5:]
    qkv_sems, sems = sems[:3], sems[3:]
    up_sems, sems = sems[:3], sems[3:]
    line_q, sems = sems[:4], sems[4:]
    line_u, sems = sems[:8], sems[8:]
    down_local, out_local, out_send, out_recv = sems
    greet_all(me, count)
    spread_start(me, place, base, qkv_ref, qkv_all, *qkv_sems)
    gather_start(place, base, x_ref, x_all, x_sems)
    pltpu.make_async_copy(down_ref, down_all.at[mine], down_local).start()
    per = count // GROUP
    wanted = me // per
    slot = me % per
    for group in range(groups):
        target = group * GROUP + wanted

        @pl.when(target != me)
        def _(target=target, group=group):
            remote(
                out_ref, out_all.at[slot], out_send.at[group], out_recv.at[slot], target
            ).start()

        @pl.when(target == me)
        def _(target=target, group=group):
            pltpu.make_async_copy(out_ref, out_all.at[slot], out_local).start()

    spread_wait(me, place, base, qkv_ref, qkv_all, *qkv_sems)
    spread_start(me, place, base, up_ref, up_all, *up_sems)
    line_gather(me, groups, [qkv_all], line_q)
    gather_finish(place, base, x_ref, x_all, x_sems)
    gather_start(place, base, ct_ref, ct_all, ct_sems)
    spread_wait(me, place, base, up_ref, up_all, *up_sems)
    pltpu.make_async_copy(down_ref, down_all.at[mine], down_local).wait()
    line_gather(me, groups, [up_all, down_all], line_u)
    gather_finish(place, base, ct_ref, ct_all, ct_sems)
    line_gather_drain(me, groups, [qkv_all], line_q)
    line_gather_drain(me, groups, [up_all, down_all], line_u)
    for group in range(groups):
        target = group * GROUP + wanted

        @pl.when(target != me)
        def _(group=group):
            remote(
                out_ref, out_all.at[slot], out_send.at[group], out_recv.at[slot], me
            ).wait_send()

        @pl.when(target == me)
        def _():
            pltpu.make_async_copy(out_ref, out_all.at[slot], out_local).wait()

    for index in range(per):
        owner = place * per + index

        @pl.when(owner != me)
        def _(index=index):
            remote(
                out_ref, out_all.at[index], out_send.at[0], out_recv.at[index], me
            ).wait_recv()


def fetch(count, x, ct, qkv, up, down, out, collective_id):
    groups = count // GROUP

    def shaped(*shape):
        return jax.ShapeDtypeStruct(shape, bf16)

    return pl.pallas_call(
        functools.partial(fetch_kernel, count),
        out_shape=[
            shaped(GROUP, *x.shape),
            shaped(GROUP, *ct.shape),
            shaped(groups, *qkv.shape),
            shaped(groups, *up.shape),
            shaped(groups, *down.shape),
            shaped(groups, *out.shape),
        ],
        in_specs=[VSPEC] * 6,
        out_specs=[ANYSPEC] * 6,
        scratch_shapes=gather_sems()
        + gather_sems()
        + [DMA, DMA((GROUP,)), DMA((GROUP,))] * 2
        + line_sems(groups, 1)
        + line_sems(groups, 2)
        + [DMA, DMA, DMA((groups,)), DMA((groups,))],
        compiler_params=params(collective_id),
        name="fetch",
    )(x, ct, qkv, up, down, out)


def add_slabs(blocks, store, *terms):
    def body(index, unused):
        value = terms[0](index).astype(f32)
        for term in terms[1:]:
            value = value + term(index).astype(f32)
        store(index, value)
        return unused

    lax.fori_loop(0, blocks, body, 0)


def line_sum(me, groups, own, stage, from_low, from_high, sems):
    up_send, up_recv, down_send, down_recv = sems
    mine = me // GROUP
    blocks = own.shape[1]

    def add(target, other):
        def store(index, value):
            stage[target, index] = value.astype(bf16)

        add_slabs(blocks, store, lambda index: own[target, index], lambda index: other[target, index])

    for target in range(groups - 1, 0, -1):
        low = groups - 1 - target

        def up(src, target=target):
            return remote(
                src.at[target],
                from_low.at[target],
                up_send.at[target],
                up_recv.at[target],
                me + GROUP,
            )

        def down(src, low=low):
            return remote(
                src.at[low], from_high.at[low], down_send.at[low], down_recv.at[low], me - GROUP
            )

        @pl.when((mine < target) & (mine == 0))
        def _(up=up):
            up(own).start()

        @pl.when((mine > low) & (mine == groups - 1))
        def _(down=down):
            down(own).start()

        @pl.when((mine < target) & (mine > 0))
        def _(up=up, target=target):
            up(own).wait_recv()
            add(target, from_low)
            up(stage).start()

        @pl.when((mine > low) & (mine < groups - 1))
        def _(down=down, low=low):
            down(own).wait_recv()
            add(low, from_high)
            down(stage).start()


def line_sum_finish(me, groups, own, from_low, from_high, total, sems):
    up_send, up_recv, down_send, down_recv = sems
    mine = me // GROUP
    blocks = own.shape[1]

    def store(index, value):
        total[index] = value

    def put(index, value):
        total[index] = total[index] + value

    add_slabs(blocks, store, lambda index: own[mine, index])
    for target in range(groups):
        low_copy = remote(
            own.at[target], from_low.at[target], up_send.at[target], up_recv.at[target], me
        )
        high_copy = remote(
            own.at[target], from_high.at[target], down_send.at[target], down_recv.at[target], me
        )

        @pl.when((mine == target) & (mine > 0))
        def _(low_copy=low_copy, target=target):
            low_copy.wait_recv()
            add_slabs(blocks, put, lambda index: from_low[target, index])

        @pl.when((mine == target) & (mine < groups - 1))
        def _(high_copy=high_copy, target=target):
            high_copy.wait_recv()
            add_slabs(blocks, put, lambda index: from_high[target, index])

        @pl.when(mine < target)
        def _(low_copy=low_copy):
            low_copy.wait_send()

        @pl.when(mine > target)
        def _(high_copy=high_copy):
            high_copy.wait_send()


def return_kernel(
    count,
    cols_ref,
    down_ref,
    out_ref,
    vec_ref,
    cols_all,
    down_total,
    out_all,
    vec_all,
    cols_stage,
    cols_low,
    cols_high,
    cols_total,
    cols_send,
    down_stage,
    down_low,
    down_high,
    *sems,
):
    groups = count // GROUP
    per = count // GROUP
    me = lax.axis_index("fsdp")
    place = me % GROUP
    base = me - place
    mine = me // GROUP
    line_c, line_d = sems[:4], sems[4:8]
    swap_local, swap_send, swap_recv = sems[8:11]
    out_local, out_send, out_recv = sems[11:14]
    vec_local, vec_send, vec_recv = sems[14:17]
    greet_all(me, count)

    def vec_copy(step):
        target = (me + step) % count
        return remote(
            vec_ref.at[target], vec_all.at[me], vec_send.at[step], vec_recv.at[step], target
        )

    def vec_start(step, unused):
        vec_copy(step).start()
        return unused

    lax.fori_loop(1, count, vec_start, 0)
    own_vec = pltpu.make_async_copy(vec_ref.at[me], vec_all.at[me], vec_local)
    own_vec.start()
    for index in range(per):
        owner = place * per + index

        @pl.when(owner != me)
        def _(index=index, owner=owner):
            remote(
                out_ref.at[index], out_all.at[mine], out_send.at[index], out_recv.at[mine], owner
            ).start()

        @pl.when(owner == me)
        def _(index=index):
            pltpu.make_async_copy(out_ref.at[index], out_all.at[mine], out_local).start()

    line_sum(me, groups, cols_ref, cols_stage, cols_low, cols_high, line_c)
    line_sum(me, groups, down_ref, down_stage, down_low, down_high, line_d)
    line_sum_finish(me, groups, cols_ref, cols_low, cols_high, cols_total, line_c)

    def narrow(index, value):
        cols_send[index] = value.astype(bf16)

    add_slabs(GROUP, narrow, lambda index: cols_total[index])
    own_cols = pltpu.make_async_copy(cols_send.at[place], cols_all.at[place], swap_local)
    own_cols.start()
    swaps = []
    for mask in range(1, GROUP):
        target = flip(place, mask)
        swap = remote(
            cols_send.at[target],
            cols_all.at[place],
            swap_send.at[mask],
            swap_recv.at[mask],
            base + target,
        )
        swap.start()
        swaps.append(swap)
    line_sum_finish(me, groups, down_ref, down_low, down_high, down_total, line_d)
    own_cols.wait()
    for swap in swaps:
        swap.wait()
    own_vec.wait()

    def vec_wait(step, unused):
        vec_copy(step).wait()
        return unused

    lax.fori_loop(1, count, vec_wait, 0)
    for index in range(per):
        owner = place * per + index

        @pl.when(owner != me)
        def _(index=index):
            remote(
                out_ref.at[index], out_all.at[mine], out_send.at[index], out_recv.at[mine], me
            ).wait_send()

        @pl.when(owner == me)
        def _(index=index):
            pltpu.make_async_copy(out_ref.at[index], out_all.at[mine], out_local).wait()

    wanted = me // per
    for group in range(groups):

        @pl.when(group * GROUP + wanted != me)
        def _(group=group):
            remote(
                out_ref.at[0], out_all.at[group], out_send.at[0], out_recv.at[group], me
            ).wait_recv()


def give_back(count, cols, down, out, vec, collective_id):
    groups = count // GROUP

    def line(array, kind=bf16):
        return VMEM(array.shape, kind)

    return pl.pallas_call(
        functools.partial(return_kernel, count),
        out_shape=[
            jax.ShapeDtypeStruct(cols.shape[1:], bf16),
            jax.ShapeDtypeStruct(down.shape[1:], f32),
            jax.ShapeDtypeStruct((groups,) + out.shape[1:], bf16),
            jax.ShapeDtypeStruct(vec.shape, f32),
        ],
        in_specs=[VSPEC] * 4,
        out_specs=[VSPEC] * 4,
        scratch_shapes=[
            line(cols),
            line(cols),
            line(cols),
            VMEM(cols.shape[1:], f32),
            VMEM(cols.shape[1:], bf16),
            line(down),
            line(down),
            line(down),
        ]
        + line_sems(groups, 2)
        + [DMA, DMA((GROUP,)), DMA((GROUP,))]
        + [DMA, DMA((groups,)), DMA((groups,))]
        + [DMA, DMA((count,)), DMA((count,))],
        compiler_params=params(collective_id),
        name="give_back",
    )(cols, down, out, vec)


QBLOCK = 256


def attend_kernel(length_ref, query_ref, key_ref, value_ref, mixed_ref, log_ref):
    length = length_ref[0]
    score_scale = 1.0 / math.sqrt(HD)
    scores = times_transposed(query_ref[...], key_ref[...]) * score_scale
    tail = scores[:, SURE:]
    place = SURE + lax.broadcasted_iota(jnp.int32, tail.shape, 1)
    scores = jnp.concatenate(
        [scores[:, :SURE], jnp.where(place < length, tail, masked_value)], axis=1
    )
    largest = jnp.max(scores, axis=-1, keepdims=True)
    exponent = jnp.exp(scores - largest)
    total = jnp.sum(exponent, axis=-1, keepdims=True)
    weights = (exponent * (1.0 / total)).astype(bf16)
    mixed_ref[...] = matmul(weights, value_ref[...]).astype(bf16)
    log_ref[0] = largest + jnp.log(total)


def attend(length, qkv):
    rows = qkv.shape[0]
    heads = HEADS_HERE
    return pl.pallas_call(
        attend_kernel,
        out_shape=[
            jax.ShapeDtypeStruct((rows, heads * LANES), bf16),
            jax.ShapeDtypeStruct((heads, rows, 1), f32),
        ],
        grid=(heads, rows // QBLOCK),
        in_specs=[
            pl.BlockSpec(memory_space=pltpu.SMEM),
            pl.BlockSpec((QBLOCK, LANES), lambda h, i: (i, h)),
            pl.BlockSpec((rows, LANES), lambda h, i: (0, heads + h)),
            pl.BlockSpec((rows, LANES), lambda h, i: (0, 2 * heads + h)),
        ],
        out_specs=[
            pl.BlockSpec((QBLOCK, LANES), lambda h, i: (i, h)),
            pl.BlockSpec((1, QBLOCK, 1), lambda h, i: (h, i, 0)),
        ],
        name="attend",
    )(length, qkv, qkv, qkv)


def attend_back_kernel(
    length_ref,
    query_ref,
    key_ref,
    value_ref,
    grad_ref,
    log_ref,
    grad_query_ref,
    grad_key_ref,
    grad_value_ref,
    key_sum,
    value_sum,
):
    length = length_ref[0]
    block = pl.program_id(1)
    score_scale = 1.0 / math.sqrt(HD)
    query = query_ref[...]
    key = key_ref[...]
    grad = grad_ref[...]
    scores = times_transposed(query, key) * score_scale
    tail = scores[:, SURE:]
    place = SURE + lax.broadcasted_iota(jnp.int32, tail.shape, 1)
    scores = jnp.concatenate(
        [scores[:, :SURE], jnp.where(place < length, tail, masked_value)], axis=1
    )
    weights = jnp.exp(scores - log_ref[0])
    grad_weights = times_transposed(grad, value_ref[...])
    inner = jnp.sum(weights * grad_weights, axis=-1, keepdims=True)
    grad_scores = (weights * (grad_weights - inner)).astype(bf16)
    grad_query_ref[...] = (matmul(grad_scores, key) * score_scale).astype(bf16)

    @pl.when(block == 0)
    def _():
        key_sum[...] = jnp.zeros_like(key_sum)
        value_sum[...] = jnp.zeros_like(value_sum)

    key_sum[...] += outer_sum(grad_scores, query)
    value_sum[...] += outer_sum(weights.astype(bf16), grad)

    @pl.when(block == pl.num_programs(1) - 1)
    def _():
        grad_key_ref[...] = (key_sum[...] * score_scale).astype(bf16)
        grad_value_ref[...] = value_sum[...].astype(bf16)


def attend_back(length, qkv, grad, log):
    rows = qkv.shape[0]
    heads = HEADS_HERE
    shape = jax.ShapeDtypeStruct((rows, heads * LANES), bf16)
    return pl.pallas_call(
        attend_back_kernel,
        out_shape=[shape] * 3,
        grid=(heads, rows // QBLOCK),
        in_specs=[
            pl.BlockSpec(memory_space=pltpu.SMEM),
            pl.BlockSpec((QBLOCK, LANES), lambda h, i: (i, h)),
            pl.BlockSpec((rows, LANES), lambda h, i: (0, heads + h)),
            pl.BlockSpec((rows, LANES), lambda h, i: (0, 2 * heads + h)),
            pl.BlockSpec((QBLOCK, LANES), lambda h, i: (i, h)),
            pl.BlockSpec((1, QBLOCK, 1), lambda h, i: (h, i, 0)),
        ],
        out_specs=[
            pl.BlockSpec((QBLOCK, LANES), lambda h, i: (i, h)),
            pl.BlockSpec((rows, LANES), lambda h, i: (0, h)),
            pl.BlockSpec((rows, LANES), lambda h, i: (0, h)),
        ],
        scratch_shapes=[VMEM((rows, LANES), f32), VMEM((rows, LANES), f32)],
        name="attend_back",
    )(length, qkv, qkv, qkv, grad, log)


def layer_norm(values, gain, offset):
    average = jnp.mean(values, axis=-1, keepdims=True)
    centred = values - average
    variance = jnp.mean(centred * centred, axis=-1, keepdims=True)
    return centred * lax.rsqrt(variance + epsilon) * gain + offset


def norm_backward(values, gain, grad_out):
    average = jnp.mean(values, axis=-1, keepdims=True)
    centred = values - average
    inverse = lax.rsqrt(jnp.mean(centred * centred, axis=-1, keepdims=True) + epsilon)
    xhat = centred * inverse
    scaled = grad_out * gain
    grad_values = inverse * (
        scaled
        - jnp.mean(scaled, axis=-1, keepdims=True)
        - xhat * jnp.mean(scaled * xhat, axis=-1, keepdims=True)
    )
    return grad_values, jnp.sum(grad_out * xhat, axis=0), jnp.sum(grad_out, axis=0)


def gelu_exact(values):
    return jax.nn.gelu(values, approximate=False)


def column_sums(matrix):
    return jnp.sum(matrix.astype(f32), axis=0)


def widen(cols, count):
    lead = cols.shape[:-1]
    split = cols.reshape(lead + (count, HD))
    return jnp.pad(split, [(0, 0)] * (len(lead) + 1) + [(0, LANES - HD)]).reshape(
        lead + (count * LANES,)
    )


def narrow(cols, count):
    lead = cols.shape[:-1]
    return cols.reshape(lead + (count, LANES))[..., :HD].reshape(lead + (count * HD,))


def on_device(
    inputs,
    ln1_gain,
    ln1_bias,
    w_query,
    b_query,
    w_key,
    w_value,
    b_value,
    w_out,
    b_out,
    ln2_gain,
    ln2_bias,
    w_up,
    b_up,
    w_down,
    b_down,
    lengths,
    cotangent,
):
    count = lax.axis_size("fsdp")
    groups = count // GROUP
    me = lax.axis_index("fsdp")
    place = me % GROUP
    few = w_query.shape[0]
    many = w_down.shape[0]
    rows = inputs.shape[0]
    wide = 3 * HEAD_COLS
    ff_here = groups * many

    qkv_pack = (
        jnp.stack([w_query, w_key, w_value], axis=1)
        .astype(bf16)
        .reshape(few, 3, GROUP, HEAD_COLS)
        .transpose(2, 0, 1, 3)
        .reshape(GROUP, few, wide)
    )
    small = (ln1_gain, ln1_bias, b_query, b_value, b_out, ln2_gain, ln2_bias, b_down, b_up)
    small = jnp.concatenate(small).astype(bf16)
    small_pack = jnp.broadcast_to(
        jnp.pad(small, (0, wide - small.shape[0]))[None, None], (GROUP, 1, wide)
    )
    qkv_pack = jnp.concatenate([qkv_pack, small_pack], axis=1)
    up_pack = (
        w_up.astype(bf16)
        .reshape(few, groups, GROUP, many)
        .transpose(2, 0, 1, 3)
        .reshape(GROUP, few, ff_here)
    )
    x_all, ct_all, qkv_all, up_all, down_all, out_all = fetch(
        count,
        inputs,
        cotangent,
        qkv_pack,
        up_pack,
        w_down.astype(bf16),
        w_out.astype(bf16),
        0,
    )
    w_qkv = widen(qkv_all[:, :, :few].reshape(D, wide), 3 * HEADS_HERE)
    small_all = qkv_all[:, :, few].reshape(count, wide).astype(f32)
    whole = [small_all[:, i * few : (i + 1) * few].reshape(D) for i in range(8)]
    g1, o1, bq, bv, bo, g2, o2, bd = whole
    b_up_all = small_all[:, 8 * few : 8 * few + many].reshape(groups, GROUP, many)
    b_up_here = lax.dynamic_index_in_dim(b_up_all, place, 1, keepdims=False).reshape(ff_here)
    w_up_here = up_all.reshape(D, ff_here)
    w_down_here = down_all.reshape(ff_here, D)
    w_out_here = out_all.reshape(HEADS_HERE, HD, D)
    w_out_here = jnp.pad(w_out_here, ((0, 0), (0, LANES - HD), (0, 0))).reshape(
        HEADS_HERE * LANES, D
    )

    def head_slice(vector):
        return lax.dynamic_slice_in_dim(vector, place * HEAD_COLS, HEAD_COLS)

    b_qkv = jnp.concatenate([head_slice(bq), jnp.zeros((HEAD_COLS,), f32), head_slice(bv)])
    b_qkv = widen(b_qkv, 3 * HEADS_HERE)
    length = lax.dynamic_slice_in_dim(lengths, me // GROUP, 1)

    clip = x_all.reshape(GROUP * rows, D).astype(f32)
    normed = layer_norm(clip, g1, o1).astype(bf16)
    qkv = (matmul(normed, w_qkv) + b_qkv).astype(bf16)
    attended, log = attend(length, qkv)
    part = matmul(attended, w_out_here).astype(bf16).reshape(GROUP, rows, D)
    (branch,) = plane_scatter([part], 1)
    source = inputs.astype(f32)
    residual = source + (branch + bo)
    normed_two_rows = layer_norm(residual, g2, o2).astype(bf16)
    normed_two = plane_gather(normed_two_rows, 2).reshape(GROUP * rows, D)
    ct = ct_all.reshape(GROUP * rows, D)
    hidden = matmul(normed_two, w_up_here) + b_up_here
    activated = gelu_exact(hidden).astype(bf16)
    out_part = matmul(activated, w_down_here).astype(bf16).reshape(GROUP, rows, D)

    grad_activated = times_transposed(ct, w_down_here)
    unused, gelu_pullback = jax.vjp(gelu_exact, hidden)
    grad_hidden = gelu_pullback(grad_activated)[0].astype(bf16)
    two_part = times_transposed(grad_hidden, w_up_here).astype(bf16).reshape(GROUP, rows, D)
    branch_two, grad_normed_two = plane_scatter([out_part, two_part], 3)
    output = residual + (branch_two + bd)
    grad_second, grad_g2, grad_o2 = norm_backward(residual, g2, grad_normed_two)
    grad_residual = cotangent.astype(f32) + grad_second
    grad_branch_rows = grad_residual.astype(bf16)
    grad_branch = plane_gather(grad_branch_rows, 4).reshape(GROUP * rows, D)
    grad_attended = times_transposed(grad_branch, w_out_here).astype(bf16)
    grad_parts = attend_back(length, qkv, grad_attended, log)
    grad_qkv = jnp.concatenate(grad_parts, axis=1)
    one_part = times_transposed(grad_qkv, w_qkv).astype(bf16).reshape(GROUP, rows, D)
    (grad_normed,) = plane_scatter([one_part], 5)
    grad_first, grad_g1, grad_o1 = norm_backward(source, g1, grad_normed)
    grad_inputs = grad_residual + grad_first

    grad_w_qkv = narrow(outer_sum(normed, grad_qkv), 3 * HEADS_HERE).astype(bf16)
    grad_w_up = outer_sum(normed_two, grad_hidden).astype(bf16)
    cols = jnp.concatenate([grad_w_qkv, grad_w_up], axis=1).reshape(
        groups, GROUP, few, wide + ff_here
    )
    down = outer_sum(activated, ct).astype(bf16).reshape(groups, many // few, few, D)
    out = outer_sum(attended, grad_branch).astype(bf16)
    out = out.reshape(HEADS_HERE, LANES, D)[:, :HD].reshape(groups, few, D)
    grad_b = narrow(column_sums(grad_qkv), 3 * HEADS_HERE)

    def spread_heads(part):
        return lax.dynamic_update_slice_in_dim(
            jnp.zeros((D,), f32), part, place * HEAD_COLS, 0
        ).reshape(count, few)

    grad_b_up = lax.dynamic_update_slice_in_dim(
        jnp.zeros((groups, GROUP, many), f32),
        column_sums(grad_hidden).reshape(groups, 1, many),
        place,
        1,
    ).reshape(count, many)
    vec = jnp.concatenate(
        [
            grad_g1.reshape(count, few),
            grad_o1.reshape(count, few),
            spread_heads(grad_b[:HEAD_COLS]),
            spread_heads(grad_b[2 * HEAD_COLS :]),
            column_sums(grad_branch_rows).reshape(count, few),
            grad_g2.reshape(count, few),
            grad_o2.reshape(count, few),
            column_sums(cotangent).reshape(count, few),
            grad_b_up,
        ],
        axis=1,
    )
    vec = jnp.pad(vec, ((0, 0), (0, 4 * LANES - vec.shape[1]))).reshape(count, 4, LANES)
    cols_all, down_total, out_got, vec_all = give_back(count, cols, down, out, vec, 6)
    cols_all = cols_all.astype(f32)

    def shard_of(which):
        piece = cols_all[:, :, which * HEAD_COLS : (which + 1) * HEAD_COLS]
        return piece.transpose(1, 0, 2).reshape(few, D)

    shard_w_up = (
        cols_all[:, :, wide:]
        .reshape(GROUP, few, groups, many)
        .transpose(1, 2, 0, 3)
        .reshape(few, groups * GROUP * many)
    )
    shard_w_out = jnp.sum(out_got.astype(f32), axis=0)
    vec_sum = jnp.sum(vec_all, axis=0).reshape(4 * LANES)
    shards = [vec_sum[i * few : (i + 1) * few] for i in range(8)]
    sg1, so1, sbq, sbv, sbo, sg2, so2, sbd = shards
    return (
        output,
        grad_inputs,
        sg1,
        so1,
        shard_of(0),
        sbq,
        shard_of(1),
        shard_of(2),
        sbv,
        shard_w_out,
        sbo,
        sg2,
        so2,
        shard_w_up,
        vec_sum[8 * few : 8 * few + many],
        down_total.reshape(many, D),
        sbd,
    )


def solution(mesh):
    in_specs = (
        P("fsdp", None),
        P("fsdp"),
        P("fsdp"),
        P("fsdp", None),
        P("fsdp"),
        P("fsdp", None),
        P("fsdp", None),
        P("fsdp"),
        P("fsdp", None),
        P("fsdp"),
        P("fsdp"),
        P("fsdp"),
        P("fsdp", None),
        P("fsdp"),
        P("fsdp", None),
        P("fsdp"),
        P(),
        P("fsdp", None),
    )
    out_specs = (
        P("fsdp", None),
        P("fsdp", None),
        P("fsdp"),
        P("fsdp"),
        P("fsdp", None),
        P("fsdp"),
        P("fsdp", None),
        P("fsdp", None),
        P("fsdp"),
        P("fsdp", None),
        P("fsdp"),
        P("fsdp"),
        P("fsdp"),
        P("fsdp", None),
        P("fsdp"),
        P("fsdp", None),
        P("fsdp"),
    )
    return jax.shard_map(
        on_device, mesh=mesh, in_specs=in_specs, out_specs=out_specs, check_vma=False
    )
```

```python
import functools
import math

import jax
import jax.numpy as jnp
from jax import lax
from jax.experimental import pallas as pl
from jax.experimental.pallas import tpu as pltpu
from jax.sharding import PartitionSpec as P

D = 1280
H = 16
HD = 80
CLIP_LEN = 1536
GROUP = 8
LANES = 128
HEADS_HERE = H // GROUP
HEAD_COLS = HEADS_HERE * HD
SURE = CLIP_LEN * 3 // 4

epsilon = 1e-05
masked_value = -1e30
MESH = pl.DeviceIdType.MESH
VMEM = pltpu.VMEM
DMA = pltpu.SemaphoreType.DMA
bf16 = jnp.bfloat16
f32 = jnp.float32


def matmul(left, right):
    return jnp.dot(left, right, preferred_element_type=f32)


def outer_sum(left, right):
    return lax.dot_general(left, right, (((0,), (0,)), ((), ())), preferred_element_type=f32)


def times_transposed(left, right):
    return lax.dot_general(left, right, (((1,), (1,)), ((), ())), preferred_element_type=f32)


def flip(place, mask):
    for bit in (1, 2, 4):
        if mask & bit:
            place = place + bit - 2 * bit * (place // bit % 2)
    return place


def remote(src, dst, send_sem, recv_sem, target):
    return pltpu.make_async_remote_copy(
        src_ref=src,
        dst_ref=dst,
        send_sem=send_sem,
        recv_sem=recv_sem,
        device_id=(target,),
        device_id_type=MESH,
    )


def greet(targets):
    barrier = pltpu.get_barrier_semaphore()
    for target in targets:
        pl.semaphore_signal(barrier, inc=1, device_id=(target,), device_id_type=MESH)
    pl.semaphore_wait(barrier, len(targets))


def greet_all(me, count):
    barrier = pltpu.get_barrier_semaphore()

    def signal(step, unused):
        pl.semaphore_signal(
            barrier, inc=1, device_id=((me + step) % count,), device_id_type=MESH
        )
        return unused

    lax.fori_loop(1, count, signal, 0)
    pl.semaphore_wait(barrier, count - 1)


def params(collective_id):
    return pltpu.CompilerParams(collective_id=collective_id, has_side_effects=True)


ANYSPEC = pl.BlockSpec(memory_space=pl.ANY)
VSPEC = pl.BlockSpec(memory_space=pltpu.VMEM)


FAR = (2, 4, 6)
PIECES = ((0, 2), (1, 4), (1, 2), (0, 4), (0, 6), (1, 6))


def half_of(ref, owner, half):
    rows = ref.shape[1] // 2
    return ref.at[owner, pl.ds(half * rows, rows)]


def gather_sems():
    return [DMA, DMA, DMA, DMA((6,)), DMA((6,)), DMA((6,)), DMA((6,))]


def gather_piece(place, base, block, out, sems, slot):
    send, recv = sems[3:5]
    half, mask = PIECES[slot]
    rows = block.shape[0] // 2
    if slot < 4:
        src = block.at[pl.ds(half * rows, rows)]
        dst = half_of(out, place, half)
        target = flip(place, mask)
    else:
        near, far = (2, 4) if half == 0 else (4, 2)
        src = half_of(out, flip(place, near), half)
        dst = src
        target = flip(place, far)
    return remote(src, dst, send.at[slot], recv.at[slot], base + target)


def gather_pass(place, base, out, sems, slot):
    pass_send, pass_recv = sems[5:7]
    half, mask = PIECES[slot]
    piece = half_of(out, flip(place, mask), half)
    return remote(piece, piece, pass_send.at[slot], pass_recv.at[slot], base + flip(place, 1))


def gather_own(place, base, block, out, sems):
    return remote(block, out.at[place], sems[1], sems[2], base + flip(place, 1))


def gather_start(place, base, block, out, sems):
    for slot in (0, 1, 2, 3):
        gather_piece(place, base, block, out, sems, slot).start()
    pltpu.make_async_copy(block, out.at[place], sems[0]).start()
    gather_own(place, base, block, out, sems).start()


def gather_relay(place, base, block, out, sems):
    for slot, relay in ((0, 4), (1, 5)):
        gather_piece(place, base, block, out, sems, slot).wait_recv()
        gather_piece(place, base, block, out, sems, relay).start()
        gather_pass(place, base, out, sems, slot).start()


def gather_finish(place, base, block, out, sems):
    for slot in (2, 3, 4, 5):
        gather_piece(place, base, block, out, sems, slot).wait_recv()
        gather_pass(place, base, out, sems, slot).start()
    pltpu.make_async_copy(block, out.at[place], sems[0]).wait()
    gather_own(place, base, block, out, sems).wait()
    for slot in range(6):
        gather_piece(place, base, block, out, sems, slot).wait_send()
        gather_pass(place, base, out, sems, slot).wait()


def gather_kernel(x_ref, out_ref, *sems):
    me = lax.axis_index("fsdp")
    place = me % GROUP
    base = me - place
    greet([base + flip(place, mask) for mask in FAR + (1,)])
    gather_start(place, base, x_ref, out_ref, sems)
    gather_relay(place, base, x_ref, out_ref, sems)
    gather_finish(place, base, x_ref, out_ref, sems)


def plane_gather(block, collective_id):
    return pl.pallas_call(
        gather_kernel,
        out_shape=jax.ShapeDtypeStruct((GROUP,) + block.shape, block.dtype),
        in_specs=[VSPEC],
        out_specs=ANYSPEC,
        scratch_shapes=gather_sems(),
        compiler_params=params(collective_id),
        name=f"plane_gather_{collective_id}",
    )(block)


ORDER = (6, 2, 4, 0)


def row_loop(rows, step, body):
    def run(index, unused):
        body(pl.ds(pl.multiple_of(index * step, step), step))
        return unused

    lax.fori_loop(0, rows // step, run, 0)


def scatter_scratch(rows, width, ready=False):
    half = rows // 2
    return [
        VMEM((4, rows, width) if ready else (4, 2, rows, width), bf16),
        VMEM((4, rows, width), bf16),
        VMEM((2, half, width), bf16),
        VMEM((2, rows, width), bf16),
        DMA((4,)),
        DMA((4,)),
        DMA((4,)),
        DMA((6,)),
        DMA((6,)),
    ]


SCATTER = 9


class Scatter:
    def __init__(self, place, base, scratch, ready=None):
        self.place, self.base, self.ready = place, base, ready
        self.parts, self.sib, self.relay, self.got = scratch[:4]
        self.local, self.sib_send, self.sib_recv, self.send, self.recv = scratch[4:]
        self.rows = self.got.shape[1]
        self.half = self.rows // 2

    def block(self, i, other):
        return flip(flip(self.place, ORDER[i]), 1 if other else 0)

    def keep(self, i):
        return self.parts.at[i, 1] if self.ready is None else self.parts.at[i]

    def sibling(self, i):
        if self.ready is None:
            src = self.parts.at[i, 0]
        else:
            src = self.ready.at[self.block(i, True)]
        return remote(
            src,
            self.sib.at[i],
            self.sib_send.at[i],
            self.sib_recv.at[i],
            self.base + flip(self.place, 1),
        )

    def load(self, i):
        return pltpu.make_async_copy(
            self.ready.at[self.block(i, False)], self.keep(i), self.local.at[i]
        )

    def begin(self):
        for i in range(4):
            self.sibling(i).start()
            self.load(i).start()

    def link(self, slot):
        half = slot % 2
        span = pl.ds(half * self.half, self.half)
        if slot < 2:
            i, mask, dst = 0, (2, 4)[half], self.relay.at[half]
        else:
            i = slot // 2
            mask, dst = ORDER[i], self.got.at[i - 1, span]
        return remote(
            self.keep(i).at[span],
            dst,
            self.send.at[slot],
            self.recv.at[slot],
            self.base + flip(self.place, mask),
        )

    def merge(self, i):
        if self.ready is not None:
            self.load(i).wait()
        self.sibling(i).wait_recv()
        keep = self.keep(i)

        def body(span):
            keep[span, :] = (
                keep[span, :].astype(f32) + self.sib[i, span, :].astype(f32)
            ).astype(bf16)

        row_loop(self.rows, 32, body)

    def merge_relay(self, i, half):
        self.link(half).wait_recv()
        start = half * self.half
        keep = self.keep(i)

        def run(index, unused):
            here = pl.multiple_of(index * 32, 32)
            span = pl.ds(start + here, 32)
            keep[span, :] = (
                keep[span, :].astype(f32) + self.relay[half, pl.ds(here, 32), :].astype(f32)
            ).astype(bf16)
            return unused

        lax.fori_loop(0, self.half // 32, run, 0)

    def after(self, i):
        if i < 3:
            self.merge(i)
        if i == 0:
            self.link(0).start()
            self.link(1).start()
        if i == 1:
            self.link(2).start()
        if i == 2:
            self.link(5).start()
            self.merge_relay(1, 1)
            self.link(3).start()
            self.merge_relay(2, 0)
            self.link(4).start()

    def finish(self, use):
        if self.ready is not None:
            self.load(3).wait()
        self.sibling(3).wait_recv()
        for slot in range(2, 6):
            self.link(slot).wait_recv()
        keep = self.keep(3)

        def body(span):
            value = keep[span, :].astype(f32) + self.sib[3, span, :].astype(f32)
            value = value + self.got[0, span, :].astype(f32)
            use(span, value + self.got[1, span, :].astype(f32))

        row_loop(self.rows, 32, body)

    def drain(self):
        for i in range(4):
            self.sibling(i).wait_send()
        for slot in range(6):
            self.link(slot).wait_send()


def line_send(me, groups, outs, sems, step):
    mine = me // GROUP
    for which, out in enumerate(outs):
        up_send, up_recv, down_send, down_recv = sems[4 * which : 4 * which + 4]

        @pl.when((mine - step >= 0) & (mine + 1 < groups))
        def _(out=out, up_send=up_send, up_recv=up_recv):
            slab = out.at[mine - step]
            remote(slab, slab, up_send.at[step], up_recv.at[step], me + GROUP).start()

        @pl.when((mine + step < groups) & (mine >= 1))
        def _(out=out, down_send=down_send, down_recv=down_recv):
            slab = out.at[mine + step]
            remote(slab, slab, down_send.at[step], down_recv.at[step], me - GROUP).start()


def line_wait(me, groups, outs, sems, step):
    mine = me // GROUP
    for which, out in enumerate(outs):
        up_send, up_recv, down_send, down_recv = sems[4 * which : 4 * which + 4]

        @pl.when(mine - 1 - step >= 0)
        def _(out=out, up_send=up_send, up_recv=up_recv):
            slab = out.at[mine - 1 - step]
            remote(slab, slab, up_send.at[step], up_recv.at[step], me).wait_recv()

        @pl.when(mine + 1 + step < groups)
        def _(out=out, down_send=down_send, down_recv=down_recv):
            slab = out.at[mine + 1 + step]
            remote(slab, slab, down_send.at[step], down_recv.at[step], me).wait_recv()


def line_gather(me, groups, outs, sems):
    for step in range(groups - 1):
        line_send(me, groups, outs, sems, step)
        line_wait(me, groups, outs, sems, step)


def line_gather_drain(me, groups, outs, sems):
    mine = me // GROUP
    for step in range(groups - 1):
        for which, out in enumerate(outs):
            up_send, up_recv, down_send, down_recv = sems[4 * which : 4 * which + 4]

            @pl.when((mine - step >= 0) & (mine + 1 < groups))
            def _(out=out, up_send=up_send, up_recv=up_recv):
                slab = out.at[0]
                remote(slab, slab, up_send.at[step], up_recv.at[step], me).wait_send()

            @pl.when((mine + step < groups) & (mine >= 1))
            def _(out=out, down_send=down_send, down_recv=down_recv):
                slab = out.at[0]
                remote(slab, slab, down_send.at[step], down_recv.at[step], me).wait_send()


def line_sems(groups, arrays):
    return [DMA((groups,))] * (4 * arrays)


def spread_start(me, place, base, pack, out, local, send, recv):
    slot_of = me // GROUP
    pltpu.make_async_copy(pack.at[place], out.at[slot_of, place], local).start()
    for mask in range(1, GROUP):
        target = flip(place, mask)
        remote(
            pack.at[target],
            out.at[slot_of, place],
            send.at[mask],
            recv.at[mask],
            base + target,
        ).start()


def spread_wait(me, place, base, pack, out, local, send, recv):
    slot_of = me // GROUP
    pltpu.make_async_copy(pack.at[place], out.at[slot_of, place], local).wait()
    for mask in range(1, GROUP):
        source = flip(place, mask)
        remote(
            pack.at[source], out.at[slot_of, source], send.at[mask], recv.at[mask], base + place
        ).wait()


def greet_near(me, place, base, groups, masks):
    barrier = pltpu.get_barrier_semaphore()
    mine = me // GROUP
    for mask in masks:
        pl.semaphore_signal(
            barrier, inc=1, device_id=(base + flip(place, mask),), device_id_type=MESH
        )

    @pl.when(mine > 0)
    def _():
        pl.semaphore_signal(barrier, inc=1, device_id=(me - GROUP,), device_id_type=MESH)

    @pl.when(mine < groups - 1)
    def _():
        pl.semaphore_signal(barrier, inc=1, device_id=(me + GROUP,), device_id_type=MESH)

    both = jnp.where(mine > 0, 1, 0) + jnp.where(mine < groups - 1, 1, 0)
    pl.semaphore_wait(barrier, len(masks) + both)


def fetch_kernel(count, x_ref, qkv_ref, out_ref, x_all, qkv_all, out_all, *sems):
    groups = count // GROUP
    me = lax.axis_index("fsdp")
    place = me % GROUP
    base = me - place
    x_sems, sems = sems[:7], sems[7:]
    qkv_sems, sems = sems[:3], sems[3:]
    line_q, sems = sems[:4], sems[4:]
    out_local, out_send, out_recv = sems
    greet_all(me, count)
    spread_start(me, place, base, qkv_ref, qkv_all, *qkv_sems)
    gather_start(place, base, x_ref, x_all, x_sems)
    spread_wait(me, place, base, qkv_ref, qkv_all, *qkv_sems)
    line_send(me, groups, [qkv_all], line_q, 0)
    per = count // GROUP
    wanted = me // per
    slot = me % per
    for group in range(groups):
        target = group * GROUP + wanted

        @pl.when(target != me)
        def _(target=target, group=group):
            remote(
                out_ref, out_all.at[slot], out_send.at[group], out_recv.at[slot], target
            ).start()

        @pl.when(target == me)
        def _(target=target, group=group):
            pltpu.make_async_copy(out_ref, out_all.at[slot], out_local).start()

    line_wait(me, groups, [qkv_all], line_q, 0)
    gather_relay(place, base, x_ref, x_all, x_sems)
    for step in range(1, groups - 1):
        line_send(me, groups, [qkv_all], line_q, step)
        line_wait(me, groups, [qkv_all], line_q, step)
    gather_finish(place, base, x_ref, x_all, x_sems)
    line_gather_drain(me, groups, [qkv_all], line_q)
    for group in range(groups):
        target = group * GROUP + wanted

        @pl.when(target != me)
        def _(group=group):
            remote(
                out_ref, out_all.at[slot], out_send.at[group], out_recv.at[slot], me
            ).wait_send()

        @pl.when(target == me)
        def _():
            pltpu.make_async_copy(out_ref, out_all.at[slot], out_local).wait()

    for index in range(per):
        owner = place * per + index

        @pl.when(owner != me)
        def _(index=index):
            remote(
                out_ref, out_all.at[index], out_send.at[0], out_recv.at[index], me
            ).wait_recv()


def shaped(*shape, kind=bf16):
    return jax.ShapeDtypeStruct(shape, kind)


def fetch(count, x, qkv, out, collective_id):
    groups = count // GROUP
    return pl.pallas_call(
        functools.partial(fetch_kernel, count),
        out_shape=[
            shaped(GROUP, *x.shape),
            shaped(groups, *qkv.shape),
            shaped(groups, *out.shape),
        ],
        in_specs=[VSPEC] * 3,
        out_specs=[ANYSPEC] * 3,
        scratch_shapes=gather_sems()
        + [DMA, DMA((GROUP,)), DMA((GROUP,))]
        + line_sems(groups, 1)
        + [DMA, DMA((groups,)), DMA((groups,))],
        compiler_params=params(collective_id),
        name="fetch",
    )(x, qkv, out)


def add_slabs(blocks, store, *terms):
    def body(index, unused):
        value = terms[0](index).astype(f32)
        for term in terms[1:]:
            value = value + term(index).astype(f32)
        store(index, value)
        return unused

    lax.fori_loop(0, blocks, body, 0)


def line_sum_scratch(groups, slabs, rows, width):
    return [
        VMEM((groups + 1, slabs, rows, width), bf16),
        VMEM((slabs, rows, width), f32),
    ] + line_sems(groups, 1)


LINE_SUM = 6


class LineSum:
    def __init__(self, me, groups, own, scratch):
        self.me, self.groups, self.own = me, groups, own
        self.came, self.total = scratch[:2]
        self.up_send, self.up_recv, self.down_send, self.down_recv = scratch[2:]
        self.mine = me // GROUP
        self.blocks = own.shape[1]

    def up(self, target, src):
        return remote(
            src.at[target],
            self.came.at[target],
            self.up_send.at[target],
            self.up_recv.at[target],
            self.me + GROUP,
        )

    def down(self, target, src):
        last = jnp.where(self.mine - 1 == target, self.groups, target)
        return remote(
            src.at[target],
            self.came.at[last],
            self.down_send.at[target],
            self.down_recv.at[target],
            self.me - GROUP,
        )

    def add(self, target):
        def store(index, value):
            self.came[target, index] = value.astype(bf16)

        add_slabs(
            self.blocks,
            store,
            lambda index: self.own[target, index],
            lambda index: self.came[target, index],
        )

    def begin(self):
        for target in range(self.groups - 1, 0, -1):
            low = self.groups - 1 - target

            @pl.when((self.mine == 0))
            def _(target=target):
                self.up(target, self.own).start()

            @pl.when(self.mine == self.groups - 1)
            def _(low=low):
                self.down(low, self.own).start()

    def tasks(self):
        def step(target):
            low = self.groups - 1 - target

            @pl.when((self.mine < target) & (self.mine > 0))
            def _():
                self.up(target, self.own).wait_recv()
                self.add(target)
                self.up(target, self.came).start()

            @pl.when((self.mine > low) & (self.mine < self.groups - 1))
            def _():
                self.down(low, self.own).wait_recv()
                self.add(low)
                self.down(low, self.came).start()

        return [functools.partial(step, target) for target in range(self.groups - 1, 0, -1)]

    def finish(self):
        def store(index, value):
            self.total[index] = value

        def put(index, value):
            self.total[index] = self.total[index] + value

        add_slabs(self.blocks, store, lambda index: self.own[self.mine, index])
        for target in range(self.groups):

            @pl.when((self.mine == target) & (target > 0))
            def _(target=target):
                self.up(target, self.own).wait_recv()
                add_slabs(self.blocks, put, lambda index: self.came[target, index])

            @pl.when((self.mine == target) & (target < self.groups - 1))
            def _(target=target):
                self.down(target, self.own).wait_recv()
                add_slabs(self.blocks, put, lambda index: self.came[self.groups, index])

    def drain(self):
        for target in range(self.groups):

            @pl.when(self.mine < target)
            def _(target=target):
                self.up(target, self.own).wait_send()

            @pl.when(self.mine > target)
            def _(target=target):
                self.down(target, self.own).wait_send()


def swap_scratch(rows, width):
    return [VMEM((GROUP, rows, width), bf16), DMA, DMA((GROUP,)), DMA((GROUP,))]


SWAP = 4


class Swap:
    def __init__(self, place, base, got, scratch):
        self.place, self.base, self.got = place, base, got
        self.give, self.local, self.send, self.recv = scratch

    def copy(self, mask):
        target = flip(self.place, mask)
        return remote(
            self.give.at[target],
            self.got.at[self.place],
            self.send.at[mask],
            self.recv.at[mask],
            self.base + target,
        )

    def own(self):
        return pltpu.make_async_copy(
            self.give.at[self.place], self.got.at[self.place], self.local
        )

    def begin(self, total):
        def store(index, value):
            self.give[index] = value.astype(bf16)

        add_slabs(GROUP, store, lambda index: total[index])
        for mask in range(1, GROUP):
            self.copy(mask).start()
        self.own().start()

    def finish(self):
        self.own().wait()
        for mask in range(1, GROUP):
            self.copy(mask).wait()


class Mail:
    def __init__(self, me, count, given, got, local, send, recv):
        self.me, self.count, self.given, self.got = me, count, given, got
        self.local, self.send, self.recv = local, send, recv

    def copy(self, step):
        target = (self.me + step) % self.count
        return remote(
            self.given.at[target],
            self.got.at[self.me],
            self.send.at[step],
            self.recv.at[step],
            target,
        )

    def own(self):
        return pltpu.make_async_copy(self.given.at[self.me], self.got.at[self.me], self.local)

    def begin(self):
        self.own().start()

        def run(step, unused):
            self.copy(step).start()
            return unused

        lax.fori_loop(1, self.count, run, 0)

    def finish(self, total):
        self.own().wait()

        def run(step, unused):
            self.copy(step).wait()
            return unused

        lax.fori_loop(1, self.count, run, 0)

        def add(index, value):
            return value + self.got[index]

        total[...] = lax.fori_loop(
            0, self.count, add, jnp.zeros(self.got.shape[1:], f32)
        )


def masked_scores(length, query, key):
    scores = times_transposed(query, key) * (1.0 / math.sqrt(HD))
    tail = scores[:, SURE:]
    place = SURE + lax.broadcasted_iota(jnp.int32, tail.shape, 1)
    return jnp.concatenate(
        [scores[:, :SURE], jnp.where(place < length, tail, masked_value)], axis=1
    )


def norm_rows(value):
    average = jnp.mean(value, axis=-1, keepdims=True)
    centred = value - average
    inverse = lax.rsqrt(jnp.mean(centred * centred, axis=-1, keepdims=True) + epsilon)
    return centred * inverse


def forward_kernel(
    count,
    length_ref,
    qkv_ref,
    w_out_ref,
    x_ref,
    vec_ref,
    ct_ref,
    up_ref,
    down_ref,
    mixed_ref,
    log_ref,
    residual_ref,
    two_all,
    ct_all,
    up_all,
    down_all,
    two_rows,
    *rest,
):
    groups = count // GROUP
    me = lax.axis_index("fsdp")
    place = me % GROUP
    base = me - place
    mine = me // GROUP
    scatter, rest = Scatter(place, base, rest[:SCATTER]), rest[SCATTER:]
    two_sems, rest = rest[:7], rest[7:]
    ct_sems, rest = rest[:7], rest[7:]
    up_sems, rest = rest[:3], rest[3:]
    line_u, (down_local,) = rest[:8], rest[8:]
    length = length_ref[0]
    rows = x_ref.shape[0]
    greet_near(me, place, base, groups, range(1, GROUP))
    spread_start(me, place, base, up_ref, up_all, *up_sems)
    own_down = pltpu.make_async_copy(down_ref, down_all.at[mine], down_local)
    own_down.start()
    gather_start(place, base, ct_ref, ct_all, ct_sems)
    line = [up_all, down_all]

    def first():
        spread_wait(me, place, base, up_ref, up_all, *up_sems)
        own_down.wait()
        line_send(me, groups, line, line_u, 0)
        gather_relay(place, base, ct_ref, ct_all, ct_sems)

    tasks = [first]
    for step in range(groups - 1):

        def task(step=step):
            line_wait(me, groups, line, line_u, step)
            if step < groups - 2:
                line_send(me, groups, line, line_u, step + 1)

        tasks.append(task)

    def attend_rows(block):
        here = pl.ds(pl.multiple_of(block * rows, rows), rows)
        for head in range(HEADS_HERE):
            cols = pl.ds(head * LANES, LANES)
            scores = masked_scores(
                length, qkv_ref[here, cols], qkv_ref[:, pl.ds((HEADS_HERE + head) * LANES, LANES)]
            )
            largest = jnp.max(scores, axis=-1, keepdims=True)
            exponent = jnp.exp(scores - largest)
            total = jnp.sum(exponent, axis=-1, keepdims=True)
            weights = (exponent * (1.0 / total)).astype(bf16)
            value = qkv_ref[:, pl.ds((2 * HEADS_HERE + head) * LANES, LANES)]
            mixed_ref[here, cols] = matmul(weights, value).astype(bf16)
            log_ref[head, here, :] = largest + jnp.log(total)
        return matmul(mixed_ref[here, :], w_out_ref[...]).astype(bf16)

    for i in range(4):

        def pair(turn, unused, i=i):
            block = jnp.where(turn == 0, scatter.block(i, True), scatter.block(i, False))
            scatter.parts[i, turn] = attend_rows(block)

            @pl.when(turn == 0)
            def _():
                scatter.sibling(i).start()

            return unused

        lax.fori_loop(0, 2, pair, 0)
        scatter.after(i)
        if tasks:
            tasks.pop(0)()

    def normalize(span, value):
        total = x_ref[span, :].astype(f32) + (value + vec_ref[0:1, :])
        residual_ref[span, :] = total
        two_rows[span, :] = (norm_rows(total) * vec_ref[1:2, :] + vec_ref[2:3, :]).astype(bf16)

    scatter.finish(normalize)
    gather_start(place, base, two_rows, two_all, two_sems)
    gather_finish(place, base, ct_ref, ct_all, ct_sems)
    for task in tasks:
        task()
    gather_relay(place, base, two_rows, two_all, two_sems)
    scatter.drain()
    gather_finish(place, base, two_rows, two_all, two_sems)
    line_gather_drain(me, groups, line, line_u)


def forward(count, length, qkv, w_out, x, vec, ct, up, down, collective_id):
    groups = count // GROUP
    rows, width = x.shape
    clip = qkv.shape[0]
    return pl.pallas_call(
        functools.partial(forward_kernel, count),
        out_shape=[
            shaped(clip, HEADS_HERE * LANES),
            shaped(HEADS_HERE, clip, 1, kind=f32),
            shaped(rows, width, kind=f32),
            shaped(GROUP, rows, width),
            shaped(GROUP, rows, width),
            shaped(groups, *up.shape),
            shaped(groups, *down.shape),
        ],
        in_specs=[pl.BlockSpec(memory_space=pltpu.SMEM)] + [VSPEC] * 7,
        out_specs=[VSPEC] * 3 + [ANYSPEC] * 4,
        scratch_shapes=[VMEM((rows, width), bf16)]
        + scatter_scratch(rows, width)
        + gather_sems()
        + gather_sems()
        + [DMA, DMA((GROUP,)), DMA((GROUP,))]
        + line_sems(groups, 2)
        + [DMA],
        compiler_params=params(collective_id),
        name="forward",
    )(length, qkv, w_out, x, vec, ct, up, down)


def norm_back_rows(value, gain, grad):
    average = jnp.mean(value, axis=-1, keepdims=True)
    centred = value - average
    inverse = lax.rsqrt(jnp.mean(centred * centred, axis=-1, keepdims=True) + epsilon)
    xhat = centred * inverse
    scaled = grad * gain
    moved = inverse * (
        scaled
        - jnp.mean(scaled, axis=-1, keepdims=True)
        - xhat * jnp.mean(scaled * xhat, axis=-1, keepdims=True)
    )
    return moved, grad * xhat


def fold(value):
    total = value[0:8]
    for index in range(1, value.shape[0] // 8):
        total = total + value[index * 8 : index * 8 + 8]
    return total


def middle_kernel(
    count,
    length_ref,
    two_ref,
    part_ref,
    residual_ref,
    ct_ref,
    vec_ref,
    w_out_ref,
    qkv_ref,
    log_ref,
    mixed_ref,
    up_ref,
    down_ref,
    output_ref,
    grad_ref,
    grad_qkv_ref,
    grad_out_ref,
    sums_ref,
    up_got,
    down_total,
    branch_rows,
    branch_all,
    key_sum,
    value_sum,
    grad_two,
    folded,
    *rest,
):
    groups = count // GROUP
    me = lax.axis_index("fsdp")
    place = me % GROUP
    base = me - place
    two, rest = Scatter(place, base, rest[:SCATTER], two_ref), rest[SCATTER:]
    last, rest = Scatter(place, base, rest[:SCATTER], part_ref), rest[SCATTER:]
    sems, rest = rest[:7], rest[7:]
    up_line, rest = LineSum(me, groups, up_ref, rest[:LINE_SUM]), rest[LINE_SUM:]
    down_line, rest = LineSum(me, groups, down_ref, rest[:LINE_SUM]), rest[LINE_SUM:]
    up_swap = Swap(place, base, up_got, rest)
    length = length_ref[0]
    rows = ct_ref.shape[0]
    score_scale = 1.0 / math.sqrt(HD)
    greet_near(me, place, base, groups, range(1, GROUP))
    two.begin()
    up_line.begin()
    down_line.begin()
    last.begin()
    tasks = up_line.tasks() + down_line.tasks()
    for i in range(3):
        two.after(i)
    tasks.pop(0)()
    key_sum[...] = jnp.zeros_like(key_sum)
    value_sum[...] = jnp.zeros_like(value_sum)
    folded[...] = jnp.zeros_like(folded)

    def through_norm(span, value):
        moved, by_xhat = norm_back_rows(residual_ref[span, :], vec_ref[0:1, :], value)
        cotangent = ct_ref[span, :].astype(f32)
        total = cotangent + moved
        grad_ref[span, :] = total
        branch = total.astype(bf16)
        branch_rows[span, :] = branch
        for index, term in enumerate((by_xhat, value, branch.astype(f32), cotangent)):
            folded[index] = folded[index] + fold(term)

    two.finish(through_norm)
    gather_start(place, base, branch_rows, branch_all, sems)
    for index in range(4):
        sums_ref[index : index + 1, :] = jnp.sum(folded[index], axis=0, keepdims=True)
    sums_ref[4:8, :] = jnp.zeros((4, sums_ref.shape[1]), f32)

    def attend_back(block):
        here = pl.ds(pl.multiple_of(block * rows, rows), rows)
        grads = times_transposed(branch_all[block], w_out_ref[...]).astype(bf16)
        for head in range(HEADS_HERE):
            cols = pl.ds(head * LANES, LANES)
            query = qkv_ref[here, cols]
            key = qkv_ref[:, pl.ds((HEADS_HERE + head) * LANES, LANES)]
            value = qkv_ref[:, pl.ds((2 * HEADS_HERE + head) * LANES, LANES)]
            grad = grads[:, head * LANES : (head + 1) * LANES]
            weights = jnp.exp(masked_scores(length, query, key) - log_ref[head, here, :])
            grad_weights = times_transposed(grad, value)
            inner = jnp.sum(weights * grad_weights, axis=-1, keepdims=True)
            grad_scores = (weights * (grad_weights - inner)).astype(bf16)
            grad_qkv_ref[here, cols] = (matmul(grad_scores, key) * score_scale).astype(bf16)
            key_sum[:, cols] += outer_sum(grad_scores, query)
            value_sum[:, cols] += outer_sum(weights.astype(bf16), grad)

    def attend_pair(first, second):
        def run(turn, unused):
            attend_back(jnp.where(turn == 0, flip(place, first), flip(place, second)))
            return unused

        lax.fori_loop(0, 2, run, 0)

    args = (place, base, branch_rows, branch_all, sems)
    pltpu.make_async_copy(branch_rows, branch_all.at[place], sems[0]).wait()
    gather_own(*args).wait_recv()
    attend_pair(0, 1)
    gather_relay(*args)
    for slot in (2, 3):
        gather_piece(*args, slot).wait_recv()
        gather_pass(place, base, branch_all, sems, slot).start()
    tasks.pop(0)()
    attend_pair(2, 4)
    for slot in (4, 5):
        gather_piece(*args, slot).wait_recv()
        gather_pass(place, base, branch_all, sems, slot).start()
    for slot in range(4):
        gather_pass(place, base, branch_all, sems, slot).wait_recv()
    last.after(0)
    tasks.pop(0)()
    attend_pair(3, 5)
    last.after(1)
    if tasks:
        tasks.pop(0)()
    for slot in (4, 5):
        gather_pass(place, base, branch_all, sems, slot).wait_recv()
    attend_pair(6, 7)
    last.after(2)
    for task in tasks:
        task()
    up_line.finish()
    up_swap.begin(up_line.total)
    cols = pl.ds(HEADS_HERE * LANES, HEADS_HERE * LANES)
    grad_qkv_ref[:, cols] = (key_sum[...] * score_scale).astype(bf16)
    cols = pl.ds(2 * HEADS_HERE * LANES, HEADS_HERE * LANES)
    grad_qkv_ref[:, cols] = value_sum[...].astype(bf16)
    grad_out = jnp.zeros(grad_out_ref.shape, f32)
    for block in range(GROUP):
        grad_out = grad_out + outer_sum(
            mixed_ref[block * rows : (block + 1) * rows, :], branch_all[block]
        )
    grad_out_ref[...] = grad_out.astype(bf16)

    def residual_and(span, value):
        output_ref[span, :] = residual_ref[span, :] + (value + vec_ref[1:2, :])

    last.finish(residual_and)
    down_line.finish()
    add_slabs(
        down_total.shape[0],
        lambda index, value: down_total.__setitem__(index, value),
        lambda index: down_line.total[index],
    )
    up_swap.finish()
    gather_own(*args).wait_send()
    for slot in range(6):
        gather_piece(*args, slot).wait_send()
        gather_pass(place, base, branch_all, sems, slot).wait_send()
    two.drain()
    last.drain()
    up_line.drain()
    down_line.drain()


def middle(count, length, two, part, residual, ct, vec, w_out, qkv, log, mixed, up, down, cid):
    groups = count // GROUP
    rows, width = ct.shape
    clip = qkv.shape[0]
    wide = HEADS_HERE * LANES
    return pl.pallas_call(
        functools.partial(middle_kernel, count),
        out_shape=[
            shaped(rows, width, kind=f32),
            shaped(rows, width, kind=f32),
            shaped(clip, 3 * wide),
            shaped(wide, width),
            shaped(8, width, kind=f32),
            shaped(*up.shape[1:]),
            shaped(*down.shape[1:], kind=f32),
        ],
        in_specs=[pl.BlockSpec(memory_space=pltpu.SMEM)] + [ANYSPEC] * 2 + [VSPEC] * 9,
        out_specs=[VSPEC] * 7,
        scratch_shapes=[
            VMEM((rows, width), bf16),
            VMEM((GROUP, rows, width), bf16),
            VMEM((clip, wide), f32),
            VMEM((clip, wide), f32),
            VMEM((8, width), f32),
            VMEM((4, 8, width), f32),
        ]
        + scatter_scratch(rows, width, True)
        + scatter_scratch(rows, width, True)
        + gather_sems()
        + line_sum_scratch(groups, *up.shape[1:])
        + line_sum_scratch(groups, *down.shape[1:])
        + swap_scratch(*up.shape[2:]),
        compiler_params=params(cid),
        name="middle",
    )(length, two, part, residual, ct, vec, w_out, qkv, log, mixed, up, down)


def last_kernel(
    count,
    x_ref,
    normed_ref,
    grad_qkv_ref,
    w_qkv_ref,
    grad_ref,
    gain_ref,
    early_ref,
    out_ref,
    grad_inputs_ref,
    qkv_got,
    out_total,
    early_total,
    late_total,
    own_cols,
    cols,
    folded,
    late,
    early_got,
    late_got,
    out_got,
    *rest,
):
    groups = count // GROUP
    per = groups
    me = lax.axis_index("fsdp")
    place = me % GROUP
    base = me - place
    mine = me // GROUP
    rows, width = x_ref.shape
    few = own_cols.shape[2]
    one, rest = Scatter(place, base, rest[:SCATTER]), rest[SCATTER:]
    line, rest = LineSum(me, groups, own_cols, rest[:LINE_SUM]), rest[LINE_SUM:]
    swap, rest = Swap(place, base, qkv_got, rest[:SWAP]), rest[SWAP:]
    early_mail = Mail(me, count, early_ref, early_got, *rest[:3])
    late_mail = Mail(me, count, late, late_got, *rest[3:6])
    out_local, out_send, out_recv = rest[6:]
    greet_all(me, count)
    early_mail.begin()
    for index in range(per):
        owner = place * per + index

        @pl.when(owner != me)
        def _(index=index, owner=owner):
            remote(
                out_ref.at[index], out_got.at[mine], out_send.at[index], out_recv.at[mine], owner
            ).start()

        @pl.when(owner == me)
        def _(index=index):
            pltpu.make_async_copy(out_ref.at[index], out_got.at[mine], out_local).start()

    padded = 3 * HEADS_HERE * LANES
    packed = 3 * HEAD_COLS
    row = lax.broadcasted_iota(jnp.int32, (padded, packed), 0)
    col = lax.broadcasted_iota(jnp.int32, (padded, packed), 1)
    pick = jnp.where(
        (row // LANES == col // HD) & (row % LANES == col % HD), 1.0, 0.0
    ).astype(bf16)

    def weight_grad(index, unused):
        tile = pl.ds(pl.multiple_of(index * 256, 256), 256)
        grad = outer_sum(normed_ref[:, tile], grad_qkv_ref[...]).astype(bf16)
        cols[tile, :] = matmul(grad, pick)
        return unused

    lax.fori_loop(0, width // 256, weight_grad, 0)
    for owner in range(count):
        own_cols[owner // GROUP, owner % GROUP] = cols[owner * few : (owner + 1) * few, :].astype(
            bf16
        )
    line.begin()
    tasks = line.tasks()
    for i in range(4):

        def pair(turn, unused, i=i):
            block = jnp.where(turn == 0, one.block(i, True), one.block(i, False))
            here = pl.ds(pl.multiple_of(block * rows, rows), rows)
            one.parts[i, turn] = times_transposed(grad_qkv_ref[here, :], w_qkv_ref[...]).astype(
                bf16
            )

            @pl.when(turn == 0)
            def _():
                one.sibling(i).start()

            return unused

        lax.fori_loop(0, 2, pair, 0)
        one.after(i)
        if tasks and i > 0:
            tasks.pop(0)()
    for task in tasks:
        task()
    folded[...] = jnp.zeros_like(folded)

    def through_norm(span, value):
        moved, by_xhat = norm_back_rows(x_ref[span, :].astype(f32), gain_ref[0:1, :], value)
        grad_inputs_ref[span, :] = grad_ref[span, :] + moved
        folded[0] = folded[0] + fold(by_xhat)
        folded[1] = folded[1] + fold(value)

    one.finish(through_norm)
    line.finish()
    swap.begin(line.total)

    wide = HEADS_HERE * LANES

    def bias_sum(which):
        def add(index, value):
            span = pl.ds(pl.multiple_of(index * 64, 64), 64)
            return value + fold(grad_qkv_ref[span, which * wide : (which + 1) * wide].astype(f32))

        total = lax.fori_loop(
            0, grad_qkv_ref.shape[0] // 64, add, jnp.zeros((8, wide), f32)
        )
        row = lax.broadcasted_iota(jnp.int32, (wide, width), 0)
        col = lax.broadcasted_iota(jnp.int32, (wide, width), 1) - place * HEAD_COLS
        fits = (col >= 0) & (col < HEAD_COLS) & (row % LANES < HD)
        spot = jnp.where(fits & (row // LANES * HD + row % LANES == col), 1.0, 0.0)
        return jnp.sum(
            jnp.dot(total, spot, precision=lax.Precision.HIGHEST, preferred_element_type=f32),
            axis=0,
            keepdims=True,
        )

    vectors = jnp.concatenate(
        [
            jnp.sum(folded[0], axis=0, keepdims=True),
            jnp.sum(folded[1], axis=0, keepdims=True),
            bias_sum(0),
            bias_sum(2),
            jnp.zeros((4, width), f32),
        ],
        axis=0,
    )
    stretch = lax.broadcasted_iota(jnp.int32, (1, width), 1)
    row = lax.broadcasted_iota(jnp.int32, (width, LANES), 0)
    lane = lax.broadcasted_iota(jnp.int32, (width, LANES), 1)
    spot = jnp.where(row % few == lane, 1.0, 0.0)
    many = 8

    def owners(index, unused):
        terms = [
            jnp.where(stretch // few == index * many + k, vectors, 0.0) for k in range(many)
        ]
        slabs = jnp.dot(
            jnp.concatenate(terms, axis=0),
            spot,
            precision=lax.Precision.HIGHEST,
            preferred_element_type=f32,
        )
        for k in range(many):
            late[index * many + k] = slabs[k * 8 : k * 8 + 8]
        return unused

    lax.fori_loop(0, count // many, owners, 0)
    late_mail.begin()
    early_mail.finish(early_total)
    for index in range(per):
        owner = place * per + index

        @pl.when(owner != me)
        def _(index=index):
            remote(
                out_ref.at[index], out_got.at[mine], out_send.at[index], out_recv.at[mine], me
            ).wait_send()

        @pl.when(owner == me)
        def _(index=index):
            pltpu.make_async_copy(out_ref.at[index], out_got.at[mine], out_local).wait()

    for group in range(groups):

        @pl.when(group * GROUP + me // per != me)
        def _(group=group):
            remote(
                out_ref.at[0], out_got.at[group], out_send.at[0], out_recv.at[group], me
            ).wait_recv()

    total = out_got[0].astype(f32)
    for group in range(1, groups):
        total = total + out_got[group].astype(f32)
    out_total[...] = total
    swap.finish()
    late_mail.finish(late_total)
    one.drain()
    line.drain()


def last(count, x, normed, grad_qkv, w_qkv, grad, gain, early, out, collective_id):
    groups = count // GROUP
    rows, width = x.shape
    few = width // count
    packed = 3 * HEAD_COLS

    def mail(shape):
        return [DMA, DMA((count,)), DMA((count,))]

    return pl.pallas_call(
        functools.partial(last_kernel, count),
        out_shape=[
            shaped(rows, width, kind=f32),
            shaped(GROUP, few, packed),
            shaped(few, width, kind=f32),
            shaped(*early.shape[1:], kind=f32),
            shaped(8, LANES, kind=f32),
        ],
        in_specs=[VSPEC] * 8,
        out_specs=[VSPEC] * 5,
        scratch_shapes=[
            VMEM((groups, GROUP, few, packed), bf16),
            VMEM((width, packed), f32),
            VMEM((2, 8, width), f32),
            VMEM((count, 8, LANES), f32),
            VMEM(early.shape, f32),
            VMEM((count, 8, LANES), f32),
            VMEM((groups, few, width), bf16),
        ]
        + scatter_scratch(rows, width)
        + line_sum_scratch(groups, GROUP, few, packed)
        + swap_scratch(few, packed)
        + mail(early)
        + mail(early)
        + [DMA, DMA((groups,)), DMA((groups,))],
        compiler_params=params(collective_id),
        name="last",
    )(x, normed, grad_qkv, w_qkv, grad, gain, early, out)


def layer_norm(values, gain, offset):
    average = jnp.mean(values, axis=-1, keepdims=True)
    centred = values - average
    variance = jnp.mean(centred * centred, axis=-1, keepdims=True)
    return centred * lax.rsqrt(variance + epsilon) * gain + offset


def gelu_exact(values):
    return jax.nn.gelu(values, approximate=False)


def column_sums(matrix):
    return jnp.sum(matrix.astype(f32), axis=0)


def widen(cols, count):
    lead = cols.shape[:-1]
    split = cols.reshape(lead + (count, HD))
    return jnp.pad(split, [(0, 0)] * (len(lead) + 1) + [(0, LANES - HD)]).reshape(
        lead + (count * LANES,)
    )


def on_device(
    inputs,
    ln1_gain,
    ln1_bias,
    w_query,
    b_query,
    w_key,
    w_value,
    b_value,
    w_out,
    b_out,
    ln2_gain,
    ln2_bias,
    w_up,
    b_up,
    w_down,
    b_down,
    lengths,
    cotangent,
):
    count = lax.axis_size("fsdp")
    groups = count // GROUP
    me = lax.axis_index("fsdp")
    place = me % GROUP
    few = w_query.shape[0]
    many = w_down.shape[0]
    rows = inputs.shape[0]
    wide = 3 * HEAD_COLS
    ff_here = groups * many

    qkv_pack = (
        jnp.stack([w_query, w_key, w_value], axis=1)
        .astype(bf16)
        .reshape(few, 3, GROUP, HEAD_COLS)
        .transpose(2, 0, 1, 3)
        .reshape(GROUP, few, wide)
    )
    small = (ln1_gain, ln1_bias, b_query, b_value, b_out, ln2_gain, ln2_bias, b_down, b_up)
    small = jnp.concatenate(small).astype(bf16)
    small_pack = jnp.broadcast_to(
        jnp.pad(small, (0, wide - small.shape[0]))[None, None], (GROUP, 1, wide)
    )
    qkv_pack = jnp.concatenate([qkv_pack, small_pack], axis=1)
    up_pack = (
        w_up.astype(bf16)
        .reshape(few, groups, GROUP, many)
        .transpose(2, 0, 1, 3)
        .reshape(GROUP, few, ff_here)
    )
    x_all, qkv_all, out_all = fetch(count, inputs, qkv_pack, w_out.astype(bf16), 0)
    w_qkv = widen(qkv_all[:, :, :few].reshape(D, wide), 3 * HEADS_HERE)
    small_all = qkv_all[:, :, few].reshape(count, wide).astype(f32)
    whole = [small_all[:, i * few : (i + 1) * few].reshape(D) for i in range(8)]
    g1, o1, bq, bv, bo, g2, o2, bd = whole
    b_up_all = small_all[:, 8 * few : 8 * few + many].reshape(groups, GROUP, many)
    b_up_here = lax.dynamic_index_in_dim(b_up_all, place, 1, keepdims=False).reshape(ff_here)
    w_out_here = out_all.reshape(HEADS_HERE, HD, D)
    w_out_here = jnp.pad(w_out_here, ((0, 0), (0, LANES - HD), (0, 0))).reshape(
        HEADS_HERE * LANES, D
    )

    def head_slice(vector):
        return lax.dynamic_slice_in_dim(vector, place * HEAD_COLS, HEAD_COLS)

    b_qkv = jnp.concatenate([head_slice(bq), jnp.zeros((HEAD_COLS,), f32), head_slice(bv)])
    b_qkv = widen(b_qkv, 3 * HEADS_HERE)
    length = lax.dynamic_slice_in_dim(lengths, me // GROUP, 1)

    clip = x_all.reshape(GROUP * rows, D).astype(f32)
    normed = layer_norm(clip, g1, o1).astype(bf16)
    qkv = (matmul(normed, w_qkv) + b_qkv).astype(bf16)
    source = inputs.astype(f32)
    norm_vec = jnp.pad(jnp.stack([bo, g2, o2]), ((0, 5), (0, 0)))
    attended, log, residual, two_all, ct_all, up_all, down_all = forward(
        count,
        length,
        qkv,
        w_out_here,
        inputs,
        norm_vec,
        cotangent,
        up_pack,
        w_down.astype(bf16),
        1,
    )
    w_up_here = up_all.reshape(D, ff_here)
    w_down_here = down_all.reshape(ff_here, D)
    normed_two = two_all.reshape(GROUP * rows, D)
    ct = ct_all.reshape(GROUP * rows, D)
    hidden = matmul(normed_two, w_up_here) + b_up_here
    activated = gelu_exact(hidden).astype(bf16)
    out_part = matmul(activated, w_down_here).astype(bf16).reshape(GROUP, rows, D)

    grad_activated = times_transposed(ct, w_down_here)
    unused, gelu_pullback = jax.vjp(gelu_exact, hidden)
    grad_hidden = gelu_pullback(grad_activated)[0].astype(bf16)
    two_part = times_transposed(grad_hidden, w_up_here).astype(bf16).reshape(GROUP, rows, D)
    grad_w_up = outer_sum(normed_two, grad_hidden).astype(bf16)
    grad_w_down = outer_sum(activated, ct).astype(bf16)
    back_vec = jnp.pad(jnp.stack([g2, bd]), ((0, 6), (0, 0)))
    output, grad_residual, grad_qkv, grad_out, sums, up_got, down_total = middle(
        count,
        length,
        two_part,
        out_part,
        residual,
        cotangent,
        back_vec,
        w_out_here,
        qkv,
        log,
        attended,
        grad_w_up.reshape(groups, GROUP, few, ff_here),
        grad_w_down.reshape(groups, many // few, few, D),
        2,
    )
    grad_out = grad_out.reshape(HEADS_HERE, LANES, D)[:, :HD].reshape(groups, few, D)
    up_lanes = -(-many // LANES)
    grad_b_up = jnp.pad(
        column_sums(grad_hidden).reshape(groups, 1, many),
        ((0, 0), (0, 0), (0, up_lanes * LANES - many)),
    ).reshape(groups, 1, up_lanes, LANES)
    grad_b_up = jnp.where(
        (jnp.arange(GROUP) == place)[None, :, None, None], grad_b_up, 0.0
    ).reshape(count, up_lanes, LANES)
    early = jnp.pad(
        sums[:4].reshape(4, count, few).transpose(1, 0, 2), ((0, 0), (0, 0), (0, LANES - few))
    )
    early = jnp.concatenate(
        [early, grad_b_up, jnp.zeros((count, 4 - up_lanes, LANES), f32)], axis=1
    )
    grad_inputs, qkv_got, shard_w_out, early_sum, late_sum = last(
        count,
        inputs,
        normed,
        grad_qkv,
        w_qkv,
        grad_residual,
        jnp.pad(g1[None], ((0, 7), (0, 0))),
        early,
        grad_out,
        3,
    )

    def shard_of(which):
        piece = qkv_got[:, :, which * HEAD_COLS : (which + 1) * HEAD_COLS]
        return piece.transpose(1, 0, 2).reshape(few, D).astype(f32)

    shard_w_up = (
        up_got.reshape(GROUP, few, groups, many)
        .transpose(1, 2, 0, 3)
        .reshape(few, groups * GROUP * many)
        .astype(f32)
    )
    return (
        output,
        grad_inputs,
        late_sum[0, :few],
        late_sum[1, :few],
        shard_of(0),
        late_sum[2, :few],
        shard_of(1),
        shard_of(2),
        late_sum[3, :few],
        shard_w_out,
        early_sum[2, :few],
        early_sum[0, :few],
        early_sum[1, :few],
        shard_w_up,
        early_sum[4 : 4 + up_lanes].reshape(up_lanes * LANES)[:many],
        down_total.reshape(many, D),
        early_sum[3, :few],
    )


def solution(mesh):
    in_specs = (
        P("fsdp", None),
        P("fsdp"),
        P("fsdp"),
        P("fsdp", None),
        P("fsdp"),
        P("fsdp", None),
        P("fsdp", None),
        P("fsdp"),
        P("fsdp", None),
        P("fsdp"),
        P("fsdp"),
        P("fsdp"),
        P("fsdp", None),
        P("fsdp"),
        P("fsdp", None),
        P("fsdp"),
        P(),
        P("fsdp", None),
    )
    out_specs = (
        P("fsdp", None),
        P("fsdp", None),
        P("fsdp"),
        P("fsdp"),
        P("fsdp", None),
        P("fsdp"),
        P("fsdp", None),
        P("fsdp", None),
        P("fsdp"),
        P("fsdp", None),
        P("fsdp"),
        P("fsdp"),
        P("fsdp"),
        P("fsdp", None),
        P("fsdp"),
        P("fsdp", None),
        P("fsdp"),
    )
    return jax.shard_map(
        on_device, mesh=mesh, in_specs=in_specs, out_specs=out_specs, check_vma=False
    )
```

```python
import functools
import math

import jax
import jax.numpy as jnp
from jax import lax
from jax.experimental import pallas as pl
from jax.experimental.pallas import tpu as pltpu
from jax.sharding import PartitionSpec as P

D = 1280
H = 16
HD = 80
CLIP_LEN = 1536
GROUP = 8
LANES = 128
HEADS_HERE = H // GROUP
HEAD_COLS = HEADS_HERE * HD
SURE = CLIP_LEN * 3 // 4

epsilon = 1e-05
masked_value = -1e30
MESH = pl.DeviceIdType.MESH
VMEM = pltpu.VMEM
DMA = pltpu.SemaphoreType.DMA
bf16 = jnp.bfloat16
f32 = jnp.float32


def matmul(left, right):
    return jnp.dot(left, right, preferred_element_type=f32)


def outer_sum(left, right):
    return lax.dot_general(left, right, (((0,), (0,)), ((), ())), preferred_element_type=f32)


def times_transposed(left, right):
    return lax.dot_general(left, right, (((1,), (1,)), ((), ())), preferred_element_type=f32)


def flip(place, mask):
    for bit in (1, 2, 4):
        if mask & bit:
            place = place + bit - 2 * bit * (place // bit % 2)
    return place


def remote(src, dst, send_sem, recv_sem, target):
    return pltpu.make_async_remote_copy(
        src_ref=src,
        dst_ref=dst,
        send_sem=send_sem,
        recv_sem=recv_sem,
        device_id=(target,),
        device_id_type=MESH,
    )


def greet(targets):
    barrier = pltpu.get_barrier_semaphore()
    for target in targets:
        pl.semaphore_signal(barrier, inc=1, device_id=(target,), device_id_type=MESH)
    pl.semaphore_wait(barrier, len(targets))


def greet_all(me, count):
    barrier = pltpu.get_barrier_semaphore()

    def signal(step, unused):
        pl.semaphore_signal(
            barrier, inc=1, device_id=((me + step) % count,), device_id_type=MESH
        )
        return unused

    lax.fori_loop(1, count, signal, 0)
    pl.semaphore_wait(barrier, count - 1)


def params(collective_id):
    return pltpu.CompilerParams(collective_id=collective_id, has_side_effects=True)


ANYSPEC = pl.BlockSpec(memory_space=pl.ANY)
VSPEC = pl.BlockSpec(memory_space=pltpu.VMEM)


FAR = (2, 4, 6)
PIECES = ((0, 2), (1, 4), (1, 2), (0, 4), (0, 6), (1, 6))


def half_of(ref, owner, half):
    rows = ref.shape[1] // 2
    return ref.at[owner, pl.ds(half * rows, rows)]


def gather_sems():
    return [DMA, DMA, DMA, DMA((6,)), DMA((6,)), DMA((6,)), DMA((6,))]


def gather_piece(place, base, block, out, sems, slot):
    send, recv = sems[3:5]
    half, mask = PIECES[slot]
    rows = block.shape[0] // 2
    if slot < 4:
        src = block.at[pl.ds(half * rows, rows)]
        dst = half_of(out, place, half)
        target = flip(place, mask)
    else:
        near, far = (2, 4) if half == 0 else (4, 2)
        src = half_of(out, flip(place, near), half)
        dst = src
        target = flip(place, far)
    return remote(src, dst, send.at[slot], recv.at[slot], base + target)


def gather_pass(place, base, out, sems, slot):
    pass_send, pass_recv = sems[5:7]
    half, mask = PIECES[slot]
    piece = half_of(out, flip(place, mask), half)
    return remote(piece, piece, pass_send.at[slot], pass_recv.at[slot], base + flip(place, 1))


def gather_own(place, base, block, out, sems):
    return remote(block, out.at[place], sems[1], sems[2], base + flip(place, 1))


def gather_start(place, base, block, out, sems):
    for slot in (0, 1, 2, 3):
        gather_piece(place, base, block, out, sems, slot).start()
    pltpu.make_async_copy(block, out.at[place], sems[0]).start()
    gather_own(place, base, block, out, sems).start()


def gather_relay(place, base, block, out, sems):
    for slot, relay in ((0, 4), (1, 5)):
        gather_piece(place, base, block, out, sems, slot).wait_recv()
        gather_piece(place, base, block, out, sems, relay).start()
        gather_pass(place, base, out, sems, slot).start()


def gather_finish(place, base, block, out, sems):
    for slot in (2, 3, 4, 5):
        gather_piece(place, base, block, out, sems, slot).wait_recv()
        gather_pass(place, base, out, sems, slot).start()
    pltpu.make_async_copy(block, out.at[place], sems[0]).wait()
    gather_own(place, base, block, out, sems).wait()
    for slot in range(6):
        gather_piece(place, base, block, out, sems, slot).wait_send()
        gather_pass(place, base, out, sems, slot).wait()


ORDER = (6, 2, 4, 0)


def row_loop(rows, step, body):
    def run(index, unused):
        body(pl.ds(pl.multiple_of(index * step, step), step))
        return unused

    lax.fori_loop(0, rows // step, run, 0)


def scatter_scratch(rows, width, ready=False):
    half = rows // 2
    return [
        VMEM((4, rows, width) if ready else (4, 2, rows, width), bf16),
        VMEM((4, rows, width), bf16),
        VMEM((2, half, width), bf16),
        VMEM((2, rows, width), bf16),
        DMA((4,)),
        DMA((4,)),
        DMA((4,)),
        DMA((6,)),
        DMA((6,)),
    ]


SCATTER = 9


class Scatter:
    def __init__(self, place, base, scratch, ready=None):
        self.place, self.base, self.ready = place, base, ready
        self.parts, self.sib, self.relay, self.got = scratch[:4]
        self.local, self.sib_send, self.sib_recv, self.send, self.recv = scratch[4:]
        self.rows = self.got.shape[1]
        self.half = self.rows // 2

    def block(self, i, other):
        return flip(flip(self.place, ORDER[i]), 1 if other else 0)

    def keep(self, i):
        return self.parts.at[i, 1] if self.ready is None else self.parts.at[i]

    def sibling(self, i):
        if self.ready is None:
            src = self.parts.at[i, 0]
        else:
            src = self.ready.at[self.block(i, True)]
        return remote(
            src,
            self.sib.at[i],
            self.sib_send.at[i],
            self.sib_recv.at[i],
            self.base + flip(self.place, 1),
        )

    def load(self, i):
        return pltpu.make_async_copy(
            self.ready.at[self.block(i, False)], self.keep(i), self.local.at[i]
        )

    def begin(self):
        for i in range(4):
            self.sibling(i).start()
            self.load(i).start()

    def link(self, slot):
        half = slot % 2
        span = pl.ds(half * self.half, self.half)
        if slot < 2:
            i, mask, dst = 0, (2, 4)[half], self.relay.at[half]
        else:
            i = slot // 2
            mask, dst = ORDER[i], self.got.at[i - 1, span]
        return remote(
            self.keep(i).at[span],
            dst,
            self.send.at[slot],
            self.recv.at[slot],
            self.base + flip(self.place, mask),
        )

    def merge(self, i):
        if self.ready is not None:
            self.load(i).wait()
        self.sibling(i).wait_recv()
        keep = self.keep(i)

        def body(span):
            keep[span, :] = (
                keep[span, :].astype(f32) + self.sib[i, span, :].astype(f32)
            ).astype(bf16)

        row_loop(self.rows, 32, body)

    def merge_relay(self, i, half):
        self.link(half).wait_recv()
        start = half * self.half
        keep = self.keep(i)

        def run(index, unused):
            here = pl.multiple_of(index * 32, 32)
            span = pl.ds(start + here, 32)
            keep[span, :] = (
                keep[span, :].astype(f32) + self.relay[half, pl.ds(here, 32), :].astype(f32)
            ).astype(bf16)
            return unused

        lax.fori_loop(0, self.half // 32, run, 0)

    def after(self, i):
        if i < 3:
            self.merge(i)
        if i == 0:
            self.link(0).start()
            self.link(1).start()
        if i == 1:
            self.link(2).start()
        if i == 2:
            self.link(5).start()
            self.merge_relay(1, 1)
            self.link(3).start()
            self.merge_relay(2, 0)
            self.link(4).start()

    def finish(self, use):
        if self.ready is not None:
            self.load(3).wait()
        self.sibling(3).wait_recv()
        for slot in range(2, 6):
            self.link(slot).wait_recv()
        keep = self.keep(3)

        def body(span):
            value = keep[span, :].astype(f32) + self.sib[3, span, :].astype(f32)
            value = value + self.got[0, span, :].astype(f32)
            use(span, value + self.got[1, span, :].astype(f32))

        row_loop(self.rows, 32, body)

    def drain(self):
        for i in range(4):
            self.sibling(i).wait_send()
        for slot in range(6):
            self.link(slot).wait_send()


def line_send(me, groups, outs, sems, step):
    mine = me // GROUP
    for which, out in enumerate(outs):
        up_send, up_recv, down_send, down_recv = sems[4 * which : 4 * which + 4]

        @pl.when((mine - step >= 0) & (mine + 1 < groups))
        def _(out=out, up_send=up_send, up_recv=up_recv):
            slab = out.at[mine - step]
            remote(slab, slab, up_send.at[step], up_recv.at[step], me + GROUP).start()

        @pl.when((mine + step < groups) & (mine >= 1))
        def _(out=out, down_send=down_send, down_recv=down_recv):
            slab = out.at[mine + step]
            remote(slab, slab, down_send.at[step], down_recv.at[step], me - GROUP).start()


def line_wait(me, groups, outs, sems, step):
    mine = me // GROUP
    for which, out in enumerate(outs):
        up_send, up_recv, down_send, down_recv = sems[4 * which : 4 * which + 4]

        @pl.when(mine - 1 - step >= 0)
        def _(out=out, up_send=up_send, up_recv=up_recv):
            slab = out.at[mine - 1 - step]
            remote(slab, slab, up_send.at[step], up_recv.at[step], me).wait_recv()

        @pl.when(mine + 1 + step < groups)
        def _(out=out, down_send=down_send, down_recv=down_recv):
            slab = out.at[mine + 1 + step]
            remote(slab, slab, down_send.at[step], down_recv.at[step], me).wait_recv()


def line_gather(me, groups, outs, sems):
    for step in range(groups - 1):
        line_send(me, groups, outs, sems, step)
        line_wait(me, groups, outs, sems, step)


def line_gather_drain(me, groups, outs, sems):
    mine = me // GROUP
    for step in range(groups - 1):
        for which, out in enumerate(outs):
            up_send, up_recv, down_send, down_recv = sems[4 * which : 4 * which + 4]

            @pl.when((mine - step >= 0) & (mine + 1 < groups))
            def _(out=out, up_send=up_send, up_recv=up_recv):
                slab = out.at[0]
                remote(slab, slab, up_send.at[step], up_recv.at[step], me).wait_send()

            @pl.when((mine + step < groups) & (mine >= 1))
            def _(out=out, down_send=down_send, down_recv=down_recv):
                slab = out.at[0]
                remote(slab, slab, down_send.at[step], down_recv.at[step], me).wait_send()


def line_sems(groups, arrays):
    return [DMA((groups,))] * (4 * arrays)


class Spread:
    def __init__(self, place, base, pack, out, scratch, one=False):
        self.place, self.base, self.pack, self.out, self.one = place, base, pack, out, one
        self.local, self.send, self.recv = scratch

    def slab(self, target):
        return self.pack if self.one else self.pack.at[target]

    def copy(self, mask):
        target = flip(self.place, mask)
        return remote(
            self.slab(target),
            self.out.at[self.place],
            self.send.at[mask],
            self.recv.at[mask],
            self.base + target,
        )

    def own(self):
        return pltpu.make_async_copy(
            self.slab(self.place), self.out.at[self.place], self.local
        )

    def begin(self):
        for mask in (6, 2, 4, 7, 3, 5, 1):
            self.copy(mask).start()
        self.own().start()

    def finish(self):
        self.own().wait()
        for mask in range(1, GROUP):
            self.copy(mask).wait()


SPREAD = 3


def spread_sems():
    return [DMA, DMA((GROUP,)), DMA((GROUP,))]


def greet_near(me, place, base, groups, masks):
    barrier = pltpu.get_barrier_semaphore()
    mine = me // GROUP
    for mask in masks:
        pl.semaphore_signal(
            barrier, inc=1, device_id=(base + flip(place, mask),), device_id_type=MESH
        )

    @pl.when(mine > 0)
    def _():
        pl.semaphore_signal(barrier, inc=1, device_id=(me - GROUP,), device_id_type=MESH)

    @pl.when(mine < groups - 1)
    def _():
        pl.semaphore_signal(barrier, inc=1, device_id=(me + GROUP,), device_id_type=MESH)

    both = jnp.where(mine > 0, 1, 0) + jnp.where(mine < groups - 1, 1, 0)
    pl.semaphore_wait(barrier, len(masks) + both)


def shaped(*shape, kind=bf16):
    return jax.ShapeDtypeStruct(shape, kind)


def add_slabs(blocks, store, *terms):
    def body(index, unused):
        value = terms[0](index).astype(f32)
        for term in terms[1:]:
            value = value + term(index).astype(f32)
        store(index, value)
        return unused

    lax.fori_loop(0, blocks, body, 0)


def line_sum_scratch(groups, slabs, rows, width):
    return [
        VMEM((groups + 1, slabs, rows, width), bf16),
        VMEM((slabs, rows, width), f32),
    ] + line_sems(groups, 1)


LINE_SUM = 6


class LineSum:
    def __init__(self, me, groups, own, scratch):
        self.me, self.groups, self.own = me, groups, own
        self.came, self.total = scratch[:2]
        self.up_send, self.up_recv, self.down_send, self.down_recv = scratch[2:]
        self.mine = me // GROUP
        self.blocks = own.shape[1]

    def up(self, target, src):
        return remote(
            src.at[target],
            self.came.at[target],
            self.up_send.at[target],
            self.up_recv.at[target],
            self.me + GROUP,
        )

    def down(self, target, src):
        last = jnp.where(self.mine - 1 == target, self.groups, target)
        return remote(
            src.at[target],
            self.came.at[last],
            self.down_send.at[target],
            self.down_recv.at[target],
            self.me - GROUP,
        )

    def add(self, target):
        def store(index, value):
            self.came[target, index] = value.astype(bf16)

        add_slabs(
            self.blocks,
            store,
            lambda index: self.own[target, index],
            lambda index: self.came[target, index],
        )

    def begin(self):
        for target in range(self.groups - 1, 0, -1):
            low = self.groups - 1 - target

            @pl.when((self.mine == 0))
            def _(target=target):
                self.up(target, self.own).start()

            @pl.when(self.mine == self.groups - 1)
            def _(low=low):
                self.down(low, self.own).start()

    def tasks(self):
        def step(target):
            low = self.groups - 1 - target

            @pl.when((self.mine < target) & (self.mine > 0))
            def _():
                self.up(target, self.own).wait_recv()
                self.add(target)
                self.up(target, self.came).start()

            @pl.when((self.mine > low) & (self.mine < self.groups - 1))
            def _():
                self.down(low, self.own).wait_recv()
                self.add(low)
                self.down(low, self.came).start()

        return [functools.partial(step, target) for target in range(self.groups - 1, 0, -1)]

    def finish(self):
        def store(index, value):
            self.total[index] = value

        def put(index, value):
            self.total[index] = self.total[index] + value

        add_slabs(self.blocks, store, lambda index: self.own[self.mine, index])
        for target in range(self.groups):

            @pl.when((self.mine == target) & (target > 0))
            def _(target=target):
                self.up(target, self.own).wait_recv()
                add_slabs(self.blocks, put, lambda index: self.came[target, index])

            @pl.when((self.mine == target) & (target < self.groups - 1))
            def _(target=target):
                self.down(target, self.own).wait_recv()
                add_slabs(self.blocks, put, lambda index: self.came[self.groups, index])

    def drain(self):
        for target in range(self.groups):

            @pl.when(self.mine < target)
            def _(target=target):
                self.up(target, self.own).wait_send()

            @pl.when(self.mine > target)
            def _(target=target):
                self.down(target, self.own).wait_send()


def swap_scratch(rows, width):
    return [VMEM((GROUP, rows, width), bf16), DMA, DMA((GROUP,)), DMA((GROUP,))]


SWAP = 4


class Swap:
    def __init__(self, place, base, got, scratch):
        self.place, self.base, self.got = place, base, got
        self.give, self.local, self.send, self.recv = scratch

    def copy(self, mask):
        target = flip(self.place, mask)
        return remote(
            self.give.at[target],
            self.got.at[self.place],
            self.send.at[mask],
            self.recv.at[mask],
            self.base + target,
        )

    def own(self):
        return pltpu.make_async_copy(
            self.give.at[self.place], self.got.at[self.place], self.local
        )

    def begin(self, total):
        def store(index, value):
            self.give[index] = value.astype(bf16)

        add_slabs(GROUP, store, lambda index: total[index])
        for mask in range(1, GROUP):
            self.copy(mask).start()
        self.own().start()

    def finish(self):
        self.own().wait()
        for mask in range(1, GROUP):
            self.copy(mask).wait()


class Mail:
    def __init__(self, me, count, given, got, local, send, recv):
        self.me, self.count, self.given, self.got = me, count, given, got
        self.local, self.send, self.recv = local, send, recv

    def copy(self, step):
        target = (self.me + step) % self.count
        return remote(
            self.given.at[target],
            self.got.at[self.me],
            self.send.at[step],
            self.recv.at[step],
            target,
        )

    def own(self):
        return pltpu.make_async_copy(self.given.at[self.me], self.got.at[self.me], self.local)

    def begin(self):
        self.own().start()

        def run(step, unused):
            self.copy(step).start()
            return unused

        lax.fori_loop(1, self.count, run, 0)

    def finish(self, total):
        self.own().wait()

        def run(step, unused):
            self.copy(step).wait()
            return unused

        lax.fori_loop(1, self.count, run, 0)

        def add(index, value):
            return value + self.got[index]

        total[...] = lax.fori_loop(
            0, self.count, add, jnp.zeros(self.got.shape[1:], f32)
        )


def masked_scores(length, query, key):
    scores = times_transposed(query, key) * (1.0 / math.sqrt(HD))
    tail = scores[:, SURE:]
    place = SURE + lax.broadcasted_iota(jnp.int32, tail.shape, 1)
    return jnp.concatenate(
        [scores[:, :SURE], jnp.where(place < length, tail, masked_value)], axis=1
    )


def norm_rows(value):
    average = jnp.mean(value, axis=-1, keepdims=True)
    centred = value - average
    inverse = lax.rsqrt(jnp.mean(centred * centred, axis=-1, keepdims=True) + epsilon)
    return centred * inverse


def head_pick(rows, cols):
    row = lax.broadcasted_iota(jnp.int32, (rows, cols), 0)
    col = lax.broadcasted_iota(jnp.int32, (rows, cols), 1)
    return jnp.where((col // LANES == row // HD) & (col % LANES == row % HD), 1.0, 0.0).astype(bf16)


def front_kernel(
    count,
    length_ref,
    x_ref,
    ct_ref,
    wq_ref,
    wk_ref,
    wv_ref,
    wo_ref,
    wu_ref,
    wd_ref,
    small_ref,
    normed_out,
    w_qkv_out,
    qkv_out,
    w_out_ref,
    mixed_ref,
    log_ref,
    residual_ref,
    vec_ref,
    small_all,
    two_all,
    ct_all,
    up_all,
    down_all,
    x_all,
    normed_ref,
    w_qkv_ref,
    qkv_ref,
    two_rows,
    pack_qkv,
    pack_up,
    down_ref,
    out_ref,
    qkv_slabs,
    out_slabs,
    wide_w,
    wide_out,
    *rest,
):
    groups = count // GROUP
    per = groups
    me = lax.axis_index("fsdp")
    place = me % GROUP
    base = me - place
    mine = me // GROUP
    rows, width = x_ref.shape
    few = wq_ref.shape[0]
    many = wd_ref.shape[0]
    packed = 3 * HEAD_COLS
    wide = HEADS_HERE * LANES
    scatter, rest = Scatter(place, base, rest[:SCATTER]), rest[SCATTER:]
    x_sems, rest = rest[:7], rest[7:]
    two_sems, rest = rest[:7], rest[7:]
    ct_sems, rest = rest[:7], rest[7:]
    qkv_spread, rest = (
        Spread(place, base, pack_qkv, qkv_slabs.at[mine], rest[:SPREAD]),
        rest[SPREAD:],
    )
    small_spread, rest = (
        Spread(place, base, small_ref, small_all.at[mine], rest[:SPREAD], True),
        rest[SPREAD:],
    )
    up_spread, rest = (
        Spread(place, base, pack_up, up_all.at[mine], rest[:SPREAD]),
        rest[SPREAD:],
    )
    line_q, rest = rest[:8], rest[8:]
    line_u, rest = rest[:8], rest[8:]
    down_local, out_local, out_send, out_recv, keep_normed, keep_w, keep_qkv = rest
    length = length_ref[me // GROUP]

    for other in range(GROUP):
        cols = slice(other * HEAD_COLS, (other + 1) * HEAD_COLS)
        for index, ref in enumerate((wq_ref, wk_ref, wv_ref)):
            pack_qkv[other, :, index * HEAD_COLS : (index + 1) * HEAD_COLS] = ref[:, cols].astype(
                bf16
            )
    greet_all(me, count)
    qkv_spread.begin()
    small_spread.begin()
    x_args = (place, base, x_ref, x_all, x_sems)
    ct_args = (place, base, ct_ref, ct_all, ct_sems)
    two_args = (place, base, two_rows, two_all, two_sems)
    gather_start(*x_args)
    for other in range(GROUP):
        for group in range(groups):
            start = (group * GROUP + other) * many
            pack_up[other, :, group * many : (group + 1) * many] = wu_ref[
                :, start : start + many
            ].astype(bf16)
    down_ref[...] = wd_ref[...].astype(bf16)
    out_ref[...] = wo_ref[...].astype(bf16)
    own_down = pltpu.make_async_copy(down_ref, down_all.at[mine], down_local)
    own_down.start()
    qkv_spread.finish()
    small_spread.finish()
    first_line = [qkv_slabs, small_all]
    line_send(me, groups, first_line, line_q, 0)
    up_spread.begin()
    gather_relay(*x_args)
    line_wait(me, groups, first_line, line_q, 0)
    line_send(me, groups, first_line, line_q, 1)
    gather_finish(*x_args)
    gather_start(*ct_args)
    for step in range(1, groups - 1):
        if step > 1:
            line_send(me, groups, first_line, line_q, step)
        line_wait(me, groups, first_line, line_q, step)

    wanted = me // per
    slot = me % per
    for group in range(groups):
        target = group * GROUP + wanted

        @pl.when(target != me)
        def _(target=target, group=group):
            remote(
                out_ref, out_slabs.at[slot], out_send.at[group], out_recv.at[slot], target
            ).start()

        @pl.when(target == me)
        def _(target=target, group=group):
            pltpu.make_async_copy(out_ref, out_slabs.at[slot], out_local).start()

    up_spread.finish()
    own_down.wait()
    line = [up_all, down_all]
    line_send(me, groups, line, line_u, 0)
    gather_relay(*ct_args)

    def ct_end():
        gather_finish(*ct_args)

    tasks = [ct_end]
    for step in range(groups - 1):

        def task(step=step):
            line_wait(me, groups, line, line_u, step)
            if step < groups - 2:
                line_send(me, groups, line, line_u, step + 1)

        tasks.append(task)

    row = lax.broadcasted_iota(jnp.int32, (LANES, width), 0)
    lane = lax.broadcasted_iota(jnp.int32, (LANES, width), 1)
    tile = jnp.where((lane % few == row) & (row < few), 1.0, 0.0).astype(bf16)
    owner = lax.broadcasted_iota(jnp.int32, (1, width), 1) // few

    def lay(group, value):
        for other in range(GROUP):
            spot = matmul(small_all[group, other], tile)
            value = value + jnp.where(owner == group * GROUP + other, spot, 0.0)
        return value

    vectors = lax.fori_loop(0, groups, lay, jnp.zeros((small_ref.shape[0], width), f32))
    vec_ref[...] = vectors[:8]
    gain, offset = vec_ref[0:1, :], vec_ref[1:2, :]

    def first_norm(index, unused):
        for part in range(rows // 32):
            span = pl.ds(part * 32, 32)
            value = x_all[index, span, :].astype(f32)
            normed_ref[
                pl.ds(pl.multiple_of(index * rows, rows) + part * 32, 32), :
            ] = (norm_rows(value) * gain + offset).astype(bf16)
        return unused

    lax.fori_loop(0, GROUP, first_norm, 0)
    keep = pltpu.make_async_copy(normed_ref, normed_out, keep_normed)
    keep.start()

    for source in range(count):
        wide_w[source * few : (source + 1) * few, :] = qkv_slabs[
            source // GROUP, source % GROUP
        ].astype(f32)
    pick = head_pick(packed, 3 * wide)

    def widen_rows(span):
        w_qkv_ref[span, :] = matmul(wide_w[span, :].astype(bf16), pick).astype(bf16)

    row_loop(width, 256, widen_rows)
    keep_two = pltpu.make_async_copy(w_qkv_ref, w_qkv_out, keep_w)
    keep_two.start()
    row = lax.broadcasted_iota(jnp.int32, (width, wide), 0) - place * HEAD_COLS
    col = lax.broadcasted_iota(jnp.int32, (width, wide), 1)
    spot = jnp.where(
        (col % LANES < HD) & (row == col // LANES * HD + col % LANES), 1.0, 0.0
    ).astype(bf16)
    biases = matmul(vectors.astype(bf16), spot)
    bias = jnp.concatenate(
        [biases[2:3], jnp.zeros((1, wide), f32), biases[3:4]], axis=1
    )

    def project(index, unused):
        span = pl.ds(pl.multiple_of(index * rows, rows), rows)
        qkv_ref[span, :] = (matmul(normed_ref[span, :], w_qkv_ref[...]) + bias).astype(bf16)
        return unused

    lax.fori_loop(0, GROUP, project, 0)
    keep_three = pltpu.make_async_copy(qkv_ref, qkv_out, keep_qkv)
    keep_three.start()

    for group in range(groups):
        target = group * GROUP + wanted

        @pl.when(target != me)
        def _(group=group):
            remote(
                out_ref, out_slabs.at[slot], out_send.at[group], out_recv.at[slot], me
            ).wait_send()

        @pl.when(target == me)
        def _():
            pltpu.make_async_copy(out_ref, out_slabs.at[slot], out_local).wait()

    for index in range(per):
        sender = place * per + index

        @pl.when(sender != me)
        def _(index=index):
            remote(
                out_ref, out_slabs.at[index], out_send.at[0], out_recv.at[index], me
            ).wait_recv()

    wide_out[...] = jnp.zeros_like(wide_out)
    for index in range(per):
        start = index * few
        start = start // HD * LANES + start % HD
        wide_out[start : start + few, :] = out_slabs[index].astype(f32)
    w_out_ref[...] = wide_out[...].astype(bf16)

    def attend_rows(block):
        here = pl.ds(pl.multiple_of(block * rows, rows), rows)
        for head in range(HEADS_HERE):
            cols = pl.ds(head * LANES, LANES)
            scores = masked_scores(
                length, qkv_ref[here, cols], qkv_ref[:, pl.ds((HEADS_HERE + head) * LANES, LANES)]
            )
            largest = jnp.max(scores, axis=-1, keepdims=True)
            exponent = jnp.exp(scores - largest)
            total = jnp.sum(exponent, axis=-1, keepdims=True)
            weights = (exponent * (1.0 / total)).astype(bf16)
            value = qkv_ref[:, pl.ds((2 * HEADS_HERE + head) * LANES, LANES)]
            mixed_ref[here, cols] = matmul(weights, value).astype(bf16)
            log_ref[head, here, :] = largest + jnp.log(total)
        return matmul(mixed_ref[here, :], w_out_ref[...]).astype(bf16)

    for i in range(4):

        def pair(turn, unused, i=i):
            block = jnp.where(turn == 0, scatter.block(i, True), scatter.block(i, False))
            scatter.parts[i, turn] = attend_rows(block)

            @pl.when(turn == 0)
            def _():
                scatter.sibling(i).start()

            return unused

        lax.fori_loop(0, 2, pair, 0)
        scatter.after(i)
        if tasks:
            tasks.pop(0)()

    def normalize(span, value):
        total = x_ref[span, :].astype(f32) + (value + vec_ref[4:5, :])
        residual_ref[span, :] = total
        two_rows[span, :] = (norm_rows(total) * vec_ref[5:6, :] + vec_ref[6:7, :]).astype(bf16)

    scatter.finish(normalize)
    gather_start(*two_args)
    for task in tasks:
        task()
    gather_relay(*two_args)
    scatter.drain()
    line_gather_drain(me, groups, first_line, line_q)
    line_gather_drain(me, groups, line, line_u)
    gather_finish(*two_args)
    keep.wait()
    keep_two.wait()
    keep_three.wait()


def front(count, lengths, x, ct, wq, wk, wv, wo, wu, wd, small, collective_id):
    groups = count // GROUP
    rows, width = x.shape
    clip = GROUP * rows
    few = wq.shape[0]
    many = wd.shape[0]
    packed = 3 * HEAD_COLS
    wide = HEADS_HERE * LANES
    return pl.pallas_call(
        functools.partial(front_kernel, count),
        out_shape=[
            shaped(clip, width),
            shaped(width, 3 * wide),
            shaped(clip, 3 * wide),
            shaped(wide, width),
            shaped(clip, wide),
            shaped(HEADS_HERE, clip, 1, kind=f32),
            shaped(rows, width, kind=f32),
            shaped(8, width, kind=f32),
            shaped(groups, GROUP, *small.shape),
            shaped(GROUP, rows, width),
            shaped(GROUP, rows, width),
            shaped(groups, GROUP, few, groups * many),
            shaped(groups, many, width),
        ],
        in_specs=[pl.BlockSpec(memory_space=pltpu.SMEM)] + [VSPEC] * 9,
        out_specs=[ANYSPEC] * 3 + [VSPEC] * 6 + [ANYSPEC] * 4,
        scratch_shapes=[
            VMEM((GROUP, rows, width), bf16),
            VMEM((clip, width), bf16),
            VMEM((width, 3 * wide), bf16),
            VMEM((clip, 3 * wide), bf16),
            VMEM((rows, width), bf16),
            VMEM((GROUP, few, packed), bf16),
            VMEM((GROUP, few, groups * many), bf16),
            VMEM((many, width), bf16),
            VMEM((few, width), bf16),
            VMEM((groups, GROUP, few, packed), bf16),
            VMEM((groups, few, width), bf16),
            VMEM((width, packed), f32),
            VMEM((wide, width), f32),
        ]
        + scatter_scratch(rows, width)
        + gather_sems() * 3
        + spread_sems() * 3
        + line_sems(groups, 2) * 2
        + [DMA, DMA, DMA((groups,)), DMA((groups,)), DMA, DMA, DMA],
        compiler_params=params(collective_id),
        name="front",
    )(lengths, x, ct, wq, wk, wv, wo, wu, wd, small)


def norm_back_rows(value, gain, grad):
    average = jnp.mean(value, axis=-1, keepdims=True)
    centred = value - average
    inverse = lax.rsqrt(jnp.mean(centred * centred, axis=-1, keepdims=True) + epsilon)
    xhat = centred * inverse
    scaled = grad * gain
    moved = inverse * (
        scaled
        - jnp.mean(scaled, axis=-1, keepdims=True)
        - xhat * jnp.mean(scaled * xhat, axis=-1, keepdims=True)
    )
    return moved, grad * xhat


def fold(value):
    total = value[0:8]
    for index in range(1, value.shape[0] // 8):
        total = total + value[index * 8 : index * 8 + 8]
    return total


def middle_kernel(
    count,
    length_ref,
    two_ref,
    part_ref,
    residual_ref,
    ct_ref,
    vec_ref,
    w_out_ref,
    qkv_ref,
    log_ref,
    mixed_ref,
    up_ref,
    down_ref,
    output_ref,
    grad_ref,
    grad_qkv_ref,
    grad_out_ref,
    sums_ref,
    up_got,
    down_total,
    branch_rows,
    branch_all,
    key_sum,
    value_sum,
    grad_two,
    folded,
    *rest,
):
    groups = count // GROUP
    me = lax.axis_index("fsdp")
    place = me % GROUP
    base = me - place
    two, rest = Scatter(place, base, rest[:SCATTER], two_ref), rest[SCATTER:]
    last, rest = Scatter(place, base, rest[:SCATTER], part_ref), rest[SCATTER:]
    sems, rest = rest[:7], rest[7:]
    up_line, rest = LineSum(me, groups, up_ref, rest[:LINE_SUM]), rest[LINE_SUM:]
    down_line, rest = LineSum(me, groups, down_ref, rest[:LINE_SUM]), rest[LINE_SUM:]
    up_swap = Swap(place, base, up_got, rest)
    length = length_ref[0]
    rows = ct_ref.shape[0]
    score_scale = 1.0 / math.sqrt(HD)
    greet_near(me, place, base, groups, range(1, GROUP))
    two.begin()
    up_line.begin()
    down_line.begin()
    last.begin()
    tasks = up_line.tasks() + down_line.tasks()
    for i in range(3):
        two.after(i)
    tasks.pop(0)()
    key_sum[...] = jnp.zeros_like(key_sum)
    value_sum[...] = jnp.zeros_like(value_sum)
    folded[...] = jnp.zeros_like(folded)

    def through_norm(span, value):
        moved, by_xhat = norm_back_rows(residual_ref[span, :], vec_ref[5:6, :], value)
        cotangent = ct_ref[span, :].astype(f32)
        total = cotangent + moved
        grad_ref[span, :] = total
        branch = total.astype(bf16)
        branch_rows[span, :] = branch
        for index, term in enumerate((by_xhat, value, branch.astype(f32), cotangent)):
            folded[index] = folded[index] + fold(term)

    two.finish(through_norm)
    gather_start(place, base, branch_rows, branch_all, sems)
    for index in range(4):
        sums_ref[index : index + 1, :] = jnp.sum(folded[index], axis=0, keepdims=True)
    sums_ref[4:8, :] = jnp.zeros((4, sums_ref.shape[1]), f32)

    def attend_back(block):
        here = pl.ds(pl.multiple_of(block * rows, rows), rows)
        grads = times_transposed(branch_all[block], w_out_ref[...]).astype(bf16)
        for head in range(HEADS_HERE):
            cols = pl.ds(head * LANES, LANES)
            query = qkv_ref[here, cols]
            key = qkv_ref[:, pl.ds((HEADS_HERE + head) * LANES, LANES)]
            value = qkv_ref[:, pl.ds((2 * HEADS_HERE + head) * LANES, LANES)]
            grad = grads[:, head * LANES : (head + 1) * LANES]
            weights = jnp.exp(masked_scores(length, query, key) - log_ref[head, here, :])
            grad_weights = times_transposed(grad, value)
            inner = jnp.sum(weights * grad_weights, axis=-1, keepdims=True)
            grad_scores = (weights * (grad_weights - inner)).astype(bf16)
            grad_qkv_ref[here, cols] = (matmul(grad_scores, key) * score_scale).astype(bf16)
            key_sum[:, cols] += outer_sum(grad_scores, query)
            value_sum[:, cols] += outer_sum(weights.astype(bf16), grad)

    def attend_pair(first, second):
        def run(turn, unused):
            attend_back(jnp.where(turn == 0, flip(place, first), flip(place, second)))
            return unused

        lax.fori_loop(0, 2, run, 0)

    args = (place, base, branch_rows, branch_all, sems)
    pltpu.make_async_copy(branch_rows, branch_all.at[place], sems[0]).wait()
    gather_own(*args).wait_recv()
    attend_pair(0, 1)
    gather_relay(*args)
    for slot in (2, 3):
        gather_piece(*args, slot).wait_recv()
        gather_pass(place, base, branch_all, sems, slot).start()
    tasks.pop(0)()
    attend_pair(2, 4)
    for slot in (4, 5):
        gather_piece(*args, slot).wait_recv()
        gather_pass(place, base, branch_all, sems, slot).start()
    for slot in range(4):
        gather_pass(place, base, branch_all, sems, slot).wait_recv()
    last.after(0)
    tasks.pop(0)()
    attend_pair(3, 5)
    last.after(1)
    if tasks:
        tasks.pop(0)()
    for slot in (4, 5):
        gather_pass(place, base, branch_all, sems, slot).wait_recv()
    attend_pair(6, 7)
    last.after(2)
    for task in tasks:
        task()
    up_line.finish()
    up_swap.begin(up_line.total)
    cols = pl.ds(HEADS_HERE * LANES, HEADS_HERE * LANES)
    grad_qkv_ref[:, cols] = (key_sum[...] * score_scale).astype(bf16)
    cols = pl.ds(2 * HEADS_HERE * LANES, HEADS_HERE * LANES)
    grad_qkv_ref[:, cols] = value_sum[...].astype(bf16)
    grad_out = jnp.zeros(grad_out_ref.shape, f32)
    for block in range(GROUP):
        grad_out = grad_out + outer_sum(
            mixed_ref[block * rows : (block + 1) * rows, :], branch_all[block]
        )
    grad_out_ref[...] = grad_out.astype(bf16)

    def residual_and(span, value):
        output_ref[span, :] = residual_ref[span, :] + (value + vec_ref[7:8, :])

    last.finish(residual_and)
    down_line.finish()
    add_slabs(
        down_total.shape[0],
        lambda index, value: down_total.__setitem__(index, value),
        lambda index: down_line.total[index],
    )
    up_swap.finish()
    gather_own(*args).wait_send()
    for slot in range(6):
        gather_piece(*args, slot).wait_send()
        gather_pass(place, base, branch_all, sems, slot).wait_send()
    two.drain()
    last.drain()
    up_line.drain()
    down_line.drain()


def middle(count, length, two, part, residual, ct, vec, w_out, qkv, log, mixed, up, down, cid):
    groups = count // GROUP
    rows, width = ct.shape
    clip = qkv.shape[0]
    wide = HEADS_HERE * LANES
    return pl.pallas_call(
        functools.partial(middle_kernel, count),
        out_shape=[
            shaped(rows, width, kind=f32),
            shaped(rows, width, kind=f32),
            shaped(clip, 3 * wide),
            shaped(wide, width),
            shaped(8, width, kind=f32),
            shaped(*up.shape[1:]),
            shaped(*down.shape[1:], kind=f32),
        ],
        in_specs=[pl.BlockSpec(memory_space=pltpu.SMEM)] + [ANYSPEC] * 2 + [VSPEC] * 9,
        out_specs=[VSPEC] * 7,
        scratch_shapes=[
            VMEM((rows, width), bf16),
            VMEM((GROUP, rows, width), bf16),
            VMEM((clip, wide), f32),
            VMEM((clip, wide), f32),
            VMEM((8, width), f32),
            VMEM((4, 8, width), f32),
        ]
        + scatter_scratch(rows, width, True)
        + scatter_scratch(rows, width, True)
        + gather_sems()
        + line_sum_scratch(groups, *up.shape[1:])
        + line_sum_scratch(groups, *down.shape[1:])
        + swap_scratch(*up.shape[2:]),
        compiler_params=params(cid),
        name="middle",
    )(length, two, part, residual, ct, vec, w_out, qkv, log, mixed, up, down)


def last_kernel(
    count,
    x_ref,
    normed_ref,
    grad_qkv_ref,
    w_qkv_ref,
    grad_ref,
    gain_ref,
    early_ref,
    out_ref,
    grad_inputs_ref,
    qkv_got,
    out_total,
    early_total,
    late_total,
    own_cols,
    cols,
    folded,
    late,
    early_got,
    late_got,
    out_got,
    *rest,
):
    groups = count // GROUP
    per = groups
    me = lax.axis_index("fsdp")
    place = me % GROUP
    base = me - place
    mine = me // GROUP
    rows, width = x_ref.shape
    few = own_cols.shape[2]
    one, rest = Scatter(place, base, rest[:SCATTER]), rest[SCATTER:]
    line, rest = LineSum(me, groups, own_cols, rest[:LINE_SUM]), rest[LINE_SUM:]
    swap, rest = Swap(place, base, qkv_got, rest[:SWAP]), rest[SWAP:]
    early_mail = Mail(me, count, early_ref, early_got, *rest[:3])
    late_mail = Mail(me, count, late, late_got, *rest[3:6])
    out_local, out_send, out_recv = rest[6:]
    greet_all(me, count)
    early_mail.begin()
    for index in range(per):
        owner = place * per + index

        @pl.when(owner != me)
        def _(index=index, owner=owner):
            remote(
                out_ref.at[index], out_got.at[mine], out_send.at[index], out_recv.at[mine], owner
            ).start()

        @pl.when(owner == me)
        def _(index=index):
            pltpu.make_async_copy(out_ref.at[index], out_got.at[mine], out_local).start()

    padded = 3 * HEADS_HERE * LANES
    packed = 3 * HEAD_COLS
    row = lax.broadcasted_iota(jnp.int32, (padded, packed), 0)
    col = lax.broadcasted_iota(jnp.int32, (padded, packed), 1)
    pick = jnp.where(
        (row // LANES == col // HD) & (row % LANES == col % HD), 1.0, 0.0
    ).astype(bf16)

    def weight_grad(index, unused):
        tile = pl.ds(pl.multiple_of(index * 256, 256), 256)
        grad = outer_sum(normed_ref[:, tile], grad_qkv_ref[...]).astype(bf16)
        cols[tile, :] = matmul(grad, pick)
        return unused

    lax.fori_loop(0, width // 256, weight_grad, 0)
    for owner in range(count):
        own_cols[owner // GROUP, owner % GROUP] = cols[owner * few : (owner + 1) * few, :].astype(
            bf16
        )
    line.begin()
    tasks = line.tasks()
    for i in range(4):

        def pair(turn, unused, i=i):
            block = jnp.where(turn == 0, one.block(i, True), one.block(i, False))
            here = pl.ds(pl.multiple_of(block * rows, rows), rows)
            one.parts[i, turn] = times_transposed(grad_qkv_ref[here, :], w_qkv_ref[...]).astype(
                bf16
            )

            @pl.when(turn == 0)
            def _():
                one.sibling(i).start()

            return unused

        lax.fori_loop(0, 2, pair, 0)
        one.after(i)
        if tasks and i > 0:
            tasks.pop(0)()
    for task in tasks:
        task()
    folded[...] = jnp.zeros_like(folded)

    def through_norm(span, value):
        moved, by_xhat = norm_back_rows(x_ref[span, :].astype(f32), gain_ref[0:1, :], value)
        grad_inputs_ref[span, :] = grad_ref[span, :] + moved
        folded[0] = folded[0] + fold(by_xhat)
        folded[1] = folded[1] + fold(value)

    one.finish(through_norm)
    line.finish()
    swap.begin(line.total)

    wide = HEADS_HERE * LANES

    def bias_sum(which):
        def add(index, value):
            span = pl.ds(pl.multiple_of(index * 64, 64), 64)
            return value + fold(grad_qkv_ref[span, which * wide : (which + 1) * wide].astype(f32))

        total = lax.fori_loop(
            0, grad_qkv_ref.shape[0] // 64, add, jnp.zeros((8, wide), f32)
        )
        row = lax.broadcasted_iota(jnp.int32, (wide, width), 0)
        col = lax.broadcasted_iota(jnp.int32, (wide, width), 1) - place * HEAD_COLS
        fits = (col >= 0) & (col < HEAD_COLS) & (row % LANES < HD)
        spot = jnp.where(fits & (row // LANES * HD + row % LANES == col), 1.0, 0.0)
        return jnp.sum(
            jnp.dot(total, spot, precision=lax.Precision.HIGHEST, preferred_element_type=f32),
            axis=0,
            keepdims=True,
        )

    vectors = jnp.concatenate(
        [
            jnp.sum(folded[0], axis=0, keepdims=True),
            jnp.sum(folded[1], axis=0, keepdims=True),
            bias_sum(0),
            bias_sum(2),
            jnp.zeros((4, width), f32),
        ],
        axis=0,
    )
    stretch = lax.broadcasted_iota(jnp.int32, (1, width), 1)
    row = lax.broadcasted_iota(jnp.int32, (width, LANES), 0)
    lane = lax.broadcasted_iota(jnp.int32, (width, LANES), 1)
    spot = jnp.where(row % few == lane, 1.0, 0.0)
    many = 8

    def owners(index, unused):
        terms = [
            jnp.where(stretch // few == index * many + k, vectors, 0.0) for k in range(many)
        ]
        slabs = jnp.dot(
            jnp.concatenate(terms, axis=0),
            spot,
            precision=lax.Precision.HIGHEST,
            preferred_element_type=f32,
        )
        for k in range(many):
            late[index * many + k] = slabs[k * 8 : k * 8 + 8]
        return unused

    lax.fori_loop(0, count // many, owners, 0)
    late_mail.begin()
    early_mail.finish(early_total)
    for index in range(per):
        owner = place * per + index

        @pl.when(owner != me)
        def _(index=index):
            remote(
                out_ref.at[index], out_got.at[mine], out_send.at[index], out_recv.at[mine], me
            ).wait_send()

        @pl.when(owner == me)
        def _(index=index):
            pltpu.make_async_copy(out_ref.at[index], out_got.at[mine], out_local).wait()

    for group in range(groups):

        @pl.when(group * GROUP + me // per != me)
        def _(group=group):
            remote(
                out_ref.at[0], out_got.at[group], out_send.at[0], out_recv.at[group], me
            ).wait_recv()

    total = out_got[0].astype(f32)
    for group in range(1, groups):
        total = total + out_got[group].astype(f32)
    out_total[...] = total
    swap.finish()
    late_mail.finish(late_total)
    one.drain()
    line.drain()


def last(count, x, normed, grad_qkv, w_qkv, grad, gain, early, out, collective_id):
    groups = count // GROUP
    rows, width = x.shape
    few = width // count
    packed = 3 * HEAD_COLS

    def mail(shape):
        return [DMA, DMA((count,)), DMA((count,))]

    return pl.pallas_call(
        functools.partial(last_kernel, count),
        out_shape=[
            shaped(rows, width, kind=f32),
            shaped(GROUP, few, packed),
            shaped(few, width, kind=f32),
            shaped(*early.shape[1:], kind=f32),
            shaped(8, LANES, kind=f32),
        ],
        in_specs=[VSPEC] * 8,
        out_specs=[VSPEC] * 5,
        scratch_shapes=[
            VMEM((groups, GROUP, few, packed), bf16),
            VMEM((width, packed), f32),
            VMEM((2, 8, width), f32),
            VMEM((count, 8, LANES), f32),
            VMEM(early.shape, f32),
            VMEM((count, 8, LANES), f32),
            VMEM((groups, few, width), bf16),
        ]
        + scatter_scratch(rows, width)
        + line_sum_scratch(groups, GROUP, few, packed)
        + swap_scratch(few, packed)
        + mail(early)
        + mail(early)
        + [DMA, DMA((groups,)), DMA((groups,))],
        compiler_params=params(collective_id),
        name="last",
    )(x, normed, grad_qkv, w_qkv, grad, gain, early, out)


def gelu_exact(values):
    return jax.nn.gelu(values, approximate=False)


def column_sums(matrix):
    return jnp.sum(matrix.astype(f32), axis=0)


def on_device(
    inputs,
    ln1_gain,
    ln1_bias,
    w_query,
    b_query,
    w_key,
    w_value,
    b_value,
    w_out,
    b_out,
    ln2_gain,
    ln2_bias,
    w_up,
    b_up,
    w_down,
    b_down,
    lengths,
    cotangent,
):
    count = lax.axis_size("fsdp")
    groups = count // GROUP
    me = lax.axis_index("fsdp")
    place = me % GROUP
    few = w_query.shape[0]
    many = w_down.shape[0]
    rows = inputs.shape[0]
    ff_here = groups * many

    up_lanes = -(-many // LANES)
    small = jnp.stack([ln1_gain, ln1_bias, b_query, b_value, b_out, ln2_gain, ln2_bias, b_down])
    small = jnp.concatenate(
        [
            jnp.pad(small, ((0, 0), (0, LANES - few))),
            jnp.pad(b_up, (0, up_lanes * LANES - many)).reshape(up_lanes, LANES),
            jnp.zeros((8 - up_lanes, LANES), f32),
        ]
    ).astype(bf16)
    (
        normed,
        w_qkv,
        qkv,
        w_out_here,
        attended,
        log,
        residual,
        vectors,
        small_all,
        two_all,
        ct_all,
        up_all,
        down_all,
    ) = front(
        count,
        lengths,
        inputs,
        cotangent,
        w_query,
        w_key,
        w_value,
        w_out,
        w_up,
        w_down,
        small,
        0,
    )
    b_up_here = lax.dynamic_index_in_dim(small_all, place, 1, keepdims=False)
    b_up_here = b_up_here[:, 8 : 8 + up_lanes].astype(f32)
    b_up_here = b_up_here.reshape(groups, up_lanes * LANES)[:, :many].reshape(ff_here)
    w_up_here = up_all.reshape(D, ff_here)
    w_down_here = down_all.reshape(ff_here, D)
    normed_two = two_all.reshape(GROUP * rows, D)
    length = lax.dynamic_slice_in_dim(lengths, me // GROUP, 1)

    ct = ct_all.reshape(GROUP * rows, D)
    hidden = matmul(normed_two, w_up_here) + b_up_here
    activated = gelu_exact(hidden).astype(bf16)
    out_part = matmul(activated, w_down_here).astype(bf16).reshape(GROUP, rows, D)

    grad_activated = times_transposed(ct, w_down_here)
    unused, gelu_pullback = jax.vjp(gelu_exact, hidden)
    grad_hidden = gelu_pullback(grad_activated)[0].astype(bf16)
    two_part = times_transposed(grad_hidden, w_up_here).astype(bf16).reshape(GROUP, rows, D)
    grad_w_up = outer_sum(normed_two, grad_hidden).astype(bf16)
    grad_w_down = outer_sum(activated, ct).astype(bf16)
    output, grad_residual, grad_qkv, grad_out, sums, up_got, down_total = middle(
        count,
        length,
        two_part,
        out_part,
        residual,
        cotangent,
        vectors,
        w_out_here,
        qkv,
        log,
        attended,
        grad_w_up.reshape(groups, GROUP, few, ff_here),
        grad_w_down.reshape(groups, many // few, few, D),
        2,
    )
    grad_out = grad_out.reshape(HEADS_HERE, LANES, D)[:, :HD].reshape(groups, few, D)
    grad_b_up = jnp.pad(
        column_sums(grad_hidden).reshape(groups, 1, many),
        ((0, 0), (0, 0), (0, up_lanes * LANES - many)),
    ).reshape(groups, 1, up_lanes, LANES)
    grad_b_up = jnp.where(
        (jnp.arange(GROUP) == place)[None, :, None, None], grad_b_up, 0.0
    ).reshape(count, up_lanes, LANES)
    early = jnp.pad(
        sums[:4].reshape(4, count, few).transpose(1, 0, 2), ((0, 0), (0, 0), (0, LANES - few))
    )
    early = jnp.concatenate(
        [early, grad_b_up, jnp.zeros((count, 4 - up_lanes, LANES), f32)], axis=1
    )
    grad_inputs, qkv_got, shard_w_out, early_sum, late_sum = last(
        count,
        inputs,
        normed,
        grad_qkv,
        w_qkv,
        grad_residual,
        vectors,
        early,
        grad_out,
        3,
    )

    def shard_of(which):
        piece = qkv_got[:, :, which * HEAD_COLS : (which + 1) * HEAD_COLS]
        return piece.transpose(1, 0, 2).reshape(few, D).astype(f32)

    shard_w_up = (
        up_got.reshape(GROUP, few, groups, many)
        .transpose(1, 2, 0, 3)
        .reshape(few, groups * GROUP * many)
        .astype(f32)
    )
    return (
        output,
        grad_inputs,
        late_sum[0, :few],
        late_sum[1, :few],
        shard_of(0),
        late_sum[2, :few],
        shard_of(1),
        shard_of(2),
        late_sum[3, :few],
        shard_w_out,
        early_sum[2, :few],
        early_sum[0, :few],
        early_sum[1, :few],
        shard_w_up,
        early_sum[4 : 4 + up_lanes].reshape(up_lanes * LANES)[:many],
        down_total.reshape(many, D),
        early_sum[3, :few],
    )


def solution(mesh):
    in_specs = (
        P("fsdp", None),
        P("fsdp"),
        P("fsdp"),
        P("fsdp", None),
        P("fsdp"),
        P("fsdp", None),
        P("fsdp", None),
        P("fsdp"),
        P("fsdp", None),
        P("fsdp"),
        P("fsdp"),
        P("fsdp"),
        P("fsdp", None),
        P("fsdp"),
        P("fsdp", None),
        P("fsdp"),
        P(),
        P("fsdp", None),
    )
    out_specs = (
        P("fsdp", None),
        P("fsdp", None),
        P("fsdp"),
        P("fsdp"),
        P("fsdp", None),
        P("fsdp"),
        P("fsdp", None),
        P("fsdp", None),
        P("fsdp"),
        P("fsdp", None),
        P("fsdp"),
        P("fsdp"),
        P("fsdp"),
        P("fsdp", None),
        P("fsdp"),
        P("fsdp", None),
        P("fsdp"),
    )
    return jax.shard_map(
        on_device, mesh=mesh, in_specs=in_specs, out_specs=out_specs, check_vma=False
    )
```

```python
import functools
import math

import jax
import jax.numpy as jnp
from jax import lax
from jax.experimental import pallas as pl
from jax.experimental.pallas import tpu as pltpu
from jax.sharding import PartitionSpec as P

D = 1280
H = 16
HD = 80
CLIP_LEN = 1536
GROUP = 8
LANES = 128
HEADS_HERE = H // GROUP
HEAD_COLS = HEADS_HERE * HD
SURE = CLIP_LEN * 3 // 4

epsilon = 1e-05
masked_value = -1e30
MESH = pl.DeviceIdType.MESH
VMEM = pltpu.VMEM
DMA = pltpu.SemaphoreType.DMA
bf16 = jnp.bfloat16
f32 = jnp.float32


def matmul(left, right):
    return jnp.dot(left, right, preferred_element_type=f32)


def outer_sum(left, right):
    return lax.dot_general(left, right, (((0,), (0,)), ((), ())), preferred_element_type=f32)


def times_transposed(left, right):
    return lax.dot_general(left, right, (((1,), (1,)), ((), ())), preferred_element_type=f32)


def flip(place, mask):
    for bit in (1, 2, 4):
        if mask & bit:
            place = place + bit - 2 * bit * (place // bit % 2)
    return place


def head_of(place, index):
    return place // 2 + H // 4 * (HEADS_HERE * (place % 2) + index)


def place_of(head):
    return 2 * (head % (H // 4)) + head // (H // 2)


def remote(src, dst, send_sem, recv_sem, target):
    return pltpu.make_async_remote_copy(
        src_ref=src,
        dst_ref=dst,
        send_sem=send_sem,
        recv_sem=recv_sem,
        device_id=(target,),
        device_id_type=MESH,
    )


def greet(targets):
    barrier = pltpu.get_barrier_semaphore()
    for target in targets:
        pl.semaphore_signal(barrier, inc=1, device_id=(target,), device_id_type=MESH)
    pl.semaphore_wait(barrier, len(targets))


def greet_all(me, count):
    barrier = pltpu.get_barrier_semaphore()

    def signal(step, unused):
        pl.semaphore_signal(
            barrier, inc=1, device_id=((me + step) % count,), device_id_type=MESH
        )
        return unused

    lax.fori_loop(1, count, signal, 0)
    pl.semaphore_wait(barrier, count - 1)


def params(collective_id):
    return pltpu.CompilerParams(collective_id=collective_id, has_side_effects=True)


ANYSPEC = pl.BlockSpec(memory_space=pl.ANY)
VSPEC = pl.BlockSpec(memory_space=pltpu.VMEM)


FAR = (2, 4, 6)
PIECES = ((0, 2), (1, 4), (1, 2), (0, 4), (0, 6), (1, 6))


def half_of(ref, owner, half):
    rows = ref.shape[1] // 2
    return ref.at[owner, pl.ds(half * rows, rows)]


def gather_sems():
    return [DMA, DMA, DMA, DMA((6,)), DMA((6,)), DMA((6,)), DMA((6,))]


def gather_piece(place, base, block, out, sems, slot):
    send, recv = sems[3:5]
    half, mask = PIECES[slot]
    rows = block.shape[0] // 2
    if slot < 4:
        src = block.at[pl.ds(half * rows, rows)]
        dst = half_of(out, place, half)
        target = flip(place, mask)
    else:
        near, far = (2, 4) if half == 0 else (4, 2)
        src = half_of(out, flip(place, near), half)
        dst = src
        target = flip(place, far)
    return remote(src, dst, send.at[slot], recv.at[slot], base + target)


def gather_pass(place, base, out, sems, slot):
    pass_send, pass_recv = sems[5:7]
    half, mask = PIECES[slot]
    piece = half_of(out, flip(place, mask), half)
    return remote(piece, piece, pass_send.at[slot], pass_recv.at[slot], base + flip(place, 1))


def gather_own(place, base, block, out, sems):
    return remote(block, out.at[place], sems[1], sems[2], base + flip(place, 1))


def gather_start(place, base, block, out, sems):
    for slot in (0, 1, 2, 3):
        gather_piece(place, base, block, out, sems, slot).start()
    pltpu.make_async_copy(block, out.at[place], sems[0]).start()
    gather_own(place, base, block, out, sems).start()


def gather_relay(place, base, block, out, sems):
    for slot, relay in ((0, 4), (1, 5)):
        gather_piece(place, base, block, out, sems, slot).wait_recv()
        gather_piece(place, base, block, out, sems, relay).start()
        gather_pass(place, base, out, sems, slot).start()


def gather_finish(place, base, block, out, sems):
    for slot in (2, 3, 4, 5):
        gather_piece(place, base, block, out, sems, slot).wait_recv()
        gather_pass(place, base, out, sems, slot).start()
    pltpu.make_async_copy(block, out.at[place], sems[0]).wait()
    gather_own(place, base, block, out, sems).wait()
    for slot in range(6):
        gather_piece(place, base, block, out, sems, slot).wait_send()
        gather_pass(place, base, out, sems, slot).wait()


ORDER = (6, 2, 4, 0)


def row_loop(rows, step, body):
    def run(index, unused):
        body(pl.ds(pl.multiple_of(index * step, step), step))
        return unused

    lax.fori_loop(0, rows // step, run, 0)


def scatter_scratch(rows, width, ready=False):
    half = rows // 2
    return [
        VMEM((4, rows, width) if ready else (4, 2, rows, width), bf16),
        VMEM((4, rows, width), bf16),
        VMEM((2, half, width), bf16),
        VMEM((2, rows, width), bf16),
        DMA((4,)),
        DMA((4,)),
        DMA((4,)),
        DMA((6,)),
        DMA((6,)),
    ]


SCATTER = 9


class Scatter:
    def __init__(self, place, base, scratch, ready=None):
        self.place, self.base, self.ready = place, base, ready
        self.parts, self.sib, self.relay, self.got = scratch[:4]
        self.local, self.sib_send, self.sib_recv, self.send, self.recv = scratch[4:]
        self.rows = self.got.shape[1]
        self.half = self.rows // 2

    def block(self, i, other):
        return flip(flip(self.place, ORDER[i]), 1 if other else 0)

    def block_at(self, step):
        i = step // 2
        place = self.place
        place = place + (1 - i // 2) * (2 - 4 * (place // 2 % 2))
        place = place + (1 - i % 2) * (4 - 8 * (place // 4 % 2))
        return place + (1 - step % 2) * (1 - 2 * (place % 2))

    def keep(self, i):
        return self.parts.at[i, 1] if self.ready is None else self.parts.at[i]

    def sibling(self, i):
        if self.ready is None:
            src = self.parts.at[i, 0]
        else:
            src = self.ready.at[self.block(i, True)]
        return remote(
            src,
            self.sib.at[i],
            self.sib_send.at[i],
            self.sib_recv.at[i],
            self.base + flip(self.place, 1),
        )

    def load(self, i):
        return pltpu.make_async_copy(
            self.ready.at[self.block(i, False)], self.keep(i), self.local.at[i]
        )

    def begin(self):
        for i in range(4):
            self.sibling(i).start()
            self.load(i).start()

    def link(self, slot):
        half = slot % 2
        span = pl.ds(half * self.half, self.half)
        if slot < 2:
            i, mask, dst = 0, (2, 4)[half], self.relay.at[half]
        else:
            i = slot // 2
            mask, dst = ORDER[i], self.got.at[i - 1, span]
        return remote(
            self.keep(i).at[span],
            dst,
            self.send.at[slot],
            self.recv.at[slot],
            self.base + flip(self.place, mask),
        )

    def merge(self, i):
        if self.ready is not None:
            self.load(i).wait()
        self.sibling(i).wait_recv()
        keep = self.keep(i)

        def body(span):
            keep[span, :] = (
                keep[span, :].astype(f32) + self.sib[i, span, :].astype(f32)
            ).astype(bf16)

        row_loop(self.rows, 32, body)

    def merge_relay(self, i, half):
        self.link(half).wait_recv()
        start = half * self.half
        keep = self.keep(i)

        def run(index, unused):
            here = pl.multiple_of(index * 32, 32)
            span = pl.ds(start + here, 32)
            keep[span, :] = (
                keep[span, :].astype(f32) + self.relay[half, pl.ds(here, 32), :].astype(f32)
            ).astype(bf16)
            return unused

        lax.fori_loop(0, self.half // 32, run, 0)

    def after(self, i):
        if i < 3:
            self.merge(i)
        if i == 0:
            self.link(0).start()
            self.link(1).start()
        if i == 1:
            self.link(2).start()
        if i == 2:
            self.link(5).start()
            self.merge_relay(1, 1)
            self.link(3).start()
            self.merge_relay(2, 0)
            self.link(4).start()

    def finish(self, use):
        if self.ready is not None:
            self.load(3).wait()
        self.sibling(3).wait_recv()
        for slot in range(2, 6):
            self.link(slot).wait_recv()
        keep = self.keep(3)

        def body(span):
            value = keep[span, :].astype(f32) + self.sib[3, span, :].astype(f32)
            value = value + self.got[0, span, :].astype(f32)
            use(span, value + self.got[1, span, :].astype(f32))

        row_loop(self.rows, 32, body)

    def drain(self):
        for i in range(4):
            self.sibling(i).wait_send()
        for slot in range(6):
            self.link(slot).wait_send()


def line_send(me, groups, outs, sems, step):
    mine = me // GROUP
    for which, out in enumerate(outs):
        up_send, up_recv, down_send, down_recv = sems[4 * which : 4 * which + 4]

        @pl.when((mine - step >= 0) & (mine + 1 < groups))
        def _(out=out, up_send=up_send, up_recv=up_recv):
            slab = out.at[mine - step]
            remote(slab, slab, up_send.at[step], up_recv.at[step], me + GROUP).start()

        @pl.when((mine + step < groups) & (mine >= 1))
        def _(out=out, down_send=down_send, down_recv=down_recv):
            slab = out.at[mine + step]
            remote(slab, slab, down_send.at[step], down_recv.at[step], me - GROUP).start()


def line_wait(me, groups, outs, sems, step):
    mine = me // GROUP
    for which, out in enumerate(outs):
        up_send, up_recv, down_send, down_recv = sems[4 * which : 4 * which + 4]

        @pl.when(mine - 1 - step >= 0)
        def _(out=out, up_send=up_send, up_recv=up_recv):
            slab = out.at[mine - 1 - step]
            remote(slab, slab, up_send.at[step], up_recv.at[step], me).wait_recv()

        @pl.when(mine + 1 + step < groups)
        def _(out=out, down_send=down_send, down_recv=down_recv):
            slab = out.at[mine + 1 + step]
            remote(slab, slab, down_send.at[step], down_recv.at[step], me).wait_recv()


def line_gather(me, groups, outs, sems):
    for step in range(groups - 1):
        line_send(me, groups, outs, sems, step)
        line_wait(me, groups, outs, sems, step)


def line_gather_drain(me, groups, outs, sems):
    mine = me // GROUP
    for step in range(groups - 1):
        for which, out in enumerate(outs):
            up_send, up_recv, down_send, down_recv = sems[4 * which : 4 * which + 4]

            @pl.when((mine - step >= 0) & (mine + 1 < groups))
            def _(out=out, up_send=up_send, up_recv=up_recv):
                slab = out.at[0]
                remote(slab, slab, up_send.at[step], up_recv.at[step], me).wait_send()

            @pl.when((mine + step < groups) & (mine >= 1))
            def _(out=out, down_send=down_send, down_recv=down_recv):
                slab = out.at[0]
                remote(slab, slab, down_send.at[step], down_recv.at[step], me).wait_send()


def line_sems(groups, arrays):
    return [DMA((groups,))] * (4 * arrays)


class Spread:
    def __init__(self, place, base, pack, out, scratch, one=False):
        self.place, self.base, self.pack, self.out, self.one = place, base, pack, out, one
        self.local, self.send, self.recv = scratch

    def slab(self, target):
        return self.pack if self.one else self.pack.at[target]

    def copy(self, mask):
        target = flip(self.place, mask)
        return remote(
            self.slab(target),
            self.out.at[self.place],
            self.send.at[mask],
            self.recv.at[mask],
            self.base + target,
        )

    def own(self):
        return pltpu.make_async_copy(
            self.slab(self.place), self.out.at[self.place], self.local
        )

    def begin(self):
        for mask in (6, 2, 4, 7, 3, 5, 1):
            self.copy(mask).start()
        self.own().start()

    def finish(self):
        self.own().wait()
        for mask in range(1, GROUP):
            self.copy(mask).wait()


SPREAD = 3


def spread_sems():
    return [DMA, DMA((GROUP,)), DMA((GROUP,))]


def greet_near(me, place, base, groups, masks):
    barrier = pltpu.get_barrier_semaphore()
    mine = me // GROUP
    for mask in masks:
        pl.semaphore_signal(
            barrier, inc=1, device_id=(base + flip(place, mask),), device_id_type=MESH
        )

    @pl.when(mine > 0)
    def _():
        pl.semaphore_signal(barrier, inc=1, device_id=(me - GROUP,), device_id_type=MESH)

    @pl.when(mine < groups - 1)
    def _():
        pl.semaphore_signal(barrier, inc=1, device_id=(me + GROUP,), device_id_type=MESH)

    both = jnp.where(mine > 0, 1, 0) + jnp.where(mine < groups - 1, 1, 0)
    pl.semaphore_wait(barrier, len(masks) + both)


def shaped(*shape, kind=bf16):
    return jax.ShapeDtypeStruct(shape, kind)


def add_slabs(blocks, store, *terms):
    def body(index, unused):
        value = terms[0](index).astype(f32)
        for term in terms[1:]:
            value = value + term(index).astype(f32)
        store(index, value)
        return unused

    lax.fori_loop(0, blocks, body, 0)


def line_sum_scratch(groups, slabs, rows, width):
    return [
        VMEM((groups + 1, slabs, rows, width), bf16),
        VMEM((slabs, rows, width), f32),
    ] + line_sems(groups, 1)


LINE_SUM = 6


class LineSum:
    def __init__(self, me, groups, own, scratch):
        self.me, self.groups, self.own = me, groups, own
        self.came, self.total = scratch[:2]
        self.up_send, self.up_recv, self.down_send, self.down_recv = scratch[2:]
        self.mine = me // GROUP
        self.blocks = own.shape[1]

    def up(self, target, src):
        return remote(
            src.at[target],
            self.came.at[target],
            self.up_send.at[target],
            self.up_recv.at[target],
            self.me + GROUP,
        )

    def down(self, target, src):
        last = jnp.where(self.mine - 1 == target, self.groups, target)
        return remote(
            src.at[target],
            self.came.at[last],
            self.down_send.at[target],
            self.down_recv.at[target],
            self.me - GROUP,
        )

    def add(self, target):
        def store(index, value):
            self.came[target, index] = value.astype(bf16)

        add_slabs(
            self.blocks,
            store,
            lambda index: self.own[target, index],
            lambda index: self.came[target, index],
        )

    def begin(self):
        for target in range(self.groups - 1, 0, -1):
            low = self.groups - 1 - target

            @pl.when((self.mine == 0))
            def _(target=target):
                self.up(target, self.own).start()

            @pl.when(self.mine == self.groups - 1)
            def _(low=low):
                self.down(low, self.own).start()

    def pass_up(self, target):
        self.up(target, self.own).wait_recv()
        self.add(target)
        self.up(target, self.came).start()

    def pass_down(self, target):
        self.down(target, self.own).wait_recv()
        self.add(target)
        self.down(target, self.came).start()

    def tasks(self):
        top = self.groups - 1

        def step(hops):
            for order in range(top):
                passed = hops - order
                if 1 <= passed < top - order:
                    pl.when(self.mine == passed)(functools.partial(self.pass_up, top - order))
                    pl.when(self.mine == top - passed)(functools.partial(self.pass_down, order))

        return [functools.partial(step, hops) for hops in range(1, top)]

    def finish(self):
        def store(index, value):
            self.total[index] = value

        def put(index, value):
            self.total[index] = self.total[index] + value

        add_slabs(self.blocks, store, lambda index: self.own[self.mine, index])
        for target in range(self.groups):

            @pl.when((self.mine == target) & (target > 0))
            def _(target=target):
                self.up(target, self.own).wait_recv()
                add_slabs(self.blocks, put, lambda index: self.came[target, index])

            @pl.when((self.mine == target) & (target < self.groups - 1))
            def _(target=target):
                self.down(target, self.own).wait_recv()
                add_slabs(self.blocks, put, lambda index: self.came[self.groups, index])

    def drain(self):
        for target in range(self.groups):

            @pl.when(self.mine < target)
            def _(target=target):
                self.up(target, self.own).wait_send()

            @pl.when(self.mine > target)
            def _(target=target):
                self.down(target, self.own).wait_send()


def swap_scratch(rows, width):
    return [VMEM((GROUP, rows, width), bf16), DMA, DMA((GROUP,)), DMA((GROUP,))]


SWAP = 4


class Swap:
    def __init__(self, place, base, got, scratch):
        self.place, self.base, self.got = place, base, got
        self.give, self.local, self.send, self.recv = scratch

    def copy(self, mask):
        target = flip(self.place, mask)
        return remote(
            self.give.at[target],
            self.got.at[self.place],
            self.send.at[mask],
            self.recv.at[mask],
            self.base + target,
        )

    def own(self):
        return pltpu.make_async_copy(
            self.give.at[self.place], self.got.at[self.place], self.local
        )

    def begin(self, total):
        def store(index, value):
            self.give[index] = value.astype(bf16)

        add_slabs(GROUP, store, lambda index: total[index])
        for mask in range(1, GROUP):
            self.copy(mask).start()
        self.own().start()

    def finish(self):
        self.own().wait()
        for mask in range(1, GROUP):
            self.copy(mask).wait()


class Mail:
    def __init__(self, me, count, given, got, local, send, recv, one=False):
        self.me, self.count, self.given, self.got, self.one = me, count, given, got, one
        self.local, self.send, self.recv = local, send, recv

    def slab(self, target):
        return self.given if self.one else self.given.at[target]

    def copy(self, step):
        target = (self.me + step) % self.count
        return remote(
            self.slab(target),
            self.got.at[self.me],
            self.send.at[step],
            self.recv.at[step],
            target,
        )

    def own(self):
        return pltpu.make_async_copy(self.slab(self.me), self.got.at[self.me], self.local)

    def begin(self):
        self.own().start()

        def run(step, unused):
            self.copy(step).start()
            return unused

        lax.fori_loop(1, self.count, run, 0)

    def wait(self):
        self.own().wait()

        def run(step, unused):
            self.copy(step).wait()
            return unused

        lax.fori_loop(1, self.count, run, 0)

    def finish(self, total):
        self.wait()

        def add(index, value):
            return value + self.got[index]

        total[...] = lax.fori_loop(
            0, self.count, add, jnp.zeros(self.got.shape[1:], f32)
        )


def masked_scores(length, query, key):
    scores = times_transposed(query, key) * (1.0 / math.sqrt(HD))
    tail = scores[:, SURE:]
    place = SURE + lax.broadcasted_iota(jnp.int32, tail.shape, 1)
    return jnp.concatenate(
        [scores[:, :SURE], jnp.where(place < length, tail, masked_value)], axis=1
    )


def norm_rows(value):
    average = jnp.mean(value, axis=-1, keepdims=True)
    centred = value - average
    inverse = lax.rsqrt(jnp.mean(centred * centred, axis=-1, keepdims=True) + epsilon)
    return centred * inverse


class DirectOut:
    def __init__(self, me, count, shard, slabs, local, send, recv):
        self.me, self.groups, self.shard, self.slabs = me, count // GROUP, shard, slabs
        self.local, self.send, self.recv = local, send, recv
        self.each = self.groups // HEADS_HERE
        head = me // self.each
        self.wanted = place_of(head)
        self.slot = head // (H // 4) % HEADS_HERE * self.each + me % self.each

    def owner(self, place, index):
        return head_of(place, index // self.each) * self.each + index % self.each

    def copy(self, group):
        return remote(
            self.shard,
            self.slabs.at[self.slot],
            self.send.at[group],
            self.recv.at[self.slot],
            group * GROUP + self.wanted,
        )

    def own(self):
        return pltpu.make_async_copy(self.shard, self.slabs.at[self.slot], self.local)

    def begin(self):
        for group in range(self.groups):
            mine = group * GROUP + self.wanted == self.me
            pl.when(jnp.logical_not(mine))(self.copy(group).start)
            pl.when(mine)(self.own().start)

    def finish(self, place):
        for group in range(self.groups):
            mine = group * GROUP + self.wanted == self.me
            pl.when(jnp.logical_not(mine))(self.copy(group).wait_send)
            pl.when(mine)(self.own().wait)
        for index in range(self.groups):
            copy = remote(
                self.shard, self.slabs.at[index], self.send.at[0], self.recv.at[index], self.me
            )
            pl.when(self.owner(place, index) != self.me)(copy.wait_recv)


class DirectBack:
    def __init__(self, me, count, given, got, local, send, recv):
        self.me, self.groups, self.given, self.got = me, count // GROUP, given, got
        self.local, self.send, self.recv = local, send, recv
        self.each = self.groups // HEADS_HERE
        self.mine = me // GROUP

    def owner(self, index):
        head = head_of(self.me % GROUP, index // self.each)
        return head * self.each + index % self.each

    def copy(self, index):
        return remote(
            self.given.at[index],
            self.got.at[self.mine],
            self.send.at[index],
            self.recv.at[self.mine],
            self.owner(index),
        )

    def own(self, index):
        return pltpu.make_async_copy(self.given.at[index], self.got.at[self.mine], self.local)

    def begin(self):
        for index in range(self.groups):
            mine = self.owner(index) == self.me
            pl.when(jnp.logical_not(mine))(self.copy(index).start)
            pl.when(mine)(self.own(index).start)

    def finish(self, total_ref):
        for index in range(self.groups):
            mine = self.owner(index) == self.me
            pl.when(jnp.logical_not(mine))(self.copy(index).wait_send)
            pl.when(mine)(self.own(index).wait)
        sender = place_of(self.me // self.each)
        for group in range(self.groups):
            copy = remote(
                self.given.at[0], self.got.at[group], self.send.at[0], self.recv.at[group], self.me
            )
            pl.when(group * GROUP + sender != self.me)(copy.wait_recv)
        total = self.got[0].astype(f32)
        for group in range(1, self.groups):
            total = total + self.got[group].astype(f32)
        total_ref[...] = total


def on_lines(count):
    return count == 2 * H


def head_pick(rows, cols):
    row = lax.broadcasted_iota(jnp.int32, (rows, cols), 0)
    col = lax.broadcasted_iota(jnp.int32, (rows, cols), 1)
    return jnp.where((col // LANES == row // HD) & (col % LANES == row % HD), 1.0, 0.0).astype(bf16)


def front_kernel(
    count,
    length_ref,
    x_ref,
    ct_ref,
    wq_ref,
    wk_ref,
    wv_ref,
    wo_ref,
    wu_ref,
    wd_ref,
    small_ref,
    normed_out,
    w_qkv_out,
    qkv_out,
    w_out_ref,
    mixed_ref,
    log_ref,
    residual_ref,
    vec_ref,
    small_all,
    two_all,
    ct_all,
    up_all,
    down_all,
    x_all,
    normed_ref,
    w_qkv_ref,
    qkv_ref,
    two_rows,
    pack_qkv,
    pack_up,
    down_ref,
    out_ref,
    qkv_slabs,
    out_slabs,
    out_sib,
    small_flat,
    wide_w,
    wide_out,
    *rest,
):
    groups = count // GROUP
    per = groups
    me = lax.axis_index("fsdp")
    place = me % GROUP
    base = me - place
    mine = me // GROUP
    rows, width = x_ref.shape
    few = wq_ref.shape[0]
    many = wd_ref.shape[0]
    packed = 3 * HEAD_COLS
    wide = HEADS_HERE * LANES
    scatter, rest = Scatter(place, base, rest[:SCATTER]), rest[SCATTER:]
    x_sems, rest = rest[:7], rest[7:]
    two_sems, rest = rest[:7], rest[7:]
    ct_sems, rest = rest[:7], rest[7:]
    qkv_spread, rest = (
        Spread(place, base, pack_qkv, qkv_slabs.at[mine], rest[:SPREAD]),
        rest[SPREAD:],
    )
    up_spread, rest = (
        Spread(place, base, pack_up, up_all.at[mine], rest[:SPREAD]),
        rest[SPREAD:],
    )
    line_q, rest = rest[:4], rest[4:]
    line_u, rest = rest[:8], rest[8:]
    line_o, rest = rest[:4], rest[4:]
    small_mail, rest = Mail(me, count, small_ref, small_flat, *rest[:3], one=True), rest[3:]
    down_local, out_local, out_send, out_recv, keep_normed, keep_w, keep_qkv, keep_small = rest
    length = length_ref[me // GROUP]
    core = place % 2
    fast = on_lines(count)

    for other in range(GROUP):
        for head in range(HEADS_HERE):
            cols = slice(head_of(other, head) * HD, (head_of(other, head) + 1) * HD)
            for index, ref in enumerate((wq_ref, wk_ref, wv_ref)):
                start = index * HEAD_COLS + head * HD
                pack_qkv[other, :, start : start + HD] = ref[:, cols].astype(bf16)
    greet_all(me, count)
    qkv_spread.begin()
    small_mail.begin()
    x_args = (place, base, x_ref, x_all, x_sems)
    ct_args = (place, base, ct_ref, ct_all, ct_sems)
    two_args = (place, base, two_rows, two_all, two_sems)
    gather_start(*x_args)
    for other in range(GROUP):
        for group in range(groups):
            start = (group * GROUP + other) * many
            pack_up[other, :, group * many : (group + 1) * many] = wu_ref[
                :, start : start + many
            ].astype(bf16)
    down_ref[...] = wd_ref[...].astype(bf16)
    out_ref[...] = wo_ref[...].astype(bf16)
    own_down = pltpu.make_async_copy(down_ref, down_all.at[mine], down_local)
    own_down.start()
    qkv_spread.finish()
    line_send(me, groups, [qkv_slabs], line_q, 0)
    small_mail.wait()
    keep_four = pltpu.make_async_copy(small_flat, small_all, keep_small)
    keep_four.start()

    kinds = small_ref.shape[0]
    row = lax.broadcasted_iota(jnp.int32, (LANES, width), 0)
    lane = lax.broadcasted_iota(jnp.int32, (LANES, width), 1)
    tile = jnp.where((lane % few == row) & (row < few), 1.0, 0.0).astype(bf16)
    owner = lax.broadcasted_iota(jnp.int32, (1, width), 1) // few

    def lay(group, value):
        slabs = small_flat[pl.ds(pl.multiple_of(group * GROUP, GROUP), GROUP)]
        spots = matmul(slabs.reshape(GROUP * kinds, LANES), tile)
        for other in range(GROUP):
            spot = spots[other * kinds : (other + 1) * kinds]
            value = value + jnp.where(owner == group * GROUP + other, spot, 0.0)
        return value

    vectors = lax.fori_loop(0, groups, lay, jnp.zeros((kinds, width), f32))
    vec_ref[...] = vectors[:8]
    gain, offset = vec_ref[0:1, :], vec_ref[1:2, :]

    def first_norm(index, unused):
        for part in range(rows // 32):
            span = pl.ds(part * 32, 32)
            value = x_all[index, span, :].astype(f32)
            normed_ref[
                pl.ds(pl.multiple_of(index * rows, rows) + part * 32, 32), :
            ] = (norm_rows(value) * gain + offset).astype(bf16)
        return unused

    gather_relay(*x_args)
    line_wait(me, groups, [qkv_slabs], line_q, 0)
    line_send(me, groups, [qkv_slabs], line_q, 1)
    gather_finish(*x_args)
    up_spread.begin()
    gather_start(*ct_args)
    lax.fori_loop(0, GROUP // 2, first_norm, 0)
    line_wait(me, groups, [qkv_slabs], line_q, 1)
    for step in range(2, groups - 1):
        line_send(me, groups, [qkv_slabs], line_q, step)
        if step < groups - 2:
            line_wait(me, groups, [qkv_slabs], line_q, step)
    lax.fori_loop(GROUP // 2, GROUP, first_norm, 0)
    keep = pltpu.make_async_copy(normed_ref, normed_out, keep_normed)
    keep.start()
    line_wait(me, groups, [qkv_slabs], line_q, groups - 2)

    line = [up_all, down_all]
    if fast:
        keep_out = pltpu.make_async_copy(out_ref, out_slabs.at[mine], out_local)
        keep_out.start()
        keep_out.wait()
        line_send(me, groups, [out_slabs], line_o, 0)
    else:
        direct = DirectOut(me, count, out_ref, out_slabs, out_local, out_send, out_recv)
        direct.begin()

    for source in range(count):
        wide_w[source * few : (source + 1) * few, :] = qkv_slabs[
            source // GROUP, source % GROUP
        ].astype(f32)
    pick = head_pick(packed, 3 * wide)

    def widen_rows(span):
        w_qkv_ref[span, :] = matmul(wide_w[span, :].astype(bf16), pick).astype(bf16)

    row_loop(width, 256, widen_rows)
    if fast:
        line_wait(me, groups, [out_slabs], line_o, 0)
        line_send(me, groups, [out_slabs], line_o, 1)
    keep_two = pltpu.make_async_copy(w_qkv_ref, w_qkv_out, keep_w)
    keep_two.start()
    row = lax.broadcasted_iota(jnp.int32, (width, wide), 0)
    col = lax.broadcasted_iota(jnp.int32, (width, wide), 1)
    spot = jnp.where(
        (col % LANES < HD) & (row == head_of(place, col // LANES) * HD + col % LANES), 1.0, 0.0
    ).astype(bf16)
    biases = matmul(vectors.astype(bf16), spot)
    bias = jnp.concatenate([biases[2:3], jnp.zeros((1, wide), f32), biases[3:4]], axis=1)

    def project(index, unused):
        span = pl.ds(pl.multiple_of(index * rows, rows), rows)
        qkv_ref[span, :] = (matmul(normed_ref[span, :], w_qkv_ref[...]) + bias).astype(bf16)
        return unused

    gather_relay(*ct_args)
    up_spread.finish()
    own_down.wait()
    lax.fori_loop(0, GROUP // 2, project, 0)
    if fast:
        line_wait(me, groups, [out_slabs], line_o, 1)
        line_send(me, groups, [out_slabs], line_o, 2)
    line_send(me, groups, line[:1], line_u[:4], 0)
    line_send(me, groups, line[1:], line_u[4:], 0)
    lax.fori_loop(GROUP // 2, GROUP, project, 0)
    keep_three = pltpu.make_async_copy(qkv_ref, qkv_out, keep_qkv)
    keep_three.start()

    wide_out[...] = jnp.zeros_like(wide_out)
    if fast:
        line_wait(me, groups, [out_slabs], line_o, 2)
        crossing = []
        for head in range(HEADS_HERE):
            copy = remote(
                out_slabs.at[HEADS_HERE * (1 - core) + head],
                out_sib.at[head],
                out_send.at[head],
                out_recv.at[head],
                base + flip(place, 1),
            )
            copy.start()
            crossing.append(copy)
        for head in range(HEADS_HERE):
            here = pl.multiple_of(head * LANES + few * core, 8)
            wide_out[pl.ds(here, few), :] = out_slabs[HEADS_HERE * core + head].astype(f32)
        for head, copy in enumerate(crossing):
            copy.wait()
            here = pl.multiple_of(head * LANES + few * (1 - core), 8)
            wide_out[pl.ds(here, few), :] = out_sib[head].astype(f32)
    else:
        direct.finish(place)
        for index in range(per):
            start = index * few
            start = start // HD * LANES + start % HD
            wide_out[start : start + few, :] = out_slabs[index].astype(f32)
    w_out_ref[...] = wide_out[...].astype(bf16)

    tasks = []
    for step in range(groups - 1):
        for which in range(2):

            def task(step=step, which=which):
                sems = line_u[4 * which : 4 * which + 4]
                line_wait(me, groups, [line[which]], sems, step)
                if step < groups - 2:
                    line_send(me, groups, [line[which]], sems, step + 1)

            tasks.append(task)

    def attend_rows(block):
        here = pl.ds(pl.multiple_of(block * rows, rows), rows)
        for head in range(HEADS_HERE):
            cols = pl.ds(head * LANES, LANES)
            scores = masked_scores(
                length, qkv_ref[here, cols], qkv_ref[:, pl.ds((HEADS_HERE + head) * LANES, LANES)]
            )
            largest = jnp.max(scores, axis=-1, keepdims=True)
            exponent = jnp.exp(scores - largest)
            total = jnp.sum(exponent, axis=-1, keepdims=True)
            weights = (exponent * (1.0 / total)).astype(bf16)
            value = qkv_ref[:, pl.ds((2 * HEADS_HERE + head) * LANES, LANES)]
            mixed_ref[here, cols] = matmul(weights, value).astype(bf16)
            log_ref[head, here, :] = largest + jnp.log(total)
        return matmul(mixed_ref[here, :], w_out_ref[...]).astype(bf16)

    def attend_step(step, unused):
        i, turn = step // 2, step % 2
        scatter.parts[i, turn] = attend_rows(scatter.block_at(step))
        pl.when(turn == 0)(lambda: scatter.sibling(i).start())
        for k in range(8):

            @pl.when(step == k)
            def _(k=k):
                if k % 2:
                    scatter.after(k // 2)
                if k == 4:
                    gather_finish(*ct_args)
                if k == 6:
                    tasks[0]()

        return unused

    lax.fori_loop(0, 8, attend_step, 0)

    def normalize(span, value):
        total = x_ref[span, :].astype(f32) + (value + vec_ref[4:5, :])
        residual_ref[span, :] = total
        two_rows[span, :] = (norm_rows(total) * vec_ref[5:6, :] + vec_ref[6:7, :]).astype(bf16)

    scatter.finish(normalize)
    gather_start(*two_args)
    tasks[1]()
    gather_relay(*two_args)
    tasks[2]()
    gather_finish(*two_args)
    for task in tasks[3:]:
        task()
    scatter.drain()
    line_gather_drain(me, groups, [qkv_slabs], line_q)
    line_gather_drain(me, groups, line, line_u)
    if fast:
        line_gather_drain(me, groups, [out_slabs], line_o)
    keep.wait()
    keep_two.wait()
    keep_three.wait()
    keep_four.wait()


def front(count, lengths, x, ct, wq, wk, wv, wo, wu, wd, small, collective_id):
    groups = count // GROUP
    rows, width = x.shape
    clip = GROUP * rows
    few = wq.shape[0]
    many = wd.shape[0]
    packed = 3 * HEAD_COLS
    wide = HEADS_HERE * LANES
    return pl.pallas_call(
        functools.partial(front_kernel, count),
        out_shape=[
            shaped(clip, width),
            shaped(width, 3 * wide),
            shaped(clip, 3 * wide),
            shaped(wide, width),
            shaped(clip, wide),
            shaped(HEADS_HERE, clip, 1, kind=f32),
            shaped(rows, width, kind=f32),
            shaped(8, width, kind=f32),
            shaped(count, *small.shape),
            shaped(GROUP, rows, width),
            shaped(GROUP, rows, width),
            shaped(groups, GROUP, few, groups * many),
            shaped(groups, many, width),
        ],
        in_specs=[pl.BlockSpec(memory_space=pltpu.SMEM)] + [VSPEC] * 9,
        out_specs=[ANYSPEC] * 3 + [VSPEC] * 6 + [ANYSPEC] * 4,
        scratch_shapes=[
            VMEM((GROUP, rows, width), bf16),
            VMEM((clip, width), bf16),
            VMEM((width, 3 * wide), bf16),
            VMEM((clip, 3 * wide), bf16),
            VMEM((rows, width), bf16),
            VMEM((GROUP, few, packed), bf16),
            VMEM((GROUP, few, groups * many), bf16),
            VMEM((many, width), bf16),
            VMEM((few, width), bf16),
            VMEM((groups, GROUP, few, packed), bf16),
            VMEM((groups, few, width), bf16),
            VMEM((HEADS_HERE, few, width), bf16),
            VMEM((count, *small.shape), bf16),
            VMEM((width, packed), f32),
            VMEM((wide, width), f32),
        ]
        + scatter_scratch(rows, width)
        + gather_sems() * 3
        + spread_sems() * 2
        + line_sems(groups, 1)
        + line_sems(groups, 2)
        + line_sems(groups, 1)
        + [DMA, DMA((count,)), DMA((count,))]
        + [DMA, DMA, DMA((groups,)), DMA((groups,)), DMA, DMA, DMA, DMA],
        compiler_params=params(collective_id),
        name="front",
    )(lengths, x, ct, wq, wk, wv, wo, wu, wd, small)


def norm_back_rows(value, gain, grad):
    average = jnp.mean(value, axis=-1, keepdims=True)
    centred = value - average
    inverse = lax.rsqrt(jnp.mean(centred * centred, axis=-1, keepdims=True) + epsilon)
    xhat = centred * inverse
    scaled = grad * gain
    moved = inverse * (
        scaled
        - jnp.mean(scaled, axis=-1, keepdims=True)
        - xhat * jnp.mean(scaled * xhat, axis=-1, keepdims=True)
    )
    return moved, grad * xhat


def fold(value):
    total = value[0:8]
    for index in range(1, value.shape[0] // 8):
        total = total + value[index * 8 : index * 8 + 8]
    return total


def middle_kernel(
    count,
    length_ref,
    two_ref,
    part_ref,
    residual_ref,
    ct_ref,
    vec_ref,
    w_out_ref,
    qkv_ref,
    log_ref,
    mixed_ref,
    up_ref,
    down_ref,
    output_ref,
    grad_ref,
    grad_qkv_ref,
    grad_out_ref,
    sums_ref,
    up_got,
    down_total,
    branch_rows,
    branch_all,
    key_sum,
    value_sum,
    grad_two,
    folded,
    *rest,
):
    groups = count // GROUP
    me = lax.axis_index("fsdp")
    place = me % GROUP
    base = me - place
    two, rest = Scatter(place, base, rest[:SCATTER], two_ref), rest[SCATTER:]
    last, rest = Scatter(place, base, rest[:SCATTER], part_ref), rest[SCATTER:]
    sems, rest = rest[:7], rest[7:]
    up_line, rest = LineSum(me, groups, up_ref, rest[:LINE_SUM]), rest[LINE_SUM:]
    down_line, rest = LineSum(me, groups, down_ref, rest[:LINE_SUM]), rest[LINE_SUM:]
    up_swap = Swap(place, base, up_got, rest)
    length = length_ref[0]
    rows = ct_ref.shape[0]
    score_scale = 1.0 / math.sqrt(HD)
    greet_near(me, place, base, groups, range(1, GROUP))
    two.begin()
    up_line.begin()
    down_line.begin()
    last.begin()
    tasks = up_line.tasks() + down_line.tasks()
    for i in range(3):
        two.after(i)
    early = len(tasks) // 4
    for task in tasks[:early]:
        task()
    tasks = tasks[early:]
    key_sum[...] = jnp.zeros_like(key_sum)
    value_sum[...] = jnp.zeros_like(value_sum)
    folded[...] = jnp.zeros_like(folded)

    def through_norm(span, value):
        moved, by_xhat = norm_back_rows(residual_ref[span, :], vec_ref[5:6, :], value)
        cotangent = ct_ref[span, :].astype(f32)
        total = cotangent + moved
        grad_ref[span, :] = total
        branch = total.astype(bf16)
        branch_rows[span, :] = branch
        for index, term in enumerate((by_xhat, value, branch.astype(f32), cotangent)):
            folded[index] = folded[index] + fold(term)

    two.finish(through_norm)
    gather_start(place, base, branch_rows, branch_all, sems)
    for index in range(4):
        sums_ref[index : index + 1, :] = jnp.sum(folded[index], axis=0, keepdims=True)
    sums_ref[4:8, :] = jnp.zeros((4, sums_ref.shape[1]), f32)

    def attend_back(block):
        here = pl.ds(pl.multiple_of(block * rows, rows), rows)
        grads = times_transposed(branch_all[block], w_out_ref[...]).astype(bf16)
        for head in range(HEADS_HERE):
            cols = pl.ds(head * LANES, LANES)
            query = qkv_ref[here, cols]
            key = qkv_ref[:, pl.ds((HEADS_HERE + head) * LANES, LANES)]
            value = qkv_ref[:, pl.ds((2 * HEADS_HERE + head) * LANES, LANES)]
            grad = grads[:, head * LANES : (head + 1) * LANES]
            weights = jnp.exp(masked_scores(length, query, key) - log_ref[head, here, :])
            grad_weights = times_transposed(grad, value)
            inner = jnp.sum(weights * grad_weights, axis=-1, keepdims=True)
            grad_scores = (weights * (grad_weights - inner)).astype(bf16)
            grad_qkv_ref[here, cols] = (matmul(grad_scores, key) * score_scale).astype(bf16)
            key_sum[:, cols] += outer_sum(grad_scores, query)
            value_sum[:, cols] += outer_sum(weights.astype(bf16), grad)

    args = (place, base, branch_rows, branch_all, sems)

    def passed(slots):
        for slot in slots:
            gather_piece(*args, slot).wait_recv()
            gather_pass(place, base, branch_all, sems, slot).start()

    def arrived(slots):
        for slot in slots:
            gather_pass(place, base, branch_all, sems, slot).wait_recv()

    def task():
        if tasks:
            tasks.pop(0)()

    def before(step):
        if step == 0:
            pltpu.make_async_copy(branch_rows, branch_all.at[place], sems[0]).wait()
        if step == 1:
            gather_own(*args).wait_recv()
            gather_relay(*args)
        if step == 2:
            passed((2, 3))
            last.after(0)
            task()
        if step == 3:
            last.after(1)
        if step == 4:
            passed((4, 5))
            arrived(range(4))
            task()
        if step == 5:
            last.after(2)
        if step == 6:
            arrived((4, 5))
        if step == 7:
            task()

    def attend_step(step, unused):
        for k in range(8):

            @pl.when(step == k)
            def _(k=k):
                before(k)

        far = step + jnp.where(step == 3, 1, 0) - jnp.where(step == 4, 1, 0)
        block = place + far % 2 * (1 - 2 * (place % 2))
        block = block + far // 2 % 2 * (2 - 4 * (place // 2 % 2))
        attend_back(block + far // 4 * (4 - 8 * (place // 4 % 2)))
        return unused

    lax.fori_loop(0, 8, attend_step, 0)
    for task in tasks:
        task()
    up_line.finish()
    up_swap.begin(up_line.total)
    cols = pl.ds(HEADS_HERE * LANES, HEADS_HERE * LANES)
    grad_qkv_ref[:, cols] = (key_sum[...] * score_scale).astype(bf16)
    cols = pl.ds(2 * HEADS_HERE * LANES, HEADS_HERE * LANES)
    grad_qkv_ref[:, cols] = value_sum[...].astype(bf16)
    grad_out = jnp.zeros(grad_out_ref.shape, f32)
    for block in range(GROUP):
        grad_out = grad_out + outer_sum(
            mixed_ref[block * rows : (block + 1) * rows, :], branch_all[block]
        )
    grad_out_ref[...] = grad_out

    def residual_and(span, value):
        output_ref[span, :] = residual_ref[span, :] + (value + vec_ref[7:8, :])

    last.finish(residual_and)
    down_line.finish()
    add_slabs(
        down_total.shape[0],
        lambda index, value: down_total.__setitem__(index, value),
        lambda index: down_line.total[index],
    )
    up_swap.finish()
    gather_own(*args).wait_send()
    for slot in range(6):
        gather_piece(*args, slot).wait_send()
        gather_pass(place, base, branch_all, sems, slot).wait_send()
    two.drain()
    last.drain()
    up_line.drain()
    down_line.drain()


def middle(count, length, two, part, residual, ct, vec, w_out, qkv, log, mixed, up, down, cid):
    groups = count // GROUP
    rows, width = ct.shape
    clip = qkv.shape[0]
    wide = HEADS_HERE * LANES
    return pl.pallas_call(
        functools.partial(middle_kernel, count),
        out_shape=[
            shaped(rows, width, kind=f32),
            shaped(rows, width, kind=f32),
            shaped(clip, 3 * wide),
            shaped(wide, width, kind=f32),
            shaped(8, width, kind=f32),
            shaped(*up.shape[1:]),
            shaped(*down.shape[1:], kind=f32),
        ],
        in_specs=[pl.BlockSpec(memory_space=pltpu.SMEM)] + [ANYSPEC] * 2 + [VSPEC] * 9,
        out_specs=[VSPEC] * 7,
        scratch_shapes=[
            VMEM((rows, width), bf16),
            VMEM((GROUP, rows, width), bf16),
            VMEM((clip, wide), f32),
            VMEM((clip, wide), f32),
            VMEM((8, width), f32),
            VMEM((4, 8, width), f32),
        ]
        + scatter_scratch(rows, width, True)
        + scatter_scratch(rows, width, True)
        + gather_sems()
        + line_sum_scratch(groups, *up.shape[1:])
        + line_sum_scratch(groups, *down.shape[1:])
        + swap_scratch(*up.shape[2:]),
        compiler_params=params(cid),
        name="middle",
    )(length, two, part, residual, ct, vec, w_out, qkv, log, mixed, up, down)


def last_kernel(
    count,
    x_ref,
    normed_ref,
    grad_qkv_ref,
    w_qkv_ref,
    grad_ref,
    gain_ref,
    early_ref,
    out_ref,
    grad_inputs_ref,
    qkv_got,
    out_total,
    early_total,
    late_total,
    own_cols,
    cols,
    folded,
    late,
    early_got,
    late_got,
    out_got,
    out_sib,
    *rest,
):
    groups = count // GROUP
    me = lax.axis_index("fsdp")
    place = me % GROUP
    base = me - place
    mine = me // GROUP
    rows, width = x_ref.shape
    few = own_cols.shape[2]
    one, rest = Scatter(place, base, rest[:SCATTER]), rest[SCATTER:]
    line, rest = LineSum(me, groups, own_cols, rest[:LINE_SUM]), rest[LINE_SUM:]
    swap, rest = Swap(place, base, qkv_got, rest[:SWAP]), rest[SWAP:]
    early_mail = Mail(me, count, early_ref, early_got, *rest[:3])
    late_mail = Mail(me, count, late, late_got, *rest[3:6])
    rest = rest[6:]
    fast = on_lines(count)
    core = place % 2
    greet_all(me, count)
    early_mail.begin()
    if fast:
        out_line = LineSum(me, groups, out_got, rest[3 : 3 + LINE_SUM])
        crossing = []
        for head in range(HEADS_HERE):
            slab = HEADS_HERE * core + head
            here = pl.multiple_of(head * LANES + few * core, 8)
            out_got[slab, 0] = out_ref[pl.ds(here, few), :].astype(bf16)
            there = pl.multiple_of(head * LANES + few * (1 - core), 8)
            out_sib[head, 0] = out_ref[pl.ds(there, few), :].astype(bf16)
            copy = remote(
                out_sib.at[head],
                out_got.at[slab],
                rest[1].at[head],
                rest[2].at[head],
                base + flip(place, 1),
            )
            copy.start()
            crossing.append(copy)
    else:
        direct = DirectBack(me, count, out_ref, out_got, *rest[:3])
        direct.begin()

    padded = 3 * HEADS_HERE * LANES
    packed = 3 * HEAD_COLS
    row = lax.broadcasted_iota(jnp.int32, (padded, packed), 0)
    col = lax.broadcasted_iota(jnp.int32, (padded, packed), 1)
    pick = jnp.where(
        (row // LANES == col // HD) & (row % LANES == col % HD), 1.0, 0.0
    ).astype(bf16)

    def weight_grad(index, unused):
        tile = pl.ds(pl.multiple_of(index * 256, 256), 256)
        grad = outer_sum(normed_ref[:, tile], grad_qkv_ref[...]).astype(bf16)
        cols[tile, :] = matmul(grad, pick)
        return unused

    if fast:
        for copy in crossing:
            copy.wait()
        out_line.begin()
    lax.fori_loop(0, width // 256, weight_grad, 0)
    for owner in range(count):
        own_cols[owner // GROUP, owner % GROUP] = cols[owner * few : (owner + 1) * few, :].astype(
            bf16
        )
    line.begin()
    tasks = line.tasks()
    out_tasks = out_line.tasks() if fast else []
    for i in range(4):

        def pair(turn, unused, i=i):
            block = jnp.where(turn == 0, one.block(i, True), one.block(i, False))
            here = pl.ds(pl.multiple_of(block * rows, rows), rows)
            one.parts[i, turn] = times_transposed(grad_qkv_ref[here, :], w_qkv_ref[...]).astype(
                bf16
            )

            @pl.when(turn == 0)
            def _():
                one.sibling(i).start()

            return unused

        lax.fori_loop(0, 2, pair, 0)
        one.after(i)
        if fast and 1 <= i <= 2:
            out_tasks[i - 1]()
        if i == 2:
            tasks.pop(0)()

    wide = HEADS_HERE * LANES

    def bias_sum(which):
        def add(index, value):
            span = pl.ds(pl.multiple_of(index * 64, 64), 64)
            return value + fold(grad_qkv_ref[span, which * wide : (which + 1) * wide].astype(f32))

        total = lax.fori_loop(
            0, grad_qkv_ref.shape[0] // 64, add, jnp.zeros((8, wide), f32)
        )
        row = lax.broadcasted_iota(jnp.int32, (wide, width), 0)
        col = lax.broadcasted_iota(jnp.int32, (wide, width), 1)
        home = head_of(place, row // LANES) * HD + row % LANES
        spot = jnp.where((row % LANES < HD) & (home == col), 1.0, 0.0)
        return jnp.sum(
            jnp.dot(total, spot, precision=lax.Precision.HIGHEST, preferred_element_type=f32),
            axis=0,
            keepdims=True,
        )

    biases = [bias_sum(0), bias_sum(2)]
    for task in tasks:
        task()
    folded[...] = jnp.zeros_like(folded)

    def through_norm(span, value):
        moved, by_xhat = norm_back_rows(x_ref[span, :].astype(f32), gain_ref[0:1, :], value)
        grad_inputs_ref[span, :] = grad_ref[span, :] + moved
        folded[0] = folded[0] + fold(by_xhat)
        folded[1] = folded[1] + fold(value)

    one.finish(through_norm)
    line.finish()
    swap.begin(line.total)

    vectors = jnp.concatenate(
        [
            jnp.sum(folded[0], axis=0, keepdims=True),
            jnp.sum(folded[1], axis=0, keepdims=True),
            *biases,
            jnp.zeros((4, width), f32),
        ],
        axis=0,
    )
    stretch = lax.broadcasted_iota(jnp.int32, (1, width), 1)
    row = lax.broadcasted_iota(jnp.int32, (width, LANES), 0)
    lane = lax.broadcasted_iota(jnp.int32, (width, LANES), 1)
    spot = jnp.where(row % few == lane, 1.0, 0.0)
    many = 8

    def owners(index, unused):
        terms = [
            jnp.where(stretch // few == index * many + k, vectors, 0.0) for k in range(many)
        ]
        slabs = jnp.dot(
            jnp.concatenate(terms, axis=0),
            spot,
            precision=lax.Precision.HIGHEST,
            preferred_element_type=f32,
        )
        for k in range(many):
            late[index * many + k] = slabs[k * 8 : k * 8 + 8]
        return unused

    lax.fori_loop(0, count // many, owners, 0)
    late_mail.begin()
    early_mail.finish(early_total)
    if fast:
        out_line.finish()
        out_total[...] = out_line.total[0]
        out_line.drain()
    else:
        direct.finish(out_total)
    swap.finish()
    late_mail.finish(late_total)
    one.drain()
    line.drain()


def last(count, x, normed, grad_qkv, w_qkv, grad, gain, early, out, collective_id):
    groups = count // GROUP
    rows, width = x.shape
    few = width // count
    packed = 3 * HEAD_COLS
    fast = on_lines(count)

    def mail(shape):
        return [DMA, DMA((count,)), DMA((count,))]

    return pl.pallas_call(
        functools.partial(last_kernel, count),
        out_shape=[
            shaped(rows, width, kind=f32),
            shaped(GROUP, few, packed),
            shaped(few, width, kind=f32),
            shaped(*early.shape[1:], kind=f32),
            shaped(8, LANES, kind=f32),
        ],
        in_specs=[VSPEC] * 8,
        out_specs=[VSPEC] * 5,
        scratch_shapes=[
            VMEM((groups, GROUP, few, packed), bf16),
            VMEM((width, packed), f32),
            VMEM((2, 8, width), f32),
            VMEM((count, 8, LANES), f32),
            VMEM(early.shape, f32),
            VMEM((count, 8, LANES), f32),
            VMEM((groups, 1, few, width) if fast else (groups, few, width), bf16),
            VMEM((HEADS_HERE, 1, few, width), bf16),
        ]
        + scatter_scratch(rows, width)
        + line_sum_scratch(groups, GROUP, few, packed)
        + swap_scratch(few, packed)
        + mail(early)
        + mail(early)
        + [DMA, DMA((groups,)), DMA((groups,))]
        + (line_sum_scratch(groups, 1, few, width) if fast else []),
        compiler_params=params(collective_id),
        name="last",
    )(x, normed, grad_qkv, w_qkv, grad, gain, early, out)


def pack_kernel(
    groups,
    output_in,
    inputs_in,
    qkv_in,
    out_in,
    early_in,
    late_in,
    up_in,
    down_in,
    output,
    grad_inputs,
    g1,
    o1,
    wq,
    bq,
    wk,
    wv,
    bv,
    wo,
    bo,
    g2,
    o2,
    wu,
    bu,
    wd,
    bd,
):
    few, many = wq.shape[0], wd.shape[0]
    output[...] = output_in[...]
    grad_inputs[...] = inputs_in[...]
    for place in range(GROUP):
        for which, ref in enumerate((wq, wk, wv)):
            for head in range(HEADS_HERE):
                start = head_of(place, head) * HD
                cols = which * HEAD_COLS + head * HD
                ref[:, start : start + HD] = qkv_in[place, :, cols : cols + HD].astype(f32)
        for group in range(groups):
            start = (group * GROUP + place) * many
            wu[:, start : start + many] = up_in[
                place, :, group * many : (group + 1) * many
            ].astype(f32)
    wo[...] = out_in[...]
    for index in range(down_in.shape[0]):
        wd[index * few : (index + 1) * few, :] = down_in[index]
    for index, ref in enumerate((g1, o1, bq, bv)):
        ref[...] = late_in[index : index + 1, :few]
    for index, ref in enumerate((g2, o2, bo, bd)):
        ref[...] = early_in[index : index + 1, :few]
    for start in range(0, many, LANES):
        stop = min(start + LANES, many)
        line = 4 + start // LANES
        bu[:, start:stop] = early_in[line : line + 1, : stop - start]


def pack(groups, output, grad_inputs, qkv, out, early, late, up, down):
    rows, width = output.shape
    few, many = out.shape[0], down.shape[0] * down.shape[1]
    ff = groups * GROUP * many

    def whole(*shape):
        return jax.ShapeDtypeStruct(shape, f32)

    line = whole(1, few)
    square = whole(few, width)
    big = whole(rows, width)
    results = pl.pallas_call(
        functools.partial(pack_kernel, groups),
        out_shape=[big, big, line, line, square, line, square, square, line, square]
        + [line, line, line, whole(few, ff), whole(1, many), whole(many, width), line],
        in_specs=[VSPEC] * 8,
        out_specs=[VSPEC] * 17,
        name="pack",
    )(output, grad_inputs, qkv, out, early, late, up, down)
    return tuple(r.reshape(r.shape[1]) if r.shape[0] == 1 else r for r in results)


def gelu_exact(values):
    return jax.nn.gelu(values, approximate=False)


def column_sums(matrix):
    return jnp.sum(matrix.astype(f32), axis=0)


def on_device(
    inputs,
    ln1_gain,
    ln1_bias,
    w_query,
    b_query,
    w_key,
    w_value,
    b_value,
    w_out,
    b_out,
    ln2_gain,
    ln2_bias,
    w_up,
    b_up,
    w_down,
    b_down,
    lengths,
    cotangent,
):
    count = lax.axis_size("fsdp")
    groups = count // GROUP
    me = lax.axis_index("fsdp")
    place = me % GROUP
    few = w_query.shape[0]
    many = w_down.shape[0]
    rows = inputs.shape[0]
    ff_here = groups * many

    up_lanes = -(-many // LANES)
    small = jnp.stack([ln1_gain, ln1_bias, b_query, b_value, b_out, ln2_gain, ln2_bias, b_down])
    small = jnp.concatenate(
        [
            jnp.pad(small, ((0, 0), (0, LANES - few))),
            jnp.pad(b_up, (0, up_lanes * LANES - many)).reshape(up_lanes, LANES),
            jnp.zeros((8 - up_lanes, LANES), f32),
        ]
    ).astype(bf16)
    (
        normed,
        w_qkv,
        qkv,
        w_out_here,
        attended,
        log,
        residual,
        vectors,
        small_all,
        two_all,
        ct_all,
        up_all,
        down_all,
    ) = front(
        count,
        lengths,
        inputs,
        cotangent,
        w_query,
        w_key,
        w_value,
        w_out,
        w_up,
        w_down,
        small,
        0,
    )
    b_up_here = small_all.reshape((groups, GROUP) + small_all.shape[1:])
    b_up_here = lax.dynamic_index_in_dim(b_up_here, place, 1, keepdims=False)
    b_up_here = b_up_here[:, 8 : 8 + up_lanes].astype(f32)
    b_up_here = b_up_here.reshape(groups, up_lanes * LANES)[:, :many].reshape(ff_here)
    w_up_here = up_all.reshape(D, ff_here)
    w_down_here = down_all.reshape(ff_here, D)
    normed_two = two_all.reshape(GROUP * rows, D)
    length = lax.dynamic_slice_in_dim(lengths, me // GROUP, 1)

    ct = ct_all.reshape(GROUP * rows, D)
    hidden = matmul(normed_two, w_up_here) + b_up_here
    activated = gelu_exact(hidden).astype(bf16)
    out_part = matmul(activated, w_down_here).astype(bf16).reshape(GROUP, rows, D)

    grad_activated = times_transposed(ct, w_down_here)
    unused, gelu_pullback = jax.vjp(gelu_exact, hidden)
    grad_hidden = gelu_pullback(grad_activated)[0].astype(bf16)
    two_part = times_transposed(grad_hidden, w_up_here).astype(bf16).reshape(GROUP, rows, D)
    grad_w_up = outer_sum(normed_two, grad_hidden).astype(bf16)
    grad_w_down = outer_sum(activated, ct).astype(bf16)
    output, grad_residual, grad_qkv, grad_out, sums, up_got, down_total = middle(
        count,
        length,
        two_part,
        out_part,
        residual,
        cotangent,
        vectors,
        w_out_here,
        qkv,
        log,
        attended,
        grad_w_up.reshape(groups, GROUP, few, ff_here),
        grad_w_down.reshape(groups, many // few, few, D),
        2,
    )
    if not on_lines(count):
        grad_out = grad_out.reshape(HEADS_HERE, LANES, D)[:, :HD].reshape(groups, few, D)
        grad_out = grad_out.astype(bf16)
    grad_b_up = jnp.pad(
        column_sums(grad_hidden).reshape(groups, 1, many),
        ((0, 0), (0, 0), (0, up_lanes * LANES - many)),
    ).reshape(groups, 1, up_lanes, LANES)
    grad_b_up = jnp.where(
        (jnp.arange(GROUP) == place)[None, :, None, None], grad_b_up, 0.0
    ).reshape(count, up_lanes, LANES)
    early = jnp.pad(
        sums[:4].reshape(4, count, few).transpose(1, 0, 2), ((0, 0), (0, 0), (0, LANES - few))
    )
    early = jnp.concatenate(
        [early, grad_b_up, jnp.zeros((count, 4 - up_lanes, LANES), f32)], axis=1
    )
    grad_inputs, qkv_got, shard_w_out, early_sum, late_sum = last(
        count,
        inputs,
        normed,
        grad_qkv,
        w_qkv,
        grad_residual,
        vectors,
        early,
        grad_out,
        3,
    )

    return pack(
        groups,
        output,
        grad_inputs,
        qkv_got,
        shard_w_out,
        early_sum,
        late_sum,
        up_got,
        down_total,
    )


def solution(mesh):
    in_specs = (
        P("fsdp", None),
        P("fsdp"),
        P("fsdp"),
        P("fsdp", None),
        P("fsdp"),
        P("fsdp", None),
        P("fsdp", None),
        P("fsdp"),
        P("fsdp", None),
        P("fsdp"),
        P("fsdp"),
        P("fsdp"),
        P("fsdp", None),
        P("fsdp"),
        P("fsdp", None),
        P("fsdp"),
        P(),
        P("fsdp", None),
    )
    out_specs = (
        P("fsdp", None),
        P("fsdp", None),
        P("fsdp"),
        P("fsdp"),
        P("fsdp", None),
        P("fsdp"),
        P("fsdp", None),
        P("fsdp", None),
        P("fsdp"),
        P("fsdp", None),
        P("fsdp"),
        P("fsdp"),
        P("fsdp"),
        P("fsdp", None),
        P("fsdp"),
        P("fsdp", None),
        P("fsdp"),
    )
    return jax.shard_map(
        on_device, mesh=mesh, in_specs=in_specs, out_specs=out_specs, check_vma=False
    )
```
